32 devices in a mesh: dp: 2 (over core), crow: 4 (over y, x), ccol: 4 (over z).
Axes of the slice: x: 2, y: 2, z: 4, core: 2. Of those that a mesh axis runs over, the one named last changes fastest.
Arguments:
- data: float32 [16, 16384], P(None, ('dp', 'crow')), may hold values from 0 to 1
- centres: float32 [16, 3072], P(None, 'ccol'), may hold values from 0 to 1
- scales: float32 [16], replicated, may hold values from 0.5 to 1.2
- factor: float32 [3072, 3072], P('crow', 'ccol'), may hold values from -1 to 1, as said below
- block_inv: float32 [12, 256, 256], P('crow'), may hold values from -1 to 2
- iterate: float32 [8, 3072], replicated, may hold values from -6 to 6
- residual: float32 [8, 3072], replicated, may hold values from -6 to 6
- direction: float32 [8, 3072], replicated, may hold values from -6 to 6
Outputs:
- new_iterate: float32 [8, 3072], replicated
- new_residual: float32 [8, 3072], replicated
- new_direction: float32 [8, 3072], replicated
The draws below stay inside these ranges and needn't reach their ends.
Inputs may be any that keep to these rules, and one draw needn't show every extreme that they name: `factor`: blocks of 256 x 256 on and above the block diagonal are zero.
All inputs are finite; a program needn't handle non-finite values.
Results may differ from the reference program's by a relative error of at most 0.0001.
Values sent between devices are 32-bit elements; how exact they have to be, the bound alone decides.
No kernel may reach another device: no remote copies, remote signals or barrier semaphores. Data moves between devices by JAX's collectives and lax.ppermute only.
A program may use at most 64 MiB of HBM per device.

```python
import math
import jax
import jax.numpy as jnp
from jax import lax

INPUTS = 16
BLOCK = 256
NBLK = 12
CENTRES = 3072
NRHS = 8
RBLK = 1024
NROWS = 16384


def draw_factor(key, part):
    total = BLOCK * NBLK
    values = jax.random.normal(key, (total, total), jnp.float32)
    row_block = jnp.arange(total)[:, None] // BLOCK
    col_block = jnp.arange(total)[None, :] // BLOCK
    scaled = values * (0.5 / math.sqrt(total))
    return jnp.where(row_block > col_block, scaled, 0.0).astype(jnp.float32)


def draw_block_inv(key, part):
    first = jax.random.fold_in(key, 11)
    second = jax.random.fold_in(key, 23)
    identity = jnp.eye(BLOCK, dtype=jnp.float32)
    leading = jax.random.uniform(first, (NBLK, BLOCK), jnp.float32, 0.7, 1.4)
    spread = jax.random.normal(second, (NBLK, BLOCK, BLOCK), jnp.float32)
    spread = spread * (0.35 / math.sqrt(BLOCK))
    return (spread * (1.0 - identity) + identity * leading[:, :, None]).astype(jnp.float32)


def shard_levels(rng, extent, split, low, largest):
    def one(axis_at, shards_of):
        steps = jax.random.uniform(jax.random.fold_in(jax.random.fold_in(rng, 6), axis_at), (shards_of,), jnp.float32, low / len(split), largest / len(split))
        return jnp.repeat(jnp.exp(steps), extent[axis_at] // shards_of).reshape((-1,) + (1,) * (len(extent) - axis_at - 1))

    factor_of = one(*split[0])
    for cut in split[1:]:
        factor_of = factor_of * one(*cut)
    return factor_of


def bell_draw(rng, dims, width, reach, kind=jnp.bfloat16):
    entries = jax.random.normal(rng, dims, jnp.float32) * width
    return jnp.minimum(jnp.maximum(entries, -reach), reach).astype(kind)


def setup_inputs(seed: int = 0) -> dict:
    streams_of = jax.random.split(jax.random.key(seed), 9)
    return {
        "data": jnp.clip(1.0 * jax.random.uniform(streams_of[0], (INPUTS, NROWS), jnp.float32) ** shard_levels(streams_of[0], (INPUTS, NROWS), ((1, 8),), -0.2, 0.2), 0.0, 1.0),
        "centres": jnp.clip(1.0 * jax.random.uniform(streams_of[1], (INPUTS, CENTRES), jnp.float32) ** shard_levels(streams_of[1], (INPUTS, CENTRES), ((1, 4),), -0.2, 0.2), 0.0, 1.0),
        "scales": jnp.clip(jnp.exp(jax.random.uniform(streams_of[2], (INPUTS,), jnp.float32, math.log(0.5), math.log(1.2))), 0.5, 1.2),
        "factor": draw_factor(jax.random.fold_in(streams_of[8], 71), 0),
        "block_inv": draw_block_inv(jax.random.fold_in(streams_of[8], 71), 0),
        "iterate": bell_draw(streams_of[5], (NRHS, CENTRES), 1.0, 6.0, jnp.float32),
        "residual": bell_draw(streams_of[6], (NRHS, CENTRES), 1.0, 6.0, jnp.float32),
        "direction": bell_draw(streams_of[7], (NRHS, CENTRES), 1.0, 6.0, jnp.float32),
    }


ridge_weight = 0.2
highest = lax.Precision.HIGHEST


def kernel_tile(sample, centre_set, scales):
    scaled_sample = sample / scales[:, None]
    scaled_centres = centre_set / scales[:, None]
    cross_terms = lax.dot_general(scaled_centres, scaled_sample, (((0,), (0,)), ((), ())), precision=highest, preferred_element_type=jnp.float32)
    distance = jnp.sum(scaled_centres * scaled_centres, axis=0)[:, None] + jnp.sum(scaled_sample * scaled_sample, axis=0)[None, :] - 2.0 * cross_terms
    return jnp.exp(-0.5 * distance)


def project(weights, tile):
    return jnp.dot(weights, tile, precision=highest, preferred_element_type=jnp.float32)


def pullback(images, tile):
    return lax.dot_general(images, tile, (((1,), (1,)), ((), ())), precision=highest, preferred_element_type=jnp.float32)


def back_solve(direction, factor, block_inv):
    solved = jnp.zeros_like(direction)
    for number in reversed(range(NBLK)):
        start = number * BLOCK
        partial_value = project(solved, factor[:, start:start + BLOCK])
        piece = project(direction[:, start:start + BLOCK] - partial_value, block_inv[number])
        solved = solved.at[:, start:start + BLOCK].set(piece)
    return solved


def fore_solve(source, factor, block_inv):
    solved = jnp.zeros_like(source)
    for number in range(NBLK):
        start = number * BLOCK
        partial_value = pullback(solved, factor[start:start + BLOCK, :])
        piece = pullback(source[:, start:start + BLOCK] - partial_value, block_inv[number])
        solved = solved.at[:, start:start + BLOCK].set(piece)
    return solved


def reference(data, centres, scales, factor, block_inv, iterate, residual, direction):
    solved = back_solve(direction, factor, block_inv)
    blocks = NROWS // RBLK
    stacked = data.reshape(INPUTS, blocks, RBLK).transpose(1, 0, 2)

    def accumulate(total, sample):
        tile = kernel_tile(sample, centres, scales)
        return total + pullback(project(solved, tile), tile), None

    summed, _ = lax.scan(accumulate, jnp.zeros((NRHS, CENTRES), jnp.float32), stacked)
    normal_image = summed / NROWS + ridge_weight * solved
    image = fore_solve(normal_image, factor, block_inv)
    gamma = jnp.sum(residual * residual, axis=1)
    curvature = jnp.sum(direction * image, axis=1)
    alpha = (gamma / curvature)[:, None]
    new_iterate = iterate + alpha * direction
    new_residual = residual - alpha * image
    gamma_next = jnp.sum(new_residual * new_residual, axis=1)
    new_direction = new_residual + (gamma_next / gamma)[:, None] * direction
    return (new_iterate, new_residual, new_direction)
```

```python
import functools
import math

import jax
import jax.numpy as jnp
from jax import lax
from jax.experimental import pallas as pl
from jax.experimental.pallas import tpu as pltpu
from jax.sharding import PartitionSpec as P

ridge_weight = 0.2
LOG2E = 1.0 / math.log(2.0)
NN = (((1,), (0,)), ((), ()))
NT = (((1,), (1,)), ((), ()))
TN = (((0,), (0,)), ((), ()))


def pair(value):
    high = value.astype(jnp.bfloat16)
    low = (value - high.astype(jnp.float32)).astype(jnp.bfloat16)
    return high, low


def stacked(value):
    high, low = pair(value)
    return jnp.concatenate([high, low], axis=0)


def fold(product, rows):
    return product[:rows] + product[rows:]


def times_pair(rows, high, low, dims):
    both = stacked(rows)
    out = lax.dot_general(both, high, dims, preferred_element_type=jnp.float32)
    out = out + lax.dot_general(both, low, dims, preferred_element_type=jnp.float32)
    return fold(out, rows.shape[0])


def times(rows, matrix, dims):
    high, low = pair(matrix)
    return times_pair(rows, high, low, dims)


def below(tri_ref, order, row, col):
    at = row * (row - 1) // 2 + col
    return tri_ref[:, at * order : (at + 1) * order]


def back_blocks(target, tri_ref, inv_ref):
    held, order = inv_ref.shape[0], inv_ref.shape[1]
    pieces = [None] * held
    for number in reversed(range(held)):
        part = target[:, number * order : (number + 1) * order]
        for later in range(number + 1, held):
            part = part - times(pieces[later], below(tri_ref, order, later, number), NN)
        pieces[number] = times(part, inv_ref[number], NN)
    return jnp.concatenate(pieces, axis=1)


def fore_blocks(source, tri_ref, inv_ref):
    held, order = inv_ref.shape[0], inv_ref.shape[1]
    pieces = []
    for number in range(held):
        part = source[:, number * order : (number + 1) * order]
        for early in range(number):
            part = part - times(pieces[early], below(tri_ref, order, number, early), NT)
        pieces.append(times(part, inv_ref[number], NT))
    return jnp.concatenate(pieces, axis=1)


def back_solve_kernel(target_ref, sub_ref, tri_ref, inv_ref, out_ref):
    out_ref[...] = back_blocks(target_ref[...] - sub_ref[...], tri_ref, inv_ref)


def back_solve_times_kernel(target_ref, sub_ref, more_ref, tri_ref, inv_ref, factor_ref, out_ref, next_ref):
    solved = back_blocks(target_ref[...] - sub_ref[...], tri_ref, inv_ref)
    out_ref[...] = solved
    next_ref[...] = more_ref[...] + times(solved, factor_ref[...], NN)


def times_kernel(rows_ref, more_ref, factor_ref, out_ref):
    out_ref[...] = more_ref[...] + times(rows_ref[...], factor_ref[...], NN)


def fore_solve_kernel(source_ref, tri_ref, inv_ref, out_ref):
    out_ref[...] = fore_blocks(source_ref[...], tri_ref, inv_ref)


def fore_times_solve_kernel(rows_ref, source_ref, factor_ref, tri_ref, inv_ref, left_ref, out_ref):
    left = source_ref[...] - times(rows_ref[...], factor_ref[...], NT)
    left_ref[...] = left
    out_ref[...] = fore_blocks(left, tri_ref, inv_ref)


def triple(value):
    high, middle = pair(value)
    rest = value - high.astype(jnp.float32) - middle.astype(jnp.float32)
    return high, middle, rest.astype(jnp.bfloat16)


def tile_kernel(centres_ref, data_ref, scales_ref, high_ref, low_ref, right):
    inputs = data_ref.shape[0]
    spare = right.shape[0] - 6 * inputs - 2 * inputs

    @pl.when(pl.program_id(0) == 0)
    def _():
        scaled = data_ref[...] / scales_ref[...]
        norm = jnp.sum(scaled * scaled, axis=0, keepdims=True) * (-0.5 * LOG2E)
        high, middle, low = triple(scaled)
        norms = norm_rows(norm, inputs)
        ones = ones_rows(norm, inputs)
        zeros = jnp.zeros((spare, scaled.shape[1]), jnp.bfloat16)
        right[...] = jnp.concatenate(
            [high, middle, high, middle, low, high, norms, ones, zeros], axis=0
        )

    scaled = centres_ref[...] / scales_ref[...]
    norm = jnp.sum(scaled * scaled, axis=0, keepdims=True) * (-0.5 * LOG2E)
    high, middle, low = triple(scaled * LOG2E)
    zeros = jnp.zeros((spare, scaled.shape[1]), jnp.bfloat16)
    left = jnp.concatenate(
        [high, high, middle, middle, high, low, ones_rows(norm, inputs), norm_rows(norm, inputs), zeros],
        axis=0,
    )
    exponent = lax.dot_general(left, right[...], TN, preferred_element_type=jnp.float32)
    value = jnp.exp2(exponent)
    high, low = pair(value)
    high_ref[...] = high
    low_ref[...] = low


def norm_rows(norm, inputs):
    row = lax.broadcasted_iota(jnp.int32, (inputs, norm.shape[1]), 0)
    wide = jnp.broadcast_to(norm, (inputs, norm.shape[1]))
    high, middle, low = (part.astype(jnp.float32) for part in triple(wide))
    return jnp.where(row == 0, high, jnp.where(row == 1, middle, jnp.where(row == 2, low, 0.0))).astype(
        jnp.bfloat16
    )


def ones_rows(norm, inputs):
    row = lax.broadcasted_iota(jnp.int32, (inputs, norm.shape[1]), 0)
    return jnp.where(row < 3, 1.0, 0.0).astype(jnp.bfloat16)


def image_kernel(rows_ref, high_ref, low_ref, out_ref):
    out_ref[...] = times_pair(rows_ref[...], high_ref[...], low_ref[...], NN)


def normal_kernel(rows_ref, high_ref, low_ref, out_ref):
    out_ref[...] = times_pair(rows_ref[...], high_ref[...], low_ref[...], NT)


def final_kernel(iterate_ref, residual_ref, direction_ref, image_ref, iterate_out, residual_out, direction_out):
    residual = residual_ref[...]
    direction = direction_ref[...]
    image = image_ref[...]
    gamma = jnp.sum(residual * residual, axis=1, keepdims=True)
    curvature = jnp.sum(direction * image, axis=1, keepdims=True)
    alpha = gamma / curvature
    iterate_out[...] = iterate_ref[...] + alpha * direction
    new_residual = residual - alpha * image
    residual_out[...] = new_residual
    gamma_next = jnp.sum(new_residual * new_residual, axis=1, keepdims=True)
    direction_out[...] = new_residual + (gamma_next / gamma) * direction


def shaped(*shape):
    return jax.ShapeDtypeStruct(shape, jnp.float32)


def call(kernel, outs, *args):
    return pl.pallas_call(kernel, out_shape=outs)(*args)


def swap(size, one, other, still):
    to = list(range(size))
    to[one], to[other] = other, one
    if not still:
        rest = [n for n in range(size) if n not in (one, other)]
        for a, b in zip(rest[::2], rest[1::2]):
            to[a], to[b] = b, a
    return to


def keep(size):
    return list(range(size))


def per_device(data, centres, scales, factor, block_inv, iterate, residual, direction):
    crow, ccol = lax.axis_size("crow"), lax.axis_size("ccol")
    row, col = lax.axis_index("crow"), lax.axis_index("ccol")
    held, order = block_inv.shape[0], block_inv.shape[1]
    width = factor.shape[0]
    rows = direction.shape[0]
    total = direction.shape[1]
    assert factor.shape[1] == width and crow == ccol

    def move(value, row_to, col_to):
        perm = [
            (r * ccol + c, row_to[r] * ccol + col_to[c]) for r in range(crow) for c in range(ccol)
        ]
        return lax.ppermute(value, ("crow", "ccol"), perm)

    def shifts(value, axis):
        size = lax.axis_size(axis)
        return [
            lax.ppermute(value, axis, [(s, (s + step) % size) for s in range(size)])
            for step in range(1, size)
        ]

    def ordered(value, others, axis):
        size = lax.axis_size(axis)
        me = lax.axis_index(axis)
        parts = jnp.stack([value] + others)
        source = (me - jnp.arange(size)) % size
        place = jnp.zeros((size,), jnp.int32).at[source].set(jnp.arange(size))
        return [lax.dynamic_index_in_dim(parts, place[n], 0, False) for n in range(size)]

    part = shaped(rows, width)
    all_centres = jnp.concatenate(ordered(centres, shifts(centres, "ccol"), "ccol"), axis=1)
    tri = jnp.concatenate(
        [
            factor[r * order : (r + 1) * order, c * order : (c + 1) * order]
            for r in range(1, held)
            for c in range(r)
        ],
        axis=1,
    )
    near = lax.ppermute(tri, "ccol", [((c + 1) % ccol, c) for c in range(ccol)])

    samples = data.shape[1]
    tile = order
    high, low = pl.pallas_call(
        tile_kernel,
        grid=(total // tile,),
        in_specs=[
            pl.BlockSpec((data.shape[0], tile), lambda i: (0, i)),
            pl.BlockSpec(data.shape, lambda i: (0, 0)),
            pl.BlockSpec((data.shape[0], 1), lambda i: (0, 0)),
        ],
        out_specs=[pl.BlockSpec((tile, samples), lambda i: (i, 0))] * 2,
        out_shape=[jax.ShapeDtypeStruct((total, samples), jnp.bfloat16)] * 2,
        scratch_shapes=[pltpu.VMEM((256, samples), jnp.bfloat16)],
    )(all_centres, data, scales[:, None])

    zero = jnp.zeros((rows, width), jnp.float32)
    target = lax.dynamic_slice_in_dim(direction, row * width, width, 1)
    mine = zero
    sums = zero
    piece = call(back_solve_kernel, part, target, zero, tri, block_inv)
    for step in reversed(range(crow)):
        mine = jnp.where((row == step) & (col == step), piece, mine)
        if step == 0:
            break
        for far in range(1, step + 1):
            got = move(piece, keep(crow), swap(ccol, step, step - far, False))
            mine = jnp.where((row == step) & (col == step - far), got, mine)
        sums = call(times_kernel, part, mine, sums, factor)
        got = move(sums, swap(crow, step, step - 1, False), keep(ccol))
        sums = jnp.where(row == step - 1, got, sums)
        piece = call(back_solve_kernel, part, target, sums, tri, block_inv)

    solved = jnp.concatenate(ordered(mine, shifts(mine, "crow"), "crow"), axis=1)
    wide = 512
    images = pl.pallas_call(
        image_kernel,
        grid=(samples // wide,),
        in_specs=[
            pl.BlockSpec((rows, total), lambda i: (0, 0)),
            pl.BlockSpec((total, wide), lambda i: (0, i)),
            pl.BlockSpec((total, wide), lambda i: (0, i)),
        ],
        out_specs=pl.BlockSpec((rows, wide), lambda i: (0, i)),
        out_shape=shaped(rows, samples),
    )(solved, high, low)
    summed = pl.pallas_call(
        normal_kernel,
        grid=(total // width,),
        in_specs=[
            pl.BlockSpec((rows, samples), lambda i: (0, 0)),
            pl.BlockSpec((width, samples), lambda i: (i, 0)),
            pl.BlockSpec((width, samples), lambda i: (i, 0)),
        ],
        out_specs=pl.BlockSpec((rows, width), lambda i: (0, i)),
        out_shape=shaped(rows, total),
    )(images, high, low)
    dp = lax.axis_size("dp")
    if dp == 2:
        summed = summed + lax.ppermute(summed, "dp", [(0, 1), (1, 0)])
    else:
        summed = lax.psum(summed, "dp")
    summed = sum(shifts(summed, "crow"), summed)
    normal = summed / (samples * dp * crow) + ridge_weight * solved
    source = lax.dynamic_slice_in_dim(normal, row * width, width, 1)

    image = call(fore_solve_kernel, part, source, tri, block_inv)
    others = ordered(image, shifts(image, "crow"), "crow")
    first = others[0]
    final = jnp.where((row == 0) & (col == 0), image, zero)
    left, image = call(fore_times_solve_kernel, [part, part], first, source, factor, near, block_inv)
    final = jnp.where((row == 1) & (col == 0), image, final)
    for step in range(2, crow):
        back = step - 2
        aside = swap(ccol, back, back + 1, False)
        source = move(left, keep(crow), aside)
        pieces = zero
        for at in range(step, crow):
            got = move(image, swap(crow, step - 1, at, False), swap(ccol, back, back + 1, True))
            pieces = jnp.where(row == at, got, pieces)
        left, image = call(fore_times_solve_kernel, [part, part], pieces, source, factor, near, block_inv)
        final = jnp.where((row == step) & (col == step - 1), image, final)
    final = sum(shifts(final, "ccol"), final)
    image = jnp.concatenate(ordered(final, shifts(final, "crow"), "crow"), axis=1)
    full = shaped(rows, total)
    return tuple(call(final_kernel, [full, full, full], iterate, residual, direction, image))


def solution(mesh):
    placed = (
        P(None, ("dp", "crow")),
        P(None, "ccol"),
        P(),
        P("crow", "ccol"),
        P("crow", None, None),
        P(),
        P(),
        P(),
    )
    return jax.shard_map(
        per_device, mesh=mesh, in_specs=placed, out_specs=(P(), P(), P()), check_vma=False
    )
```

```python
import functools
import math

import jax
import jax.numpy as jnp
from jax import lax
from jax.experimental import pallas as pl
from jax.experimental.pallas import tpu as pltpu
from jax.sharding import PartitionSpec as P

ridge_weight = 0.2
LOG2E = 1.0 / math.log(2.0)
NN = (((1,), (0,)), ((), ()))
NT = (((1,), (1,)), ((), ()))
TN = (((0,), (0,)), ((), ()))


def pair(value):
    high = value.astype(jnp.bfloat16)
    low = (value - high.astype(jnp.float32)).astype(jnp.bfloat16)
    return high, low


def stacked(value):
    high, low = pair(value)
    return jnp.concatenate([high, low], axis=0)


def fold(product, rows):
    return product[:rows] + product[rows:]


def times_pair(rows, high, low, dims):
    both = stacked(rows)
    out = lax.dot_general(both, high, dims, preferred_element_type=jnp.float32)
    out = out + lax.dot_general(both, low, dims, preferred_element_type=jnp.float32)
    return fold(out, rows.shape[0])


def times(rows, matrix, dims):
    high, low = pair(matrix)
    return times_pair(rows, high, low, dims)


def blocks_of(held):
    return [(r, c) for r in range(1, held) for c in range(r)]


def lower(low_ref, order, r, c):
    at = r * (r - 1) // 2 + c
    return low_ref[:, at * order : (at + 1) * order]


def square(one, other):
    first, first_low = pair(one)
    second, second_low = pair(other)
    out = lax.dot_general(first, second, NN, preferred_element_type=jnp.float32)
    out = out + lax.dot_general(first, second_low, NN, preferred_element_type=jnp.float32)
    return out + lax.dot_general(first_low, second, NN, preferred_element_type=jnp.float32)


def cut(ref, at, width):
    return ref[:, pl.ds(pl.multiple_of(at * width, width), width)]


def back_apply(target, low_ref, inv_ref):
    held, order = inv_ref.shape[0], inv_ref.shape[1]
    parts = [target[:, n * order : (n + 1) * order] for n in range(held)]
    pieces = []
    for c in range(held):
        piece = times(parts[c], inv_ref[c], NN)
        for r in range(c + 1, held):
            piece = piece + times(parts[r], lower(low_ref, order, r, c), NN)
        pieces.append(piece)
    return jnp.concatenate(pieces, axis=1)


def fore_apply(source, low_ref, inv_ref):
    held, order = inv_ref.shape[0], inv_ref.shape[1]
    parts = [source[:, n * order : (n + 1) * order] for n in range(held)]
    pieces = []
    for r in range(held):
        piece = times(parts[r], inv_ref[r], NT)
        for c in range(r):
            piece = piece + times(parts[c], lower(low_ref, order, r, c), NT)
        pieces.append(piece)
    return jnp.concatenate(pieces, axis=1)


def first_kernel(direction_ref, inv_ref, *refs):
    tri_refs, out_ref = refs[:-1], refs[-1]
    held, order = inv_ref.shape[0], inv_ref.shape[1]
    width = held * order
    tri = dict(zip(blocks_of(held), tri_refs))
    target = cut(direction_ref, lax.axis_index("crow"), width)
    pieces = [None] * held
    for number in reversed(range(held)):
        part = target[:, number * order : (number + 1) * order]
        for later in range(number + 1, held):
            part = part - times(pieces[later], tri[later, number][...], NN)
        pieces[number] = times(part, inv_ref[number], NN)
    out_ref[...] = jnp.concatenate(pieces, axis=1)


def lower_kernel(inv_ref, *refs):
    tri_refs, out_ref = refs[:-1], refs[-1]
    held, order = inv_ref.shape[0], inv_ref.shape[1]
    tri = dict(zip(blocks_of(held), tri_refs))
    found = {(n, n): inv_ref[n] for n in range(held)}
    for r in range(1, held):
        for c in range(r):
            total = square(tri[r, c][...], found[c, c])
            for between in range(c + 1, r):
                total = total + square(tri[r, between][...], found[between, c])
            found[r, c] = -square(inv_ref[r], total)
            at = r * (r - 1) // 2 + c
            out_ref[:, at * order : (at + 1) * order] = found[r, c]


def pair_kernel(factor_ref, high_ref, low_ref):
    high, low = pair(factor_ref[...])
    high_ref[...] = high
    low_ref[...] = low


def spread_kernel(step, cols, *refs):
    extra = refs[: len(refs) - 3 - len(cols)]
    got_refs = refs[len(extra) : len(extra) + len(cols)]
    high_ref, low_ref, out_ref = refs[-3:]
    col = lax.axis_index("ccol")
    piece = got_refs[0][...]
    for at, got in zip(cols[1:], got_refs[1:]):
        piece = jnp.where(col == at, got[...], piece)
    out = times_pair(piece, high_ref[...], low_ref[...], NN)
    for ref in extra:
        out = out + ref[...]
    out_ref[...] = out


def solve_kernel(direction_ref, sub_ref, low_ref, inv_ref, out_ref):
    width = sub_ref.shape[1]
    target = cut(direction_ref, lax.axis_index("crow"), width) - sub_ref[...]
    out_ref[...] = back_apply(target, low_ref, inv_ref)


def solve_spread_kernel(direction_ref, sub_ref, more_ref, low_ref, inv_ref, fh_ref, fl_ref, out_ref, next_ref):
    width = sub_ref.shape[1]
    target = cut(direction_ref, lax.axis_index("crow"), width) - sub_ref[...]
    piece = back_apply(target, low_ref, inv_ref)
    out_ref[...] = piece
    next_ref[...] = more_ref[...] + times_pair(piece, fh_ref[...], fl_ref[...], NN)


def pick_kernel(places, *refs):
    row, col = lax.axis_index("crow"), lax.axis_index("ccol")
    out = jnp.zeros_like(refs[0][...])
    for (r, c), ref in zip(places, refs[:-1]):
        out = jnp.where((row == r) & (col == c), ref[...], out)
    refs[-1][...] = out


def solve_pick_kernel(places, direction_ref, sub_ref, low_ref, inv_ref, *refs):
    width = sub_ref.shape[1]
    row, col = lax.axis_index("crow"), lax.axis_index("ccol")
    target = cut(direction_ref, row, width) - sub_ref[...]
    out = jnp.where((row == 0) & (col == 0), back_apply(target, low_ref, inv_ref), 0.0)
    for (r, c), ref in zip(places, refs[:-1]):
        out = jnp.where((row == r) & (col == c), ref[...], out)
    refs[-1][...] = out


def triple(value):
    high, middle = pair(value)
    rest = value - high.astype(jnp.float32) - middle.astype(jnp.float32)
    return high, middle, rest.astype(jnp.bfloat16)


def norm_rows(norm, inputs):
    row = lax.broadcasted_iota(jnp.int32, (inputs, norm.shape[1]), 0)
    wide = jnp.broadcast_to(norm, (inputs, norm.shape[1]))
    high, middle, low = (part.astype(jnp.float32) for part in triple(wide))
    rows = jnp.where(row == 0, high, jnp.where(row == 1, middle, jnp.where(row == 2, low, 0.0)))
    return rows.astype(jnp.bfloat16)


def ones_rows(norm, inputs):
    row = lax.broadcasted_iota(jnp.int32, (inputs, norm.shape[1]), 0)
    return jnp.where(row < 3, 1.0, 0.0).astype(jnp.bfloat16)


def scale_by(value, scales_ref):
    inputs = value.shape[0]
    row = lax.broadcasted_iota(jnp.int32, value.shape, 0)
    scales = jnp.full(value.shape, scales_ref[0], jnp.float32)
    for n in range(1, inputs):
        scales = jnp.where(row == n, scales_ref[n], scales)
    return value / scales


def tile_kernel(scales_ref, centres_ref, data_ref, high_ref, low_ref, right):
    inputs = data_ref.shape[0]

    @pl.when(pl.program_id(0) == 0)
    def _():
        scaled = scale_by(data_ref[...], scales_ref)
        norm = jnp.sum(scaled * scaled, axis=0, keepdims=True) * (-0.5 * LOG2E)
        high, middle, low = triple(scaled)
        right[...] = jnp.concatenate(
            [high, middle, high, middle, low, high, norm_rows(norm, inputs), ones_rows(norm, inputs)],
            axis=0,
        )

    scaled = scale_by(centres_ref[...], scales_ref)
    norm = jnp.sum(scaled * scaled, axis=0, keepdims=True) * (-0.5 * LOG2E)
    high, middle, low = triple(scaled * LOG2E)
    left = jnp.concatenate(
        [high, high, middle, middle, high, low, ones_rows(norm, inputs), norm_rows(norm, inputs)], axis=0
    )
    exponent = lax.dot_general(left, right[...], TN, preferred_element_type=jnp.float32)
    high, low = pair(jnp.exp2(exponent))
    high_ref[...] = high
    low_ref[...] = low


def image_kernel(*refs):
    part_refs = refs[:-4]
    high_ref, low_ref, mine_ref, out_ref = refs[-4:]
    piece = part_refs[0][...]
    for ref in part_refs[1:]:
        piece = piece + ref[...]
    mine_ref[...] = piece
    out_ref[...] = times_pair(piece, high_ref[...], low_ref[...], NN)


def normal_kernel(*refs):
    part_refs = refs[:-3]
    high_ref, low_ref, out_ref = refs[-3:]
    piece = part_refs[0][...]
    for ref in part_refs[1:]:
        piece = piece + ref[...]
    out_ref[...] = times_pair(piece, high_ref[...], low_ref[...], NT)


def source_kernel(scale, mine_ref, *refs):
    part_refs = refs[:-4]
    low_ref, inv_ref, out_ref, image_ref = refs[-4:]
    total = part_refs[0][...]
    for ref in part_refs[1:]:
        total = total + ref[...]
    normal = total * scale + ridge_weight * mine_ref[...]
    out_ref[...] = normal
    image_ref[...] = fore_apply(normal, low_ref, inv_ref)


def fore_kernel(step, count, sides, *refs):
    got_refs = refs[:count]
    side_refs = refs[count : count + sides]
    source_ref, fh_ref, fl_ref, low_ref, inv_ref, side_out, image_out = refs[count + sides :]
    row = lax.axis_index("crow")
    piece = got_refs[0][...]
    for at in range(1, count):
        piece = jnp.where(row == step + at, got_refs[at][...], piece)
    side = times_pair(piece, fh_ref[...], fl_ref[...], NT)
    for ref in side_refs:
        side = side + ref[...]
    side_out[...] = side
    image_out[...] = fore_apply(source_ref[...] - side, low_ref, inv_ref)


def sum_kernel(*refs):
    total = refs[0][...]
    for ref in refs[1:-1]:
        total = total + ref[...]
    refs[-1][...] = total


def final_kernel(iterate_ref, residual_ref, direction_ref, *refs):
    part_refs = refs[:-4]
    iterate_out, residual_out, direction_out, image_ref = refs[-4:]
    size = len(part_refs)
    width = part_refs[0].shape[1]
    row = lax.axis_index("crow")
    for step, ref in enumerate(part_refs):
        at = lax.rem(row - step + size, size)
        image_ref[:, pl.ds(pl.multiple_of(at * width, width), width)] = ref[...]
    residual = residual_ref[...]
    direction = direction_ref[...]
    image = image_ref[...]
    gamma = jnp.sum(residual * residual, axis=1, keepdims=True)
    curvature = jnp.sum(direction * image, axis=1, keepdims=True)
    alpha = gamma / curvature
    iterate_out[...] = iterate_ref[...] + alpha * direction
    new_residual = residual - alpha * image
    residual_out[...] = new_residual
    gamma_next = jnp.sum(new_residual * new_residual, axis=1, keepdims=True)
    direction_out[...] = new_residual + (gamma_next / gamma) * direction


def shaped(*shape):
    return jax.ShapeDtypeStruct(shape, jnp.float32)


def call(kernel, outs, *args, limit=12, cost=(10**6, 10**6), **options):
    return pl.pallas_call(
        kernel,
        out_shape=outs,
        compiler_params=pltpu.CompilerParams(vmem_limit_bytes=limit << 20),
        cost_estimate=pl.CostEstimate(flops=cost[0], bytes_accessed=cost[1], transcendentals=0),
        **options,
    )(*args)


def swap(size, one, other, still=False):
    to = list(range(size))
    to[one], to[other] = other, one
    if not still:
        rest = [n for n in range(size) if n not in (one, other)]
        for a, b in zip(rest[::2], rest[1::2]):
            to[a], to[b] = b, a
    return to


def keep(size):
    return list(range(size))


def per_device(data, centres, scales, factor, block_inv, iterate, residual, direction):
    crow, ccol = lax.axis_size("crow"), lax.axis_size("ccol")
    held, order = block_inv.shape[0], block_inv.shape[1]
    width = factor.shape[0]
    rows, total = direction.shape
    assert factor.shape[1] == width and crow == ccol and crow > 2
    part = shaped(rows, width)
    last = crow - 1

    def move(value, row_to, col_to):
        perm = [
            (r * ccol + c, row_to[r] * ccol + col_to[c]) for r in range(crow) for c in range(ccol)
        ]
        return lax.ppermute(value, ("crow", "ccol"), perm)

    def shifts(value, axis):
        size = lax.axis_size(axis)
        return [
            lax.ppermute(value, axis, [(s, (s + step) % size) for s in range(size)])
            for step in range(1, size)
        ]

    def with_tri(kernel, outs, *args):
        full = [pl.BlockSpec(a.shape, lambda i, n=a.ndim: (0,) * n) for a in args]
        tri = [pl.BlockSpec((order, order), lambda i, r=r, c=c: (r, c)) for r, c in blocks_of(held)]
        shape = outs.shape
        return call(
            kernel, outs, *args, *([factor] * len(tri)), grid=(1,), in_specs=full + tri,
            out_specs=pl.BlockSpec(shape, lambda i: (0, 0)),
        )

    piece = with_tri(first_kernel, part, direction, block_inv)
    found = {last: piece}
    low = with_tri(lower_kernel, shaped(order, len(blocks_of(held)) * order), block_inv)
    wide = jax.ShapeDtypeStruct((width, width), jnp.bfloat16)
    high_f, low_f = call(pair_kernel, [wide, wide], factor)
    near = lax.ppermute(low, "ccol", [((c + 1) % ccol, c) for c in range(ccol)])

    samples = data.shape[1]
    tile = order
    inputs = data.shape[0]
    kernel_shape = jax.ShapeDtypeStruct((width, samples), jnp.bfloat16)
    high_k, low_k = call(
        tile_kernel, [kernel_shape] * 2, scales, centres, data,
        grid=(width // tile,),
        in_specs=[
            pl.BlockSpec(memory_space=pltpu.SMEM),
            pl.BlockSpec((inputs, tile), lambda i: (0, i)),
            pl.BlockSpec((inputs, samples), lambda i: (0, 0)),
        ],
        out_specs=[pl.BlockSpec((tile, samples), lambda i: (i, 0))] * 2,
        scratch_shapes=[pltpu.VMEM((8 * inputs, samples), jnp.bfloat16)],
        limit=20,
    )

    sums = []
    for step in range(last, 1, -1):
        cols = list(range(step))[::-1]
        got = [move(piece, keep(crow), swap(ccol, step, c)) for c in cols]
        sums = call(
            functools.partial(spread_kernel, step, cols), part, *sums, *got, high_f, low_f
        )
        if step > 2:
            sub = move(sums, swap(crow, step, step - 1), keep(ccol))
            piece = call(solve_kernel, part, direction, sub, low, block_inv)
            found[step - 1] = piece
            sums = [sub]
    sub = move(sums, swap(crow, 2, 1), swap(ccol, 1, 0))
    more = move(sums, swap(crow, 2, 1), keep(ccol))
    second, sums = call(
        solve_spread_kernel, [part, part], direction, sub, more, near, block_inv, high_f, low_f
    )
    sub = move(sums, swap(crow, 1, 0), keep(ccol))
    found[1] = move(second, keep(crow), swap(ccol, 0, 1))
    places = [(n, n) for n in range(1, crow)]
    own = call(
        functools.partial(solve_pick_kernel, places), part, direction, sub, low, block_inv,
        *[found[n] for n in range(1, crow)],
    )

    parts = [own] + shifts(own, "crow")
    chunk = samples // 4
    small = pl.BlockSpec((rows, width), lambda i: (0, 0))
    tall = pl.BlockSpec((width, chunk), lambda i: (0, i))
    mine, images = call(
        image_kernel, [part, shaped(rows, samples)], *parts, high_k, low_k,
        grid=(samples // chunk,),
        in_specs=[small] * crow + [tall, tall],
        out_specs=[small, pl.BlockSpec((rows, chunk), lambda i: (0, i))],
        limit=20,
    )
    images = [images] + shifts(images, "ccol")
    long = pl.BlockSpec((rows, samples), lambda i: (0, 0))
    flat = pl.BlockSpec((tile, samples), lambda i: (i, 0))
    summed = call(
        normal_kernel, part, *images, high_k, low_k,
        grid=(width // tile,),
        in_specs=[long] * ccol + [flat, flat],
        out_specs=pl.BlockSpec((rows, tile), lambda i: (0, i)),
        limit=20,
    )
    dp = lax.axis_size("dp")
    if dp == 2:
        summed = summed + lax.ppermute(summed, "dp", [(0, 1), (1, 0)])
    else:
        summed = lax.psum(summed, "dp")
    parts = [summed] + shifts(summed, "crow")
    scale = 1.0 / (samples * dp * crow)
    source, image = call(
        functools.partial(source_kernel, scale), [part, part], mine, *parts, low, block_inv
    )
    source = lax.ppermute(source, "ccol", [((c + 1) % ccol, c) for c in range(ccol)])
    done = [image]
    places = [(0, 0)]
    side = []
    for step in range(1, crow):
        before = max(step - 2, 0)
        still = step > 1
        cols = swap(ccol, before, step - 1, True) if still else keep(ccol)
        got = [move(image, swap(crow, step - 1, at), cols) for at in range(step, crow)]
        if side:
            side = [move(side[0], keep(crow), swap(ccol, before, step - 1))]
        out = call(
            functools.partial(fore_kernel, step, len(got), len(side)), [part, part],
            *got, *side, source, high_f, low_f, near, block_inv,
        )
        side, image = [out[0]], out[1]
        done.append(image)
        places.append((step, step - 1))
    own = call(functools.partial(pick_kernel, places), part, *done)
    own = call(sum_kernel, part, own, *shifts(own, "ccol"))
    full = shaped(rows, total)
    return tuple(
        call(
            final_kernel, [full, full, full], iterate, residual, direction, own, *shifts(own, "crow"),
            scratch_shapes=[pltpu.VMEM((rows, total), jnp.float32)],
        )
    )


def solution(mesh):
    placed = (
        P(None, ("dp", "crow")),
        P(None, "ccol"),
        P(),
        P("crow", "ccol"),
        P("crow", None, None),
        P(),
        P(),
        P(),
    )
    return jax.shard_map(
        per_device, mesh=mesh, in_specs=placed, out_specs=(P(), P(), P()), check_vma=False
    )
```

```python
import functools
import math

import jax
import jax.numpy as jnp
from jax import lax
from jax.experimental import pallas as pl
from jax.experimental.pallas import tpu as pltpu
from jax.sharding import PartitionSpec as P

ridge_weight = 0.2
LOG2E = 1.0 / math.log(2.0)
NN = (((1,), (0,)), ((), ()))
NT = (((1,), (1,)), ((), ()))
TN = (((0,), (0,)), ((), ()))


def pair(value):
    high = value.astype(jnp.bfloat16)
    low = (value - high.astype(jnp.float32)).astype(jnp.bfloat16)
    return high, low


def stacked(value):
    high, low = pair(value)
    return jnp.concatenate([high, low], axis=0)


def fold(product, rows):
    return product[:rows] + product[rows:]


def times_pair(rows, high, low, dims):
    both = stacked(rows)
    out = lax.dot_general(both, high, dims, preferred_element_type=jnp.float32)
    out = out + lax.dot_general(both, low, dims, preferred_element_type=jnp.float32)
    return fold(out, rows.shape[0])


def times(rows, matrix, dims):
    high, low = pair(matrix)
    return times_pair(rows, high, low, dims)


def blocks_of(held):
    return [(r, c) for r in range(1, held) for c in range(r)]


def lower(low_ref, order, r, c):
    at = r * (r - 1) // 2 + c
    return low_ref[:, at * order : (at + 1) * order]


def square(one, other):
    first, first_low = pair(one)
    second, second_low = pair(other)
    out = lax.dot_general(first, second, NN, preferred_element_type=jnp.float32)
    out = out + lax.dot_general(first, second_low, NN, preferred_element_type=jnp.float32)
    return out + lax.dot_general(first_low, second, NN, preferred_element_type=jnp.float32)


def cut(ref, at, width):
    return ref[:, pl.ds(pl.multiple_of(at * width, width), width)]


def back_apply(target, low_ref, inv_ref):
    held, order = inv_ref.shape[0], inv_ref.shape[1]
    parts = [target[:, n * order : (n + 1) * order] for n in range(held)]
    pieces = []
    for c in range(held):
        piece = times(parts[c], inv_ref[c], NN)
        for r in range(c + 1, held):
            piece = piece + times(parts[r], lower(low_ref, order, r, c), NN)
        pieces.append(piece)
    return jnp.concatenate(pieces, axis=1)


def fore_apply(source, low_ref, inv_ref):
    held, order = inv_ref.shape[0], inv_ref.shape[1]
    parts = [source[:, n * order : (n + 1) * order] for n in range(held)]
    pieces = []
    for r in range(held):
        piece = times(parts[r], inv_ref[r], NT)
        for c in range(r):
            piece = piece + times(parts[c], lower(low_ref, order, r, c), NT)
        pieces.append(piece)
    return jnp.concatenate(pieces, axis=1)


def first_kernel(direction_ref, inv_ref, *refs):
    tri_refs, out_ref = refs[:-1], refs[-1]
    held, order = inv_ref.shape[0], inv_ref.shape[1]
    width = held * order
    tri = dict(zip(blocks_of(held), tri_refs))
    target = cut(direction_ref, lax.axis_index("crow"), width)
    pieces = [None] * held
    for number in reversed(range(held)):
        part = target[:, number * order : (number + 1) * order]
        for later in range(number + 1, held):
            part = part - times(pieces[later], tri[later, number][...], NN)
        pieces[number] = times(part, inv_ref[number], NN)
    out_ref[...] = jnp.concatenate(pieces, axis=1)


def lower_kernel(after_ref, inv_ref, *refs):
    tri_refs, out_ref = refs[:-1], refs[-1]
    held, order = inv_ref.shape[0], inv_ref.shape[1]
    tri = dict(zip(blocks_of(held), tri_refs))
    found = {(n, n): inv_ref[n] for n in range(held)}
    for r in range(1, held):
        for c in range(r):
            total = square(tri[r, c][...], found[c, c])
            for between in range(c + 1, r):
                total = total + square(tri[r, between][...], found[between, c])
            found[r, c] = -square(inv_ref[r], total)
            at = r * (r - 1) // 2 + c
            out_ref[:, at * order : (at + 1) * order] = found[r, c]


def pair_kernel(factor_ref, high_ref, low_ref):
    high, low = pair(factor_ref[...])
    high_ref[...] = high
    low_ref[...] = low


def spread_kernel(step, cols, *refs):
    extra = refs[: len(refs) - 3 - len(cols)]
    got_refs = refs[len(extra) : len(extra) + len(cols)]
    high_ref, low_ref, out_ref = refs[-3:]
    col = lax.axis_index("ccol")
    piece = got_refs[0][...]
    for at, got in zip(cols[1:], got_refs[1:]):
        piece = jnp.where(col == at, got[...], piece)
    out = times_pair(piece, high_ref[...], low_ref[...], NN)
    for ref in extra:
        out = out + ref[...]
    out_ref[...] = out


def solve_kernel(direction_ref, sub_ref, low_ref, inv_ref, out_ref):
    width = sub_ref.shape[1]
    target = cut(direction_ref, lax.axis_index("crow"), width) - sub_ref[...]
    out_ref[...] = back_apply(target, low_ref, inv_ref)


def solve_spread_kernel(direction_ref, sub_ref, more_ref, low_ref, inv_ref, fh_ref, fl_ref, out_ref, next_ref):
    width = sub_ref.shape[1]
    target = cut(direction_ref, lax.axis_index("crow"), width) - sub_ref[...]
    piece = back_apply(target, low_ref, inv_ref)
    out_ref[...] = piece
    next_ref[...] = more_ref[...] + times_pair(piece, fh_ref[...], fl_ref[...], NN)


def pick_kernel(places, *refs):
    row, col = lax.axis_index("crow"), lax.axis_index("ccol")
    out = jnp.zeros_like(refs[0][...])
    for (r, c), ref in zip(places, refs[:-1]):
        out = jnp.where((row == r) & (col == c), ref[...], out)
    refs[-1][...] = out


def solve_pick_kernel(places, direction_ref, sub_ref, low_ref, inv_ref, *refs):
    width = sub_ref.shape[1]
    row, col = lax.axis_index("crow"), lax.axis_index("ccol")
    target = cut(direction_ref, row, width) - sub_ref[...]
    out = jnp.where((row == 0) & (col == 0), back_apply(target, low_ref, inv_ref), 0.0)
    for (r, c), ref in zip(places, refs[:-1]):
        out = jnp.where((row == r) & (col == c), ref[...], out)
    refs[-1][...] = out


def triple(value):
    high, middle = pair(value)
    rest = value - high.astype(jnp.float32) - middle.astype(jnp.float32)
    return high, middle, rest.astype(jnp.bfloat16)


def norm_rows(norm, inputs):
    row = lax.broadcasted_iota(jnp.int32, (inputs, norm.shape[1]), 0)
    wide = jnp.broadcast_to(norm, (inputs, norm.shape[1]))
    high, middle, low = (part.astype(jnp.float32) for part in triple(wide))
    rows = jnp.where(row == 0, high, jnp.where(row == 1, middle, jnp.where(row == 2, low, 0.0)))
    return rows.astype(jnp.bfloat16)


def ones_rows(norm, inputs):
    row = lax.broadcasted_iota(jnp.int32, (inputs, norm.shape[1]), 0)
    return jnp.where(row < 3, 1.0, 0.0).astype(jnp.bfloat16)


def scale_by(value, scales_ref):
    inputs = value.shape[0]
    row = lax.broadcasted_iota(jnp.int32, value.shape, 0)
    scales = jnp.full(value.shape, scales_ref[0], jnp.float32)
    for n in range(1, inputs):
        scales = jnp.where(row == n, scales_ref[n], scales)
    return value / scales


def tile_kernel(scales_ref, centres_ref, data_ref, high_ref, low_ref, right):
    inputs = data_ref.shape[0]

    @pl.when(pl.program_id(0) == 0)
    def _():
        scaled = scale_by(data_ref[...], scales_ref)
        norm = jnp.sum(scaled * scaled, axis=0, keepdims=True) * (-0.5 * LOG2E)
        high, middle, low = triple(scaled)
        right[...] = jnp.concatenate(
            [high, middle, high, middle, low, high, norm_rows(norm, inputs), ones_rows(norm, inputs)],
            axis=0,
        )

    scaled = scale_by(centres_ref[...], scales_ref)
    norm = jnp.sum(scaled * scaled, axis=0, keepdims=True) * (-0.5 * LOG2E)
    high, middle, low = triple(scaled * LOG2E)
    left = jnp.concatenate(
        [high, high, middle, middle, high, low, ones_rows(norm, inputs), norm_rows(norm, inputs)], axis=0
    )
    exponent = lax.dot_general(left, right[...], TN, preferred_element_type=jnp.float32)
    high, low = pair(jnp.exp2(exponent))
    high_ref[...] = high
    low_ref[...] = low


def image_kernel(*refs):
    part_refs = refs[:-4]
    high_ref, low_ref, mine_ref, out_ref = refs[-4:]
    piece = part_refs[0][...]
    for ref in part_refs[1:]:
        piece = piece + ref[...]
    mine_ref[...] = piece
    out_ref[...] = times_pair(piece, high_ref[...], low_ref[...], NN)


def normal_kernel(*refs):
    part_refs = refs[:-3]
    high_ref, low_ref, out_ref = refs[-3:]
    piece = part_refs[0][...]
    for ref in part_refs[1:]:
        piece = piece + ref[...]
    out_ref[...] = times_pair(piece, high_ref[...], low_ref[...], NT)


def source_kernel(scale, mine_ref, *refs):
    part_refs = refs[:-4]
    low_ref, inv_ref, out_ref, image_ref = refs[-4:]
    total = part_refs[0][...]
    for ref in part_refs[1:]:
        total = total + ref[...]
    normal = total * scale + ridge_weight * mine_ref[...]
    out_ref[...] = normal
    image_ref[...] = fore_apply(normal, low_ref, inv_ref)


def fore_kernel(step, count, sides, *refs):
    got_refs = refs[:count]
    side_refs = refs[count : count + sides]
    source_ref, fh_ref, fl_ref, low_ref, inv_ref, side_out, image_out = refs[count + sides :]
    row = lax.axis_index("crow")
    piece = got_refs[0][...]
    for at in range(1, count):
        piece = jnp.where(row == step + at, got_refs[at][...], piece)
    side = times_pair(piece, fh_ref[...], fl_ref[...], NT)
    for ref in side_refs:
        side = side + ref[...]
    side_out[...] = side
    image_out[...] = fore_apply(source_ref[...] - side, low_ref, inv_ref)


def sum_kernel(*refs):
    total = refs[0][...]
    for ref in refs[1:-1]:
        total = total + ref[...]
    refs[-1][...] = total


def final_kernel(iterate_ref, residual_ref, direction_ref, *refs):
    part_refs = refs[:-4]
    iterate_out, residual_out, direction_out, image_ref = refs[-4:]
    size = len(part_refs)
    width = part_refs[0].shape[1]
    row = lax.axis_index("crow")
    for step, ref in enumerate(part_refs):
        at = row ^ step
        image_ref[:, pl.ds(pl.multiple_of(at * width, width), width)] = ref[...]
    residual = residual_ref[...]
    direction = direction_ref[...]
    image = image_ref[...]
    gamma = jnp.sum(residual * residual, axis=1, keepdims=True)
    curvature = jnp.sum(direction * image, axis=1, keepdims=True)
    alpha = gamma / curvature
    iterate_out[...] = iterate_ref[...] + alpha * direction
    new_residual = residual - alpha * image
    residual_out[...] = new_residual
    gamma_next = jnp.sum(new_residual * new_residual, axis=1, keepdims=True)
    direction_out[...] = new_residual + (gamma_next / gamma) * direction


def shaped(*shape):
    return jax.ShapeDtypeStruct(shape, jnp.float32)


def call(kernel, outs, *args, limit=12, cost=(10**6, 10**6), **options):
    return pl.pallas_call(
        kernel,
        out_shape=outs,
        compiler_params=pltpu.CompilerParams(vmem_limit_bytes=limit << 20),
        cost_estimate=pl.CostEstimate(flops=cost[0], bytes_accessed=cost[1], transcendentals=0),
        **options,
    )(*args)


def swap(size, one, other, still=False):
    to = list(range(size))
    to[one], to[other] = other, one
    if not still:
        rest = [n for n in range(size) if n not in (one, other)]
        for a, b in zip(rest[::2], rest[1::2]):
            to[a], to[b] = b, a
    return to


def keep(size):
    return list(range(size))


def per_device(data, centres, scales, factor, block_inv, iterate, residual, direction):
    crow, ccol = lax.axis_size("crow"), lax.axis_size("ccol")
    held, order = block_inv.shape[0], block_inv.shape[1]
    width = factor.shape[0]
    rows, total = direction.shape
    assert factor.shape[1] == width and crow == ccol and crow in (4, 8)
    part = shaped(rows, width)
    last = crow - 1

    def move(value, row_to, col_to):
        perm = [
            (r * ccol + c, row_to[r] * ccol + col_to[c]) for r in range(crow) for c in range(ccol)
        ]
        return lax.ppermute(value, ("crow", "ccol"), perm)

    def shifts(value, axis):
        size = lax.axis_size(axis)
        return [
            lax.ppermute(value, axis, [(s, s ^ step) for s in range(size)]) for step in range(1, size)
        ]

    def with_tri(kernel, outs, *args):
        full = [pl.BlockSpec(a.shape, lambda i, n=a.ndim: (0,) * n) for a in args]
        tri = [pl.BlockSpec((order, order), lambda i, r=r, c=c: (r, c)) for r, c in blocks_of(held)]
        shape = outs.shape
        return call(
            kernel, outs, *args, *([factor] * len(tri)), grid=(1,), in_specs=full + tri,
            out_specs=pl.BlockSpec(shape, lambda i: (0, 0)),
        )

    piece = with_tri(first_kernel, part, direction, block_inv)
    found = {last: piece}
    low = with_tri(lower_kernel, shaped(order, len(blocks_of(held)) * order), piece, block_inv)
    wide = jax.ShapeDtypeStruct((width, width), jnp.bfloat16)
    high_f, low_f = call(pair_kernel, [wide, wide], factor)

    def lend(value, givers):
        perm = [(r * ccol + r, r * ccol + r - 1) for r in givers]
        return lax.ppermute(value, ("crow", "ccol"), perm)

    near = lend(low, [1])

    samples = data.shape[1]
    tile = order
    inputs = data.shape[0]
    kernel_shape = jax.ShapeDtypeStruct((width, samples), jnp.bfloat16)
    high_k, low_k = call(
        tile_kernel, [kernel_shape] * 2, scales, centres, data,
        grid=(width // tile,),
        in_specs=[
            pl.BlockSpec(memory_space=pltpu.SMEM),
            pl.BlockSpec((inputs, tile), lambda i: (0, i)),
            pl.BlockSpec((inputs, samples), lambda i: (0, 0)),
        ],
        out_specs=[pl.BlockSpec((tile, samples), lambda i: (i, 0))] * 2,
        scratch_shapes=[pltpu.VMEM((8 * inputs, samples), jnp.bfloat16)],
        limit=20,
    )

    sums = []
    for step in range(last, 1, -1):
        cols = list(range(step))[::-1]
        got = [move(piece, keep(crow), swap(ccol, step, c)) for c in cols]
        sums = call(
            functools.partial(spread_kernel, step, cols), part, *sums, *got, high_f, low_f
        )
        if step > 2:
            sub = move(sums, swap(crow, step, step - 1), keep(ccol))
            piece = call(solve_kernel, part, direction, sub, low, block_inv)
            found[step - 1] = piece
            sums = [sub]
    sub = move(sums, swap(crow, 2, 1), swap(ccol, 1, 0))
    more = move(sums, swap(crow, 2, 1), keep(ccol))
    second, sums = call(
        solve_spread_kernel, [part, part], direction, sub, more, near, block_inv, high_f, low_f
    )
    late, _ = lax.optimization_barrier((low, sums))
    near_late = lend(late, range(2, crow))
    sub = move(sums, swap(crow, 1, 0), keep(ccol))
    found[1] = move(second, keep(crow), swap(ccol, 0, 1))
    places = [(n, n) for n in range(1, crow)]
    own = call(
        functools.partial(solve_pick_kernel, places), part, direction, sub, low, block_inv,
        *[found[n] for n in range(1, crow)],
    )

    parts = [own] + shifts(own, "crow")
    chunk = samples // 4
    small = pl.BlockSpec((rows, width), lambda i: (0, 0))
    tall = pl.BlockSpec((width, chunk), lambda i: (0, i))
    mine, images = call(
        image_kernel, [part, shaped(rows, samples)], *parts, high_k, low_k,
        grid=(samples // chunk,),
        in_specs=[small] * crow + [tall, tall],
        out_specs=[small, pl.BlockSpec((rows, chunk), lambda i: (0, i))],
        limit=20,
    )
    images = [images] + shifts(images, "ccol")
    long = pl.BlockSpec((rows, samples), lambda i: (0, 0))
    flat = pl.BlockSpec((tile, samples), lambda i: (i, 0))
    summed = call(
        normal_kernel, part, *images, high_k, low_k,
        grid=(width // tile,),
        in_specs=[long] * ccol + [flat, flat],
        out_specs=pl.BlockSpec((rows, tile), lambda i: (0, i)),
        limit=20,
    )
    dp = lax.axis_size("dp")
    if dp == 2:
        summed = summed + lax.ppermute(summed, "dp", [(0, 1), (1, 0)])
    else:
        summed = lax.psum(summed, "dp")
    parts = [summed] + shifts(summed, "crow")
    scale = 1.0 / (samples * dp * crow)
    source, image = call(
        functools.partial(source_kernel, scale), [part, part], mine, *parts, low, block_inv
    )
    source = lax.ppermute(source, "ccol", [((c + 1) % ccol, c) for c in range(ccol)])
    done = [image]
    places = [(0, 0)]
    side = []
    for step in range(1, crow):
        before = max(step - 2, 0)
        still = step > 1
        cols = swap(ccol, before, step - 1, True) if still else keep(ccol)
        got = [move(image, swap(crow, step - 1, at), cols) for at in range(step, crow)]
        if side:
            side = [move(side[0], keep(crow), swap(ccol, before, step - 1))]
        out = call(
            functools.partial(fore_kernel, step, len(got), len(side)), [part, part],
            *got, *side, source, high_f, low_f, near if step == 1 else near_late, block_inv,
        )
        side, image = [out[0]], out[1]
        done.append(image)
        places.append((step, step - 1))
    own = call(functools.partial(pick_kernel, places), part, *done)
    own = call(sum_kernel, part, own, *shifts(own, "ccol"))
    full = shaped(rows, total)
    return tuple(
        call(
            final_kernel, [full, full, full], iterate, residual, direction, own, *shifts(own, "crow"),
            scratch_shapes=[pltpu.VMEM((rows, total), jnp.float32)],
        )
    )


def solution(mesh):
    placed = (
        P(None, ("dp", "crow")),
        P(None, "ccol"),
        P(),
        P("crow", "ccol"),
        P("crow", None, None),
        P(),
        P(),
        P(),
    )
    return jax.shard_map(
        per_device, mesh=mesh, in_specs=placed, out_specs=(P(), P(), P()), check_vma=False
    )
```

```python
import functools
import math

import jax
import jax.numpy as jnp
from jax import lax
from jax.experimental import pallas as pl
from jax.experimental.pallas import tpu as pltpu
from jax.sharding import PartitionSpec as P

ridge_weight = 0.2
LOG2E = 1.0 / math.log(2.0)
NN = (((1,), (0,)), ((), ()))
NT = (((1,), (1,)), ((), ()))
TN = (((0,), (0,)), ((), ()))


def pair(value):
    high = value.astype(jnp.bfloat16)
    low = (value - high.astype(jnp.float32)).astype(jnp.bfloat16)
    return high, low


def stacked(value):
    high, low = pair(value)
    return jnp.concatenate([high, low], axis=0)


def fold(product, rows):
    return product[:rows] + product[rows:]


def times_pair(rows, high, low, dims):
    both = stacked(rows)
    out = lax.dot_general(both, high, dims, preferred_element_type=jnp.float32)
    out = out + lax.dot_general(both, low, dims, preferred_element_type=jnp.float32)
    return fold(out, rows.shape[0])


def times(rows, matrix, dims):
    high, low = pair(matrix)
    return times_pair(rows, high, low, dims)


def blocks_of(held):
    return [(r, c) for r in range(1, held) for c in range(r)]


def lower(low_ref, order, r, c):
    at = r * (r - 1) // 2 + c
    return low_ref[:, at * order : (at + 1) * order]


def square(one, other):
    first, first_low = pair(one)
    second, second_low = pair(other)
    out = lax.dot_general(first, second, NN, preferred_element_type=jnp.float32)
    out = out + lax.dot_general(first, second_low, NN, preferred_element_type=jnp.float32)
    return out + lax.dot_general(first_low, second, NN, preferred_element_type=jnp.float32)


def cut(ref, at, width):
    return ref[:, pl.ds(pl.multiple_of(at * width, width), width)]


def back_apply(target, low_ref, inv_ref):
    held, order = inv_ref.shape[0], inv_ref.shape[1]
    parts = [target[:, n * order : (n + 1) * order] for n in range(held)]
    pieces = []
    for c in range(held):
        piece = times(parts[c], inv_ref[c], NN)
        for r in range(c + 1, held):
            piece = piece + times(parts[r], lower(low_ref, order, r, c), NN)
        pieces.append(piece)
    return jnp.concatenate(pieces, axis=1)


def fore_apply(source, low_ref, inv_ref):
    held, order = inv_ref.shape[0], inv_ref.shape[1]
    parts = [source[:, n * order : (n + 1) * order] for n in range(held)]
    pieces = []
    for r in range(held):
        piece = times(parts[r], inv_ref[r], NT)
        for c in range(r):
            piece = piece + times(parts[c], lower(low_ref, order, r, c), NT)
        pieces.append(piece)
    return jnp.concatenate(pieces, axis=1)


def first_kernel(direction_ref, inv_ref, *refs):
    tri_refs, out_ref = refs[:-1], refs[-1]
    held, order = inv_ref.shape[0], inv_ref.shape[1]
    width = held * order
    tri = dict(zip(blocks_of(held), tri_refs))
    target = cut(direction_ref, lax.axis_index("crow"), width)
    pieces = [None] * held
    for number in reversed(range(held)):
        part = target[:, number * order : (number + 1) * order]
        for later in range(number + 1, held):
            part = part - times(pieces[later], tri[later, number][...], NN)
        pieces[number] = times(part, inv_ref[number], NN)
    out_ref[...] = jnp.concatenate(pieces, axis=1)


def lower_kernel(after_ref, inv_ref, *refs):
    tri_refs, out_ref = refs[:-1], refs[-1]
    held, order = inv_ref.shape[0], inv_ref.shape[1]
    tri = dict(zip(blocks_of(held), tri_refs))
    found = {(n, n): inv_ref[n] for n in range(held)}
    for r in range(1, held):
        for c in range(r):
            total = square(tri[r, c][...], found[c, c])
            for between in range(c + 1, r):
                total = total + square(tri[r, between][...], found[between, c])
            found[r, c] = -square(inv_ref[r], total)
            at = r * (r - 1) // 2 + c
            out_ref[:, at * order : (at + 1) * order] = found[r, c]


def pair_kernel(factor_ref, high_ref, low_ref):
    high, low = pair(factor_ref[...])
    high_ref[...] = high
    low_ref[...] = low


def spread_kernel(cols, lend, *refs):
    outs = refs[len(refs) - 1 - lend :]
    refs = refs[: len(refs) - 1 - lend]
    if lend:
        low_of, half = refs[-1], outs[1]
        tall = half.shape[0]
        at = lax.rem(lax.axis_index("dp"), 2) * tall
        half[...] = low_of[pl.ds(pl.multiple_of(at, tall), tall), :]
        refs = refs[:-1]
    extra = refs[: len(refs) - 2 - len(cols)]
    got_refs = refs[len(extra) : len(extra) + len(cols)]
    high_ref, low_ref = refs[-2:]
    col = lax.axis_index("ccol")
    piece = got_refs[0][...]
    for at, got in zip(cols[1:], got_refs[1:]):
        piece = jnp.where(col == at, got[...], piece)
    out = times_pair(piece, high_ref[...], low_ref[...], NN)
    for ref in extra:
        out = out + ref[...]
    outs[0][...] = out


def merge_kernel(mine_ref, other_ref, out_ref):
    tall = mine_ref.shape[0]
    odd = lax.rem(lax.axis_index("dp"), 2)
    out_ref[pl.ds(pl.multiple_of(odd * tall, tall), tall), :] = mine_ref[...]
    out_ref[pl.ds(pl.multiple_of((1 - odd) * tall, tall), tall), :] = other_ref[...]


def solve_kernel(direction_ref, sub_ref, low_ref, inv_ref, out_ref):
    width = sub_ref.shape[1]
    target = cut(direction_ref, lax.axis_index("crow"), width) - sub_ref[...]
    out_ref[...] = back_apply(target, low_ref, inv_ref)


def pick_kernel(places, *refs):
    row, col = lax.axis_index("crow"), lax.axis_index("ccol")
    out = jnp.zeros_like(refs[0][...])
    for (r, c), ref in zip(places, refs[:-1]):
        out = jnp.where((row == r) & (col == c), ref[...], out)
    refs[-1][...] = out


def solve_pick_kernel(places, direction_ref, sub_ref, low_ref, inv_ref, *refs):
    width = sub_ref.shape[1]
    row, col = lax.axis_index("crow"), lax.axis_index("ccol")
    target = cut(direction_ref, row, width) - sub_ref[...]
    out = jnp.where((row == 0) & (col == 0), back_apply(target, low_ref, inv_ref), 0.0)
    for (r, c), ref in zip(places, refs[:-1]):
        out = jnp.where((row == r) & (col == c), ref[...], out)
    refs[-1][...] = out


def triple(value):
    high, middle = pair(value)
    rest = value - high.astype(jnp.float32) - middle.astype(jnp.float32)
    return high, middle, rest.astype(jnp.bfloat16)


def norm_rows(norm, inputs):
    row = lax.broadcasted_iota(jnp.int32, (inputs, norm.shape[1]), 0)
    wide = jnp.broadcast_to(norm, (inputs, norm.shape[1]))
    high, middle, low = (part.astype(jnp.float32) for part in triple(wide))
    rows = jnp.where(row == 0, high, jnp.where(row == 1, middle, jnp.where(row == 2, low, 0.0)))
    return rows.astype(jnp.bfloat16)


def ones_rows(norm, inputs):
    row = lax.broadcasted_iota(jnp.int32, (inputs, norm.shape[1]), 0)
    return jnp.where(row < 3, 1.0, 0.0).astype(jnp.bfloat16)


def scale_by(value, scales_ref):
    inputs = value.shape[0]
    row = lax.broadcasted_iota(jnp.int32, value.shape, 0)
    scales = jnp.full(value.shape, scales_ref[0], jnp.float32)
    for n in range(1, inputs):
        scales = jnp.where(row == n, scales_ref[n], scales)
    return value / scales


def tile_kernel(scales_ref, centres_ref, data_ref, high_ref, low_ref, right):
    inputs = data_ref.shape[0]

    @pl.when(pl.program_id(0) == 0)
    def _():
        scaled = scale_by(data_ref[...], scales_ref)
        norm = jnp.sum(scaled * scaled, axis=0, keepdims=True) * (-0.5 * LOG2E)
        high, middle, low = triple(scaled)
        right[...] = jnp.concatenate(
            [high, middle, high, middle, low, high, norm_rows(norm, inputs), ones_rows(norm, inputs)],
            axis=0,
        )

    scaled = scale_by(centres_ref[...], scales_ref)
    norm = jnp.sum(scaled * scaled, axis=0, keepdims=True) * (-0.5 * LOG2E)
    high, middle, low = triple(scaled * LOG2E)
    left = jnp.concatenate(
        [high, high, middle, middle, high, low, ones_rows(norm, inputs), norm_rows(norm, inputs)], axis=0
    )
    exponent = lax.dot_general(left, right[...], TN, preferred_element_type=jnp.float32)
    high, low = pair(jnp.exp2(exponent))
    high_ref[...] = high
    low_ref[...] = low


def image_kernel(*refs):
    part_refs = refs[:-6]
    high_ref, low_ref, half_ref, mine_ref, out_ref, half_out = refs[-6:]

    @pl.when(pl.program_id(0) == 0)
    def _():
        half_out[...] = half_ref[...]

    piece = part_refs[0][...]
    for ref in part_refs[1:]:
        piece = piece + ref[...]
    mine_ref[...] = piece
    out_ref[...] = times_pair(piece, high_ref[...], low_ref[...], NN)


def normal_kernel(*refs):
    part_refs = refs[:-3]
    high_ref, low_ref, out_ref = refs[-3:]
    piece = part_refs[0][...]
    for ref in part_refs[1:]:
        piece = piece + ref[...]
    out_ref[...] = times_pair(piece, high_ref[...], low_ref[...], NT)


def source_kernel(scale, mine_ref, *refs):
    part_refs = refs[:-4]
    low_ref, inv_ref, out_ref, image_ref = refs[-4:]
    total = part_refs[0][...]
    for ref in part_refs[1:]:
        total = total + ref[...]
    normal = total * scale + ridge_weight * mine_ref[...]
    out_ref[...] = normal
    image_ref[...] = fore_apply(normal, low_ref, inv_ref)


def fore_kernel(step, count, sides, *refs):
    got_refs = refs[:count]
    side_refs = refs[count : count + sides]
    source_ref, fh_ref, fl_ref, low_ref, inv_ref, side_out, image_out = refs[count + sides :]
    row = lax.axis_index("crow")
    piece = got_refs[0][...]
    for at in range(1, count):
        piece = jnp.where(row == step + at, got_refs[at][...], piece)
    side = times_pair(piece, fh_ref[...], fl_ref[...], NT)
    for ref in side_refs:
        side = side + ref[...]
    side_out[...] = side
    image_out[...] = fore_apply(source_ref[...] - side, low_ref, inv_ref)


def sum_kernel(*refs):
    total = refs[0][...]
    for ref in refs[1:-1]:
        total = total + ref[...]
    refs[-1][...] = total


def final_kernel(iterate_ref, residual_ref, direction_ref, *refs):
    part_refs = refs[:-4]
    iterate_out, residual_out, direction_out, image_ref = refs[-4:]
    size = len(part_refs)
    width = part_refs[0].shape[1]
    row = lax.axis_index("crow")
    for step, ref in enumerate(part_refs):
        at = row ^ step
        image_ref[:, pl.ds(pl.multiple_of(at * width, width), width)] = ref[...]
    residual = residual_ref[...]
    direction = direction_ref[...]
    image = image_ref[...]
    gamma = jnp.sum(residual * residual, axis=1, keepdims=True)
    curvature = jnp.sum(direction * image, axis=1, keepdims=True)
    alpha = gamma / curvature
    iterate_out[...] = iterate_ref[...] + alpha * direction
    new_residual = residual - alpha * image
    residual_out[...] = new_residual
    gamma_next = jnp.sum(new_residual * new_residual, axis=1, keepdims=True)
    direction_out[...] = new_residual + (gamma_next / gamma) * direction


def shaped(*shape):
    return jax.ShapeDtypeStruct(shape, jnp.float32)


def call(kernel, outs, *args, limit=12, cost=(10**6, 10**6), **options):
    return pl.pallas_call(
        kernel,
        out_shape=outs,
        compiler_params=pltpu.CompilerParams(vmem_limit_bytes=limit << 20),
        cost_estimate=pl.CostEstimate(flops=cost[0], bytes_accessed=cost[1], transcendentals=0),
        **options,
    )(*args)


def swap(size, one, other, still=False):
    to = list(range(size))
    to[one], to[other] = other, one
    if not still:
        rest = [n for n in range(size) if n not in (one, other)]
        for a, b in zip(rest[::2], rest[1::2]):
            to[a], to[b] = b, a
    return to


def keep(size):
    return list(range(size))


def per_device(data, centres, scales, factor, block_inv, iterate, residual, direction):
    dp, crow, ccol = lax.axis_size("dp"), lax.axis_size("crow"), lax.axis_size("ccol")
    held, order = block_inv.shape[0], block_inv.shape[1]
    width = factor.shape[0]
    rows, total = direction.shape
    assert factor.shape[1] == width and crow == ccol and crow in (4, 8) and dp % 2 == 0
    part = shaped(rows, width)
    last = crow - 1

    def spot(d, r, c):
        return (d * crow + r) * ccol + c

    def move(value, row_to, col_to, flip=1):
        perm = [
            (spot(d, r, c), spot(d ^ flip, row_to[r], col_to[c]))
            for d in range(dp)
            for r in range(crow)
            for c in range(ccol)
        ]
        return lax.ppermute(value, ("dp", "crow", "ccol"), perm)

    def shifts(value, axis, flip=1):
        out = []
        for step in range(1, lax.axis_size(axis)):
            other = [n ^ step for n in range(lax.axis_size(axis))]
            if axis == "crow":
                out.append(move(value, other, keep(ccol), flip))
            else:
                out.append(move(value, keep(crow), other, flip))
        return out

    def with_tri(kernel, outs, *args, limit=12):
        full = [pl.BlockSpec(a.shape, lambda i, n=a.ndim: (0,) * n) for a in args]
        tri = [pl.BlockSpec((order, order), lambda i, r=r, c=c: (r, c)) for r, c in blocks_of(held)]
        shape = outs.shape
        return call(
            kernel, outs, *args, *([factor] * len(tri)), grid=(1,), in_specs=full + tri,
            out_specs=pl.BlockSpec(shape, lambda i: (0, 0)), limit=limit,
        )

    piece = with_tri(first_kernel, part, direction, block_inv, limit=58)
    found = {last: piece}
    low = with_tri(lower_kernel, shaped(order, len(blocks_of(held)) * order), piece, block_inv)
    wide = jax.ShapeDtypeStruct((width, width), jnp.bfloat16)
    high_f, low_f = call(pair_kernel, [wide, wide], factor)

    samples = data.shape[1]
    tile = order
    inputs = data.shape[0]
    kernel_shape = jax.ShapeDtypeStruct((width, samples), jnp.bfloat16)
    high_k, low_k = call(
        tile_kernel, [kernel_shape] * 2, scales, centres, data,
        grid=(width // tile,),
        in_specs=[
            pl.BlockSpec(memory_space=pltpu.SMEM),
            pl.BlockSpec((inputs, tile), lambda i: (0, i)),
            pl.BlockSpec((inputs, samples), lambda i: (0, 0)),
        ],
        out_specs=[pl.BlockSpec((tile, samples), lambda i: (i, 0))] * 2,
        scratch_shapes=[pltpu.VMEM((8 * inputs, samples), jnp.bfloat16)],
        limit=20,
    )

    sums = []
    for step in range(last, 0, -1):
        cols = list(range(step))[::-1]
        got = [move(piece, keep(crow), swap(ccol, step, c)) for c in cols]
        outs = [part, shaped(order // 2, low.shape[1])] if step == 1 else [part]
        lend = [low] if step == 1 else []
        sums, *halves = call(
            functools.partial(spread_kernel, cols, len(outs) - 1), outs, *sums, *got, high_f, low_f, *lend
        )
        sums = [move(sums, swap(crow, step, step - 1), keep(ccol))]
        if step > 1:
            piece = call(solve_kernel, part, direction, *sums, low, block_inv)
            found[step - 1] = piece
    pairs = [((n, n), (n, n - 1)) for n in range(1, crow)]
    perm = [
        (spot(d, *one), spot(d, *other))
        for d in range(dp)
        for a, b in pairs
        for one, other in ((a, b), (b, a))
    ]
    half = lax.ppermute(halves[0], ("dp", "crow", "ccol"), perm)
    places = [(n, n) for n in range(1, crow)]
    own = call(
        functools.partial(solve_pick_kernel, places), part, direction, *sums, low, block_inv,
        *[found[n] for n in range(1, crow)],
    )

    parts = [own] + shifts(own, "crow")
    chunk = samples // 4
    small = pl.BlockSpec((rows, width), lambda i: (0, 0))
    tall = pl.BlockSpec((width, chunk), lambda i: (0, i))
    thin = pl.BlockSpec(half.shape, lambda i: (0, 0))
    mine, images, half = call(
        image_kernel, [part, shaped(rows, samples), shaped(*half.shape)], *parts, high_k, low_k, half,
        grid=(samples // chunk,),
        in_specs=[small] * crow + [tall, tall, thin],
        out_specs=[small, pl.BlockSpec((rows, chunk), lambda i: (0, i)), thin],
        limit=20,
    )
    images = [images] + shifts(images, "ccol", 0)
    near = call(merge_kernel, shaped(*low.shape), half, move(half, keep(crow), keep(ccol)))
    long = pl.BlockSpec((rows, samples), lambda i: (0, 0))
    flat = pl.BlockSpec((tile, samples), lambda i: (i, 0))
    summed = call(
        normal_kernel, part, *images, high_k, low_k,
        grid=(width // tile,),
        in_specs=[long] * ccol + [flat, flat],
        out_specs=pl.BlockSpec((rows, tile), lambda i: (0, i)),
        limit=20,
    )
    if dp == 2:
        summed = summed + lax.ppermute(summed, "dp", [(0, 1), (1, 0)])
    else:
        summed = lax.psum(summed, "dp")
    parts = [summed] + shifts(summed, "crow")
    scale = 1.0 / (samples * dp * crow)
    source, image = call(
        functools.partial(source_kernel, scale), [part, part], mine, *parts, low, block_inv
    )
    done = [image]
    places = [(0, 0)]
    side = []
    for step in range(1, crow):
        before = max(step - 2, 0)
        still = step > 1
        cols = swap(ccol, before, step - 1, True) if still else keep(ccol)
        got = [move(image, swap(crow, step - 1, at), cols) for at in range(step, crow)]
        if step == 1:
            source = move(source, keep(crow), [(c - 1) % ccol for c in range(ccol)])
        if side:
            side = [move(side[0], keep(crow), swap(ccol, before, step - 1))]
        out = call(
            functools.partial(fore_kernel, step, len(got), len(side)), [part, part],
            *got, *side, source, high_f, low_f, near, block_inv,
        )
        side, image = [out[0]], out[1]
        done.append(image)
        places.append((step, step - 1))
    own = call(functools.partial(pick_kernel, places), part, *done)
    own = call(sum_kernel, part, own, *shifts(own, "ccol"))
    full = shaped(rows, total)
    return tuple(
        call(
            final_kernel, [full, full, full], iterate, residual, direction, own, *shifts(own, "crow"),
            scratch_shapes=[pltpu.VMEM((rows, total), jnp.float32)],
        )
    )


def solution(mesh):
    placed = (
        P(None, ("dp", "crow")),
        P(None, "ccol"),
        P(),
        P("crow", "ccol"),
        P("crow", None, None),
        P(),
        P(),
        P(),
    )
    return jax.shard_map(
        per_device, mesh=mesh, in_specs=placed, out_specs=(P(), P(), P()), check_vma=False
    )
```

```python
import functools
import math

import jax
import jax.numpy as jnp
from jax import lax
from jax.experimental import pallas as pl
from jax.experimental.pallas import tpu as pltpu
from jax.sharding import PartitionSpec as P

ridge_weight = 0.2
LOG2E = 1.0 / math.log(2.0)
NN = (((1,), (0,)), ((), ()))
NT = (((1,), (1,)), ((), ()))
TN = (((0,), (0,)), ((), ()))


def pair(value):
    high = value.astype(jnp.bfloat16)
    low = (value - high.astype(jnp.float32)).astype(jnp.bfloat16)
    return high, low


def stacked(value):
    high, low = pair(value)
    return jnp.concatenate([high, low], axis=0)


def fold(product, rows):
    return product[:rows] + product[rows:]


def times_pair(rows, high, low, dims):
    both = stacked(rows)
    out = lax.dot_general(both, high, dims, preferred_element_type=jnp.float32)
    out = out + lax.dot_general(both, low, dims, preferred_element_type=jnp.float32)
    return fold(out, rows.shape[0])


def times(rows, matrix, dims):
    high, low = pair(matrix)
    return times_pair(rows, high, low, dims)


def blocks_of(held):
    return [(r, c) for r in range(1, held) for c in range(r)]


def lower(low_ref, order, r, c):
    at = r * (r - 1) // 2 + c
    return low_ref[:, at * order : (at + 1) * order]


def square(one, other):
    first, first_low = pair(one)
    second, second_low = pair(other)
    out = lax.dot_general(first, second, NN, preferred_element_type=jnp.float32)
    out = out + lax.dot_general(first, second_low, NN, preferred_element_type=jnp.float32)
    return out + lax.dot_general(first_low, second, NN, preferred_element_type=jnp.float32)


def cut(ref, at, width):
    return ref[:, pl.ds(pl.multiple_of(at * width, width), width)]


def back_apply(target, low_ref, inv_ref):
    held, order = inv_ref.shape[0], inv_ref.shape[1]
    parts = [target[:, n * order : (n + 1) * order] for n in range(held)]
    pieces = []
    for c in range(held):
        piece = times(parts[c], inv_ref[c], NN)
        for r in range(c + 1, held):
            piece = piece + times(parts[r], lower(low_ref, order, r, c), NN)
        pieces.append(piece)
    return jnp.concatenate(pieces, axis=1)


def fore_apply(source, high_ref, low_ref, order):
    pieces = []
    for end in range(order, source.shape[1] + 1, order):
        block = (slice(0, end), slice(end - order, end))
        pieces.append(times_pair(source[:, :end], high_ref[block], low_ref[block], NN))
    return jnp.concatenate(pieces, axis=1)


def store_turned(low, inv_ref, high_out, low_out):
    held, order = inv_ref.shape[0], inv_ref.shape[1]
    for r in range(held):
        for c in range(r + 1):
            at = r * (r - 1) // 2 + c
            block = inv_ref[r] if r == c else low[:, at * order : (at + 1) * order]
            place = (slice(c * order, (c + 1) * order), slice(r * order, (r + 1) * order))
            high_out[place], low_out[place] = pair(block.T)


def turn_kernel(low_ref, inv_ref, high_out, low_out):
    store_turned(low_ref[...], inv_ref, high_out, low_out)


def turn_factor_kernel(factor_ref, high_out, low_out):
    high_out[...], low_out[...] = pair(factor_ref[...].T)


def first_kernel(direction_ref, inv_ref, *refs):
    tri_refs, out_ref = refs[:-1], refs[-1]
    held, order = inv_ref.shape[0], inv_ref.shape[1]
    width = held * order
    tri = dict(zip(blocks_of(held), tri_refs))
    target = cut(direction_ref, lax.axis_index("crow"), width)
    pieces = [None] * held
    for number in reversed(range(held)):
        part = target[:, number * order : (number + 1) * order]
        for later in range(number + 1, held):
            part = part - times(pieces[later], tri[later, number][...], NN)
        pieces[number] = times(part, inv_ref[number], NN)
    out_ref[...] = jnp.concatenate(pieces, axis=1)


def lower_kernel(after_ref, inv_ref, *refs):
    tri_refs, out_ref = refs[:-1], refs[-1]
    held, order = inv_ref.shape[0], inv_ref.shape[1]
    tri = dict(zip(blocks_of(held), tri_refs))
    found = {(n, n): inv_ref[n] for n in range(held)}
    for r in range(1, held):
        for c in range(r):
            total = square(tri[r, c][...], found[c, c])
            for between in range(c + 1, r):
                total = total + square(tri[r, between][...], found[between, c])
            found[r, c] = -square(inv_ref[r], total)
            at = r * (r - 1) // 2 + c
            out_ref[:, at * order : (at + 1) * order] = found[r, c]


def pair_kernel(factor_ref, high_ref, low_ref):
    high, low = pair(factor_ref[...])
    high_ref[...] = high
    low_ref[...] = low


def spread_kernel(cols, lend, *refs):
    outs = refs[len(refs) - 1 - lend :]
    refs = refs[: len(refs) - 1 - lend]
    if lend:
        low_of, half = refs[-1], outs[1]
        tall = half.shape[0]
        at = lax.rem(lax.axis_index("dp"), 2) * tall
        half[...] = low_of[pl.ds(pl.multiple_of(at, tall), tall), :]
        refs = refs[:-1]
    extra = refs[: len(refs) - 2 - len(cols)]
    got_refs = refs[len(extra) : len(extra) + len(cols)]
    high_ref, low_ref = refs[-2:]
    col = lax.axis_index("ccol")
    piece = got_refs[0][...]
    for at, got in zip(cols[1:], got_refs[1:]):
        piece = jnp.where(col == at, got[...], piece)
    out = times_pair(piece, high_ref[...], low_ref[...], NN)
    for ref in extra:
        out = out + ref[...]
    outs[0][...] = out


def merge_kernel(mine_ref, other_ref, inv_ref, high_out, low_out):
    odd = lax.rem(lax.axis_index("dp"), 2) == 1
    mine, other = mine_ref[...], other_ref[...]
    low = jnp.concatenate([jnp.where(odd, other, mine), jnp.where(odd, mine, other)], axis=0)
    store_turned(low, inv_ref, high_out, low_out)


def solve_kernel(direction_ref, sub_ref, low_ref, inv_ref, out_ref):
    width = sub_ref.shape[1]
    target = cut(direction_ref, lax.axis_index("crow"), width) - sub_ref[...]
    out_ref[...] = back_apply(target, low_ref, inv_ref)


def pick_kernel(places, *refs):
    row, col = lax.axis_index("crow"), lax.axis_index("ccol")
    out = jnp.zeros_like(refs[0][...])
    for (r, c), ref in zip(places, refs[:-1]):
        out = jnp.where((row == r) & (col == c), ref[...], out)
    refs[-1][...] = out


def solve_pick_kernel(places, direction_ref, sub_ref, low_ref, inv_ref, *refs):
    width = sub_ref.shape[1]
    row, col = lax.axis_index("crow"), lax.axis_index("ccol")
    target = cut(direction_ref, row, width) - sub_ref[...]
    out = jnp.where((row == 0) & (col == 0), back_apply(target, low_ref, inv_ref), 0.0)
    for (r, c), ref in zip(places, refs[:-1]):
        out = jnp.where((row == r) & (col == c), ref[...], out)
    refs[-1][...] = out


def triple(value):
    high, middle = pair(value)
    rest = value - high.astype(jnp.float32) - middle.astype(jnp.float32)
    return high, middle, rest.astype(jnp.bfloat16)


def norm_rows(norm, inputs):
    row = lax.broadcasted_iota(jnp.int32, (inputs, norm.shape[1]), 0)
    wide = jnp.broadcast_to(norm, (inputs, norm.shape[1]))
    high, middle, low = (part.astype(jnp.float32) for part in triple(wide))
    rows = jnp.where(row == 0, high, jnp.where(row == 1, middle, jnp.where(row == 2, low, 0.0)))
    return rows.astype(jnp.bfloat16)


def ones_rows(norm, inputs):
    row = lax.broadcasted_iota(jnp.int32, (inputs, norm.shape[1]), 0)
    return jnp.where(row < 3, 1.0, 0.0).astype(jnp.bfloat16)


def scale_by(value, scales_ref):
    inputs = value.shape[0]
    row = lax.broadcasted_iota(jnp.int32, value.shape, 0)
    scales = jnp.full(value.shape, scales_ref[0], jnp.float32)
    for n in range(1, inputs):
        scales = jnp.where(row == n, scales_ref[n], scales)
    return value / scales


def tile_kernel(scales_ref, centres_ref, data_ref, high_ref, low_ref, right):
    inputs = data_ref.shape[0]

    @pl.when(pl.program_id(0) == 0)
    def _():
        scaled = scale_by(data_ref[...], scales_ref)
        norm = jnp.sum(scaled * scaled, axis=0, keepdims=True) * (-0.5 * LOG2E)
        high, middle, low = triple(scaled)
        right[...] = jnp.concatenate(
            [high, middle, high, middle, low, high, norm_rows(norm, inputs), ones_rows(norm, inputs)],
            axis=0,
        )

    scaled = scale_by(centres_ref[...], scales_ref)
    norm = jnp.sum(scaled * scaled, axis=0, keepdims=True) * (-0.5 * LOG2E)
    high, middle, low = triple(scaled * LOG2E)
    left = jnp.concatenate(
        [high, high, middle, middle, high, low, ones_rows(norm, inputs), norm_rows(norm, inputs)], axis=0
    )
    exponent = lax.dot_general(left, right[...], TN, preferred_element_type=jnp.float32)
    high, low = pair(jnp.exp2(exponent))
    high_ref[...] = high
    low_ref[...] = low


def image_kernel(*refs):
    part_refs = refs[:-6]
    high_ref, low_ref, half_ref, mine_ref, out_ref, half_out = refs[-6:]

    half_out[...] = half_ref[...]
    piece = part_refs[0][...]
    for ref in part_refs[1:]:
        piece = piece + ref[...]
    mine_ref[...] = piece
    out_ref[...] = times_pair(piece, high_ref[...], low_ref[...], NN)


def normal_kernel(*refs):
    part_refs = refs[:-3]
    high_ref, low_ref, out_ref = refs[-3:]
    piece = part_refs[0][...]
    for ref in part_refs[1:]:
        piece = piece + ref[...]
    out_ref[...] = times_pair(piece, high_ref[...], low_ref[...], NT)


def source_kernel(scale, order, mine_ref, *refs):
    part_refs = refs[:-4]
    high_ref, low_ref, out_ref, image_ref = refs[-4:]
    total = part_refs[0][...]
    for ref in part_refs[1:]:
        total = total + ref[...]
    normal = total * scale + ridge_weight * mine_ref[...]
    out_ref[...] = normal
    image_ref[...] = fore_apply(normal, high_ref, low_ref, order)


def fore_kernel(step, order, count, sides, *refs):
    got_refs = refs[:count]
    side_refs = refs[count : count + sides]
    source_ref, fh_ref, fl_ref, high_ref, low_ref, side_out, image_out = refs[count + sides :]
    row = lax.axis_index("crow")
    piece = got_refs[0][...]
    for at in range(1, count):
        piece = jnp.where(row == step + at, got_refs[at][...], piece)
    side = times_pair(piece, fh_ref[...], fl_ref[...], NN)
    for ref in side_refs:
        side = side + ref[...]
    side_out[...] = side
    image_out[...] = fore_apply(source_ref[...] - side, high_ref, low_ref, order)


def sum_kernel(*refs):
    total = refs[0][...]
    for ref in refs[1:-1]:
        total = total + ref[...]
    refs[-1][...] = total


def final_kernel(iterate_ref, residual_ref, direction_ref, *refs):
    part_refs = refs[:-4]
    iterate_out, residual_out, direction_out, image_ref = refs[-4:]
    size = len(part_refs)
    width = part_refs[0].shape[1]
    row = lax.axis_index("crow")
    for step, ref in enumerate(part_refs):
        at = row ^ step
        image_ref[:, pl.ds(pl.multiple_of(at * width, width), width)] = ref[...]
    residual = residual_ref[...]
    direction = direction_ref[...]
    image = image_ref[...]
    gamma = jnp.sum(residual * residual, axis=1, keepdims=True)
    curvature = jnp.sum(direction * image, axis=1, keepdims=True)
    alpha = gamma / curvature
    iterate_out[...] = iterate_ref[...] + alpha * direction
    new_residual = residual - alpha * image
    residual_out[...] = new_residual
    gamma_next = jnp.sum(new_residual * new_residual, axis=1, keepdims=True)
    direction_out[...] = new_residual + (gamma_next / gamma) * direction


def shaped(*shape):
    return jax.ShapeDtypeStruct(shape, jnp.float32)


def call(kernel, outs, *args, limit=12, cost=(10**6, 10**6), **options):
    return pl.pallas_call(
        kernel,
        out_shape=outs,
        compiler_params=pltpu.CompilerParams(vmem_limit_bytes=limit << 20),
        cost_estimate=pl.CostEstimate(flops=cost[0], bytes_accessed=cost[1], transcendentals=0),
        **options,
    )(*args)


def swap(size, one, other, still=False):
    to = list(range(size))
    to[one], to[other] = other, one
    if not still:
        rest = [n for n in range(size) if n not in (one, other)]
        for a, b in zip(rest[::2], rest[1::2]):
            to[a], to[b] = b, a
    return to


def keep(size):
    return list(range(size))


def per_device(data, centres, scales, factor, block_inv, iterate, residual, direction):
    dp, crow, ccol = lax.axis_size("dp"), lax.axis_size("crow"), lax.axis_size("ccol")
    held, order = block_inv.shape[0], block_inv.shape[1]
    width = factor.shape[0]
    rows, total = direction.shape
    assert factor.shape[1] == width and crow == ccol and crow in (4, 8) and dp % 2 == 0
    part = shaped(rows, width)
    last = crow - 1

    def spot(d, r, c):
        return (d * crow + r) * ccol + c

    def move(value, row_to, col_to, flip=1):
        perm = [
            (spot(d, r, c), spot(d ^ flip, row_to[r], col_to[c]))
            for d in range(dp)
            for r in range(crow)
            for c in range(ccol)
        ]
        return lax.ppermute(value, ("dp", "crow", "ccol"), perm)

    def shifts(value, axis, flip=1):
        out = []
        for step in range(1, lax.axis_size(axis)):
            other = [n ^ step for n in range(lax.axis_size(axis))]
            if axis == "crow":
                out.append(move(value, other, keep(ccol), flip))
            else:
                out.append(move(value, keep(crow), other, flip))
        return out

    def with_tri(kernel, outs, *args, limit=12):
        full = [pl.BlockSpec(a.shape, lambda i, n=a.ndim: (0,) * n) for a in args]
        tri = [pl.BlockSpec((order, order), lambda i, r=r, c=c: (r, c)) for r, c in blocks_of(held)]
        shape = outs.shape
        return call(
            kernel, outs, *args, *([factor] * len(tri)), grid=(1,), in_specs=full + tri,
            out_specs=pl.BlockSpec(shape, lambda i: (0, 0)), limit=limit,
        )

    piece = with_tri(first_kernel, part, direction, block_inv, limit=58)
    found = {last: piece}
    low = with_tri(lower_kernel, shaped(order, len(blocks_of(held)) * order), piece, block_inv)
    wide = jax.ShapeDtypeStruct((width, width), jnp.bfloat16)
    high_f, low_f = call(pair_kernel, [wide, wide], factor)
    turned_f = call(turn_factor_kernel, [wide, wide], factor)
    turned = call(turn_kernel, [wide, wide], low, block_inv)

    samples = data.shape[1]
    tile = order
    inputs = data.shape[0]
    kernel_shape = jax.ShapeDtypeStruct((width, samples), jnp.bfloat16)
    high_k, low_k = call(
        tile_kernel, [kernel_shape] * 2, scales, centres, data,
        grid=(width // tile,),
        in_specs=[
            pl.BlockSpec(memory_space=pltpu.SMEM),
            pl.BlockSpec((inputs, tile), lambda i: (0, i)),
            pl.BlockSpec((inputs, samples), lambda i: (0, 0)),
        ],
        out_specs=[pl.BlockSpec((tile, samples), lambda i: (i, 0))] * 2,
        scratch_shapes=[pltpu.VMEM((8 * inputs, samples), jnp.bfloat16)],
        limit=20,
    )

    sums = []
    for step in range(last, 0, -1):
        cols = list(range(step))[::-1]
        got = [move(piece, keep(crow), swap(ccol, step, c)) for c in cols]
        outs = [part, shaped(order // 2, low.shape[1])] if step == 1 else [part]
        lend = [low] if step == 1 else []
        sums, *halves = call(
            functools.partial(spread_kernel, cols, len(outs) - 1), outs, *sums, *got, high_f, low_f, *lend
        )
        sums = [move(sums, swap(crow, step, step - 1), keep(ccol))]
        if step > 1:
            piece = call(solve_kernel, part, direction, *sums, low, block_inv)
            found[step - 1] = piece
    pairs = [((n, n), (n, n - 1)) for n in range(1, crow)]
    perm = [
        (spot(d, *one), spot(d, *other))
        for d in range(dp)
        for a, b in pairs
        for one, other in ((a, b), (b, a))
    ]
    half = lax.ppermute(halves[0], ("dp", "crow", "ccol"), perm)
    places = [(n, n) for n in range(1, crow)]
    own = call(
        functools.partial(solve_pick_kernel, places), part, direction, *sums, low, block_inv,
        *[found[n] for n in range(1, crow)],
    )

    parts = [own] + shifts(own, "crow")
    mine, images, half = call(
        image_kernel, [part, shaped(rows, samples), shaped(*half.shape)], *parts, high_k, low_k, half,
        limit=16,
    )
    images = [images] + shifts(images, "ccol", 0)
    near = call(merge_kernel, [wide, wide], half, move(half, keep(crow), keep(ccol)), block_inv)
    summed = call(normal_kernel, part, *images, high_k, low_k, limit=16)
    if dp == 2:
        summed = summed + lax.ppermute(summed, "dp", [(0, 1), (1, 0)])
    else:
        summed = lax.psum(summed, "dp")
    parts = [summed] + shifts(summed, "crow")
    scale = 1.0 / (samples * dp * crow)
    source, image = call(
        functools.partial(source_kernel, scale, order), [part, part], mine, *parts, *turned
    )
    done = [image]
    places = [(0, 0)]
    side = []
    for step in range(1, crow):
        before = max(step - 2, 0)
        still = step > 1
        cols = swap(ccol, before, step - 1, True) if still else keep(ccol)
        got = [move(image, swap(crow, step - 1, at), cols) for at in range(step, crow)]
        if step == 1:
            source = move(source, keep(crow), [(c - 1) % ccol for c in range(ccol)])
        if side:
            side = [move(side[0], keep(crow), swap(ccol, before, step - 1))]
        out = call(
            functools.partial(fore_kernel, step, order, len(got), len(side)), [part, part],
            *got, *side, source, *turned_f, *near,
        )
        side, image = [out[0]], out[1]
        done.append(image)
        places.append((step, step - 1))
    own = call(functools.partial(pick_kernel, places), part, *done)
    own = call(sum_kernel, part, own, *shifts(own, "ccol"))
    full = shaped(rows, total)
    return tuple(
        call(
            final_kernel, [full, full, full], iterate, residual, direction, own, *shifts(own, "crow"),
            scratch_shapes=[pltpu.VMEM((rows, total), jnp.float32)],
        )
    )


def solution(mesh):
    placed = (
        P(None, ("dp", "crow")),
        P(None, "ccol"),
        P(),
        P("crow", "ccol"),
        P("crow", None, None),
        P(),
        P(),
        P(),
    )
    return jax.shard_map(
        per_device, mesh=mesh, in_specs=placed, out_specs=(P(), P(), P()), check_vma=False
    )
```

```python
import functools
import math

import jax
import jax.numpy as jnp
from jax import lax
from jax.experimental import pallas as pl
from jax.experimental.pallas import tpu as pltpu
from jax.sharding import PartitionSpec as P


ridge_weight = 0.2
LOG2E = 1.0 / math.log(2.0)
NN = (((1,), (0,)), ((), ()))
NT = (((1,), (1,)), ((), ()))
TN = (((0,), (0,)), ((), ()))


def pair(value):
    high = value.astype(jnp.bfloat16)
    low = (value - high.astype(jnp.float32)).astype(jnp.bfloat16)
    return high, low


def stacked(value):
    high, low = pair(value)
    return jnp.concatenate([high, low], axis=0)


def fold(product, rows):
    return product[:rows] + product[rows:]


def times_pair(rows, high, low, dims):
    both = stacked(rows)
    out = lax.dot_general(both, high, dims, preferred_element_type=jnp.float32)
    out = out + lax.dot_general(both, low, dims, preferred_element_type=jnp.float32)
    return fold(out, rows.shape[0])


def times(rows, matrix, dims):
    high, low = pair(matrix)
    return times_pair(rows, high, low, dims)


def blocks_of(held):
    return [(r, c) for r in range(1, held) for c in range(r)]


def lower(low_ref, order, r, c):
    at = r * (r - 1) // 2 + c
    return low_ref[:, at * order : (at + 1) * order]


def square(one, other):
    first, first_low = pair(one)
    second, second_low = pair(other)
    out = lax.dot_general(first, second, NN, preferred_element_type=jnp.float32)
    out = out + lax.dot_general(first, second_low, NN, preferred_element_type=jnp.float32)
    return out + lax.dot_general(first_low, second, NN, preferred_element_type=jnp.float32)


def cut(ref, at, width):
    return ref[:, pl.ds(pl.multiple_of(at * width, width), width)]


def back_apply(target, low_ref, inv_ref):
    held, order = inv_ref.shape[0], inv_ref.shape[1]
    parts = [target[:, n * order : (n + 1) * order] for n in range(held)]
    pieces = []
    for c in range(held):
        piece = times(parts[c], inv_ref[c], NN)
        for r in range(c + 1, held):
            piece = piece + times(parts[r], lower(low_ref, order, r, c), NN)
        pieces.append(piece)
    return jnp.concatenate(pieces, axis=1)


def fore_apply(source, high_ref, low_ref, order):
    pieces = []
    for end in range(order, source.shape[1] + 1, order):
        block = (slice(0, end), slice(end - order, end))
        pieces.append(times_pair(source[:, :end], high_ref[block], low_ref[block], NN))
    return jnp.concatenate(pieces, axis=1)


def store_turned(low, inv_ref, high_out, low_out):
    held, order = inv_ref.shape[0], inv_ref.shape[1]
    for r in range(held):
        for c in range(r + 1):
            at = r * (r - 1) // 2 + c
            block = inv_ref[r] if r == c else low[:, at * order : (at + 1) * order]
            place = (slice(c * order, (c + 1) * order), slice(r * order, (r + 1) * order))
            high_out[place], low_out[place] = pair(block.T)


def turn_kernel(low_ref, inv_ref, high_out, low_out):
    store_turned(low_ref[...], inv_ref, high_out, low_out)


def turn_factor_kernel(factor_ref, high_out, low_out):
    high_out[...], low_out[...] = pair(factor_ref[...].T)


def first_kernel(direction_ref, inv_ref, *refs):
    tri_refs, out_ref = refs[:-1], refs[-1]
    held, order = inv_ref.shape[0], inv_ref.shape[1]
    width = held * order
    tri = dict(zip(blocks_of(held), tri_refs))
    target = cut(direction_ref, lax.axis_index("crow"), width)
    pieces = [None] * held
    for number in reversed(range(held)):
        part = target[:, number * order : (number + 1) * order]
        for later in range(number + 1, held):
            part = part - times(pieces[later], tri[later, number][...], NN)
        pieces[number] = times(part, inv_ref[number], NN)
    out_ref[...] = jnp.concatenate(pieces, axis=1)


def lower_kernel(after_ref, inv_ref, *refs):
    tri_refs, out_ref = refs[:-1], refs[-1]
    held, order = inv_ref.shape[0], inv_ref.shape[1]
    tri = dict(zip(blocks_of(held), tri_refs))
    found = {(n, n): inv_ref[n] for n in range(held)}
    for r in range(1, held):
        for c in range(r):
            total = square(tri[r, c][...], found[c, c])
            for between in range(c + 1, r):
                total = total + square(tri[r, between][...], found[between, c])
            found[r, c] = -square(inv_ref[r], total)
            at = r * (r - 1) // 2 + c
            out_ref[:, at * order : (at + 1) * order] = found[r, c]


def pair_kernel(factor_ref, high_ref, low_ref):
    high, low = pair(factor_ref[...])
    high_ref[...] = high
    low_ref[...] = low


def spread_kernel(cols, lend, *refs):
    outs = refs[len(refs) - 1 - lend :]
    refs = refs[: len(refs) - 1 - lend]
    if lend:
        low_of, half = refs[-1], outs[1]
        tall = half.shape[0]
        at = lax.rem(lax.axis_index("dp"), 2) * tall
        half[...] = low_of[pl.ds(pl.multiple_of(at, tall), tall), :]
        refs = refs[:-1]
    extra = refs[: len(refs) - 2 - len(cols)]
    got_refs = refs[len(extra) : len(extra) + len(cols)]
    high_ref, low_ref = refs[-2:]
    col = lax.axis_index("ccol")
    piece = got_refs[0][...]
    for at, got in zip(cols[1:], got_refs[1:]):
        piece = jnp.where(col == at, got[...], piece)
    out = times_pair(piece, high_ref[...], low_ref[...], NN)
    for ref in extra:
        out = out + ref[...]
    outs[0][...] = out


def merge_kernel(mine_ref, other_ref, inv_ref, high_out, low_out):
    odd = lax.rem(lax.axis_index("dp"), 2) == 1
    mine, other = mine_ref[...], other_ref[...]
    low = jnp.concatenate([jnp.where(odd, other, mine), jnp.where(odd, mine, other)], axis=0)
    store_turned(low, inv_ref, high_out, low_out)


def solve_kernel(direction_ref, sub_ref, low_ref, inv_ref, out_ref):
    width = sub_ref.shape[1]
    target = cut(direction_ref, lax.axis_index("crow"), width) - sub_ref[...]
    out_ref[...] = back_apply(target, low_ref, inv_ref)


def pick_kernel(places, *refs):
    row, col = lax.axis_index("crow"), lax.axis_index("ccol")
    out = jnp.zeros_like(refs[0][...])
    for (r, c), ref in zip(places, refs[:-1]):
        out = jnp.where((row == r) & (col == c), ref[...], out)
    refs[-1][...] = out


def solve_pick_kernel(places, direction_ref, sub_ref, low_ref, inv_ref, *refs):
    width = sub_ref.shape[1]
    row, col = lax.axis_index("crow"), lax.axis_index("ccol")
    target = cut(direction_ref, row, width) - sub_ref[...]
    out = jnp.where((row == 0) & (col == 0), back_apply(target, low_ref, inv_ref), 0.0)
    for (r, c), ref in zip(places, refs[:-1]):
        out = jnp.where((row == r) & (col == c), ref[...], out)
    refs[-1][...] = out


def triple(value):
    high, middle = pair(value)
    rest = value - high.astype(jnp.float32) - middle.astype(jnp.float32)
    return high, middle, rest.astype(jnp.bfloat16)


def norm_rows(norm, inputs):
    row = lax.broadcasted_iota(jnp.int32, (inputs, norm.shape[1]), 0)
    wide = jnp.broadcast_to(norm, (inputs, norm.shape[1]))
    high, middle, low = (part.astype(jnp.float32) for part in triple(wide))
    rows = jnp.where(row == 0, high, jnp.where(row == 1, middle, jnp.where(row == 2, low, 0.0)))
    return rows.astype(jnp.bfloat16)


def ones_rows(norm, inputs):
    row = lax.broadcasted_iota(jnp.int32, (inputs, norm.shape[1]), 0)
    return jnp.where(row < 3, 1.0, 0.0).astype(jnp.bfloat16)


def scale_by(value, scales_ref):
    inputs = value.shape[0]
    row = lax.broadcasted_iota(jnp.int32, value.shape, 0)
    scales = jnp.full(value.shape, scales_ref[0], jnp.float32)
    for n in range(1, inputs):
        scales = jnp.where(row == n, scales_ref[n], scales)
    return value / scales


def tile_kernel(scales_ref, centres_ref, data_ref, high_ref, low_ref, right):
    inputs = data_ref.shape[0]

    @pl.when(pl.program_id(0) == 0)
    def _():
        scaled = scale_by(data_ref[...], scales_ref)
        norm = jnp.sum(scaled * scaled, axis=0, keepdims=True) * (-0.5 * LOG2E)
        high, middle, low = triple(scaled)
        right[...] = jnp.concatenate(
            [high, middle, high, middle, low, high, norm_rows(norm, inputs), ones_rows(norm, inputs)],
            axis=0,
        )

    scaled = scale_by(centres_ref[...], scales_ref)
    norm = jnp.sum(scaled * scaled, axis=0, keepdims=True) * (-0.5 * LOG2E)
    high, middle, low = triple(scaled * LOG2E)
    left = jnp.concatenate(
        [high, high, middle, middle, high, low, ones_rows(norm, inputs), norm_rows(norm, inputs)], axis=0
    )
    exponent = lax.dot_general(left, right[...], TN, preferred_element_type=jnp.float32)
    high, low = pair(jnp.exp2(exponent))
    high_ref[...] = high
    low_ref[...] = low


def image_kernel(*refs):
    part_refs = refs[:-6]
    high_ref, low_ref, half_ref, mine_ref, out_ref, half_out = refs[-6:]

    half_out[...] = half_ref[...]
    piece = part_refs[0][...]
    for ref in part_refs[1:]:
        piece = piece + ref[...]
    mine_ref[...] = piece
    out_ref[...] = times_pair(piece, high_ref[...], low_ref[...], NN)


def normal_kernel(*refs):
    part_refs = refs[:-3]
    high_ref, low_ref, out_ref = refs[-3:]
    piece = part_refs[0][...]
    for ref in part_refs[1:]:
        piece = piece + ref[...]
    both = stacked(piece)
    out = lax.dot_general(high_ref[...], both, NT, preferred_element_type=jnp.float32)
    out = out + lax.dot_general(low_ref[...], both, NT, preferred_element_type=jnp.float32)
    out_ref[...] = fold(out.T, piece.shape[0])


def source_kernel(scale, order, mine_ref, *refs):
    part_refs = refs[:-4]
    high_ref, low_ref, out_ref, image_ref = refs[-4:]
    total = part_refs[0][...]
    for ref in part_refs[1:]:
        total = total + ref[...]
    normal = total * scale + ridge_weight * mine_ref[...]
    out_ref[...] = normal
    image_ref[...] = fore_apply(normal, high_ref, low_ref, order)


def fore_kernel(order, sides, *refs):
    side_refs = refs[:sides]
    got_ref, source_ref, fh_ref, fl_ref, high_ref, low_ref, image_out = refs[sides:]
    left = source_ref[...] - times_pair(got_ref[...], fh_ref[...], fl_ref[...], NN)
    for ref in side_refs:
        left = left - ref[...]
    image_out[...] = fore_apply(left, high_ref, low_ref, order)


def side_kernel(rows, sides, *refs):
    side_refs = refs[:sides]
    got_refs = refs[sides : sides + len(rows)]
    fh_ref, fl_ref, side_out = refs[sides + len(rows) :]
    row = lax.axis_index("crow")
    piece = got_refs[0][...]
    for at, ref in zip(rows[1:], got_refs[1:]):
        piece = jnp.where(row == at, ref[...], piece)
    side = times_pair(piece, fh_ref[...], fl_ref[...], NN)
    for ref in side_refs:
        side = side + ref[...]
    side_out[...] = side


def sum_kernel(*refs):
    total = refs[0][...]
    for ref in refs[1:-1]:
        total = total + ref[...]
    refs[-1][...] = total


def final_kernel(iterate_ref, residual_ref, direction_ref, *refs):
    part_refs = refs[:-4]
    iterate_out, residual_out, direction_out, image_ref = refs[-4:]
    width = part_refs[0].shape[1]
    row = lax.axis_index("crow")
    for step, ref in enumerate(part_refs):
        at = row ^ step
        image_ref[:, pl.ds(pl.multiple_of(at * width, width), width)] = ref[...]
    residual = residual_ref[...]
    direction = direction_ref[...]
    image = image_ref[...]
    gamma = jnp.sum(residual * residual, axis=1, keepdims=True)
    curvature = jnp.sum(direction * image, axis=1, keepdims=True)
    alpha = gamma / curvature
    iterate_out[...] = iterate_ref[...] + alpha * direction
    new_residual = residual - alpha * image
    residual_out[...] = new_residual
    gamma_next = jnp.sum(new_residual * new_residual, axis=1, keepdims=True)
    direction_out[...] = new_residual + (gamma_next / gamma) * direction


def shaped(*shape):
    return jax.ShapeDtypeStruct(shape, jnp.float32)


def call(kernel, outs, *args, limit=12, cost=(10**6, 10**6), **options):
    return pl.pallas_call(
        kernel,
        out_shape=outs,
        compiler_params=pltpu.CompilerParams(vmem_limit_bytes=limit << 20),
        cost_estimate=pl.CostEstimate(flops=cost[0], bytes_accessed=cost[1], transcendentals=0),
        **options,
    )(*args)


def swap(size, one, other, still=False):
    to = list(range(size))
    to[one], to[other] = other, one
    if not still:
        rest = [n for n in range(size) if n not in (one, other)]
        for a, b in zip(rest[::2], rest[1::2]):
            to[a], to[b] = b, a
    return to


def keep(size):
    return list(range(size))


def step_of(data, centres, scales, factor, block_inv, iterate, residual, direction):
    dp, crow, ccol = lax.axis_size("dp"), lax.axis_size("crow"), lax.axis_size("ccol")
    held, order = block_inv.shape[0], block_inv.shape[1]
    width = factor.shape[0]
    rows, total = direction.shape
    assert factor.shape[1] == width and crow == ccol and crow in (4, 8) and dp % 2 == 0
    part = shaped(rows, width)
    last = crow - 1

    def spot(d, r, c):
        return (d * crow + r) * ccol + c

    def move(value, row_to, col_to, flip=1):
        perm = [
            (spot(d, r, c), spot(d ^ flip, row_to[r], col_to[c]))
            for d in range(dp)
            for r in range(crow)
            for c in range(ccol)
        ]
        return lax.ppermute(value, ("dp", "crow", "ccol"), perm)

    def shifts(value, axis, flip=1):
        out = []
        for step in range(1, lax.axis_size(axis)):
            other = [n ^ step for n in range(lax.axis_size(axis))]
            if axis == "crow":
                out.append(move(value, other, keep(ccol), flip))
            else:
                out.append(move(value, keep(crow), other, flip))
        return out

    def with_tri(kernel, outs, *args, limit=12):
        full = [pl.BlockSpec(a.shape, lambda i, n=a.ndim: (0,) * n) for a in args]
        tri = [pl.BlockSpec((order, order), lambda i, r=r, c=c: (r, c)) for r, c in blocks_of(held)]
        shape = outs.shape
        return call(
            kernel, outs, *args, *([factor] * len(tri)), grid=(1,), in_specs=full + tri,
            out_specs=pl.BlockSpec(shape, lambda i: (0, 0)), limit=limit,
        )

    piece = with_tri(first_kernel, part, direction, block_inv, limit=58)
    found = {last: piece}
    low = with_tri(lower_kernel, shaped(order, len(blocks_of(held)) * order), piece, block_inv)
    wide = jax.ShapeDtypeStruct((width, width), jnp.bfloat16)
    high_f, low_f = call(pair_kernel, [wide, wide], factor)
    turned_f = call(turn_factor_kernel, [wide, wide], factor)
    turned = call(turn_kernel, [wide, wide], low, block_inv)

    samples = data.shape[1]
    tile = order
    inputs = data.shape[0]
    kernel_shape = jax.ShapeDtypeStruct((width, samples), jnp.bfloat16)
    high_k, low_k = call(
        tile_kernel, [kernel_shape] * 2, scales, centres, data,
        grid=(width // tile,),
        in_specs=[
            pl.BlockSpec(memory_space=pltpu.SMEM),
            pl.BlockSpec((inputs, tile), lambda i: (0, i)),
            pl.BlockSpec((inputs, samples), lambda i: (0, 0)),
        ],
        out_specs=[pl.BlockSpec((tile, samples), lambda i: (i, 0))] * 2,
        scratch_shapes=[pltpu.VMEM((8 * inputs, samples), jnp.bfloat16)],
        limit=20,
    )

    def spread(cols, extra, got, lend=()):
        outs = [part, shaped(order // 2, low.shape[1])] if lend else [part]
        return call(
            functools.partial(spread_kernel, cols, len(lend)), outs, *extra, *got, high_f, low_f, *lend
        )

    sums = []
    for step in range(last, 0, -1):
        cols = list(range(step))[::-1]
        got = [move(piece, keep(crow), swap(ccol, step, c)) for c in cols]
        down = (swap(crow, step, step - 1), keep(ccol))
        if step == last:
            sub = move(spread(cols[:1], [], got[:1])[0], *down)
            sums = [move(spread(cols[1:], [], got[1:])[0], *down)]
        else:
            out, *halves = spread(cols, sums, got, [low] if step == 1 else [])
            sub = move(out, *down)
            sums = [sub]
        if step > 1:
            piece = call(solve_kernel, part, direction, sub, low, block_inv)
            found[step - 1] = piece
    pairs = [((n, n), (n, n - 1)) for n in range(1, crow)]
    perm = [
        (spot(d, *one), spot(d, *other))
        for d in range(dp)
        for a, b in pairs
        for one, other in ((a, b), (b, a))
    ]
    half = lax.ppermute(halves[0], ("dp", "crow", "ccol"), perm)
    places = [(n, n) for n in range(1, crow)]
    own = call(
        functools.partial(solve_pick_kernel, places), part, direction, sub, low, block_inv,
        *[found[n] for n in range(1, crow)],
    )

    parts = [own] + shifts(own, "crow")
    mine, images, half = call(
        image_kernel, [part, shaped(rows, samples), shaped(*half.shape)], *parts, high_k, low_k, half,
        limit=16,
    )
    images = [images] + shifts(images, "ccol", 0)
    near = call(merge_kernel, [wide, wide], half, move(half, keep(crow), keep(ccol)), block_inv)
    summed = call(normal_kernel, part, *images, high_k, low_k, limit=16)
    if dp == 2:
        summed = summed + lax.ppermute(summed, "dp", [(0, 1), (1, 0)])
    else:
        summed = lax.psum(summed, "dp")
    parts = [summed] + shifts(summed, "crow")
    scale = 1.0 / (samples * dp * crow)
    source, image = call(
        functools.partial(source_kernel, scale, order), [part, part], mine, *parts, *turned
    )
    done = [image]
    places = [(0, 0)]
    side = []
    for step in range(1, crow):
        before = max(step - 2, 0)
        cols = swap(ccol, before, step - 1, True) if step > 1 else keep(ccol)
        later = list(range(step + 1, crow))
        first = move(image, swap(crow, step - 1, step), cols)
        if step == 1:
            source = move(source, keep(crow), [(c - 1) % ccol for c in range(ccol)])
        if side:
            side = [move(side[0], keep(crow), swap(ccol, before, step - 1))]
        others = [move(image, swap(crow, step - 1, at), cols) for at in later]
        image = call(
            functools.partial(fore_kernel, order, len(side)), part,
            *side, first, source, *turned_f, *near,
        )
        if later:
            side = [
                call(
                    functools.partial(side_kernel, later, len(side)), part, *side, *others, *turned_f
                )
            ]
        done.append(image)
        places.append((step, step - 1))
    own = call(functools.partial(pick_kernel, places), part, *done)
    own = call(sum_kernel, part, own, *shifts(own, "ccol"))
    full = shaped(rows, total)
    return tuple(
        call(
            final_kernel, [full, full, full], iterate, residual, direction, own, *shifts(own, "crow"),
            scratch_shapes=[pltpu.VMEM((rows, total), jnp.float32)],
        )
    )


def solution(mesh):
    placed = (
        P(None, ("dp", "crow")),
        P(None, "ccol"),
        P(),
        P("crow", "ccol"),
        P("crow", None, None),
        P(),
        P(),
        P(),
    )
    return jax.shard_map(
        step_of, mesh=mesh, in_specs=placed, out_specs=(P(), P(), P()), check_vma=False
    )
```

```python
import functools
import math

import jax
import jax.numpy as jnp
from jax import lax
from jax.experimental import pallas as pl
from jax.experimental.pallas import tpu as pltpu
from jax.sharding import PartitionSpec as P


ridge_weight = 0.2
LOG2E = 1.0 / math.log(2.0)
NN = (((1,), (0,)), ((), ()))
NT = (((1,), (1,)), ((), ()))
TN = (((0,), (0,)), ((), ()))


def pair(value):
    high = value.astype(jnp.bfloat16)
    low = (value - high.astype(jnp.float32)).astype(jnp.bfloat16)
    return high, low


def stacked(value):
    high, low = pair(value)
    return jnp.concatenate([high, low], axis=0)


def fold(product, rows):
    return product[:rows] + product[rows:]


def times_pair(rows, high, low, dims):
    both = stacked(rows)
    out = lax.dot_general(both, high, dims, preferred_element_type=jnp.float32)
    out = out + lax.dot_general(both, low, dims, preferred_element_type=jnp.float32)
    return fold(out, rows.shape[0])


def times(rows, matrix, dims):
    high, low = pair(matrix)
    return times_pair(rows, high, low, dims)


def blocks_of(held):
    return [(r, c) for r in range(1, held) for c in range(r)]


def lower(low_ref, order, r, c):
    at = r * (r - 1) // 2 + c
    return low_ref[:, at * order : (at + 1) * order]


def square(one, other):
    first, first_low = pair(one)
    second, second_low = pair(other)
    out = lax.dot_general(first, second, NN, preferred_element_type=jnp.float32)
    out = out + lax.dot_general(first, second_low, NN, preferred_element_type=jnp.float32)
    return out + lax.dot_general(first_low, second, NN, preferred_element_type=jnp.float32)


def cut(ref, at, width):
    return ref[:, pl.ds(pl.multiple_of(at * width, width), width)]


def back_apply(target, low_ref, inv_ref):
    held, order = inv_ref.shape[0], inv_ref.shape[1]
    parts = [target[:, n * order : (n + 1) * order] for n in range(held)]
    pieces = []
    for c in range(held):
        piece = times(parts[c], inv_ref[c], NN)
        for r in range(c + 1, held):
            piece = piece + times(parts[r], lower(low_ref, order, r, c), NN)
        pieces.append(piece)
    return jnp.concatenate(pieces, axis=1)


def fore_apply(source, high_ref, low_ref, order):
    pieces = []
    for end in range(order, source.shape[1] + 1, order):
        block = (slice(0, end), slice(end - order, end))
        pieces.append(times_pair(source[:, :end], high_ref[block], low_ref[block], NN))
    return jnp.concatenate(pieces, axis=1)


def store_turned(low, inv_ref, high_out, low_out):
    held, order = inv_ref.shape[0], inv_ref.shape[1]
    for r in range(held):
        for c in range(r + 1):
            at = r * (r - 1) // 2 + c
            block = inv_ref[r] if r == c else low[:, at * order : (at + 1) * order]
            place = (slice(c * order, (c + 1) * order), slice(r * order, (r + 1) * order))
            high_out[place], low_out[place] = pair(block.T)


def turn_kernel(low_ref, inv_ref, high_out, low_out):
    store_turned(low_ref[...], inv_ref, high_out, low_out)


def turn_factor_kernel(factor_ref, high_out, low_out):
    high_out[...], low_out[...] = pair(factor_ref[...].T)


def first_kernel(direction_ref, inv_ref, *refs):
    tri_refs, out_ref = refs[:-1], refs[-1]
    held, order = inv_ref.shape[0], inv_ref.shape[1]
    width = held * order
    tri = dict(zip(blocks_of(held), tri_refs))
    target = cut(direction_ref, lax.axis_index("crow"), width)
    pieces = [None] * held
    for number in reversed(range(held)):
        part = target[:, number * order : (number + 1) * order]
        for later in range(number + 1, held):
            part = part - times(pieces[later], tri[later, number][...], NN)
        pieces[number] = times(part, inv_ref[number], NN)
    out_ref[...] = jnp.concatenate(pieces, axis=1)


def lower_kernel(after_ref, inv_ref, *refs):
    tri_refs, out_ref = refs[:-1], refs[-1]
    held, order = inv_ref.shape[0], inv_ref.shape[1]
    tri = dict(zip(blocks_of(held), tri_refs))
    found = {(n, n): inv_ref[n] for n in range(held)}
    for r in range(1, held):
        for c in range(r):
            total = square(tri[r, c][...], found[c, c])
            for between in range(c + 1, r):
                total = total + square(tri[r, between][...], found[between, c])
            found[r, c] = -square(inv_ref[r], total)
            at = r * (r - 1) // 2 + c
            out_ref[:, at * order : (at + 1) * order] = found[r, c]


def pair_kernel(factor_ref, high_ref, low_ref):
    high, low = pair(factor_ref[...])
    high_ref[...] = high
    low_ref[...] = low


def spread_kernel(cols, *refs):
    extra = refs[: len(refs) - 3 - len(cols)]
    got_refs = refs[len(extra) : len(extra) + len(cols)]
    high_ref, low_ref, out_ref = refs[-3:]
    col = lax.axis_index("ccol")
    piece = got_refs[0][...]
    for at, got in zip(cols[1:], got_refs[1:]):
        piece = jnp.where(col == at, got[...], piece)
    out = times_pair(piece, high_ref[...], low_ref[...], NN)
    for ref in extra:
        out = out + ref[...]
    out_ref[...] = out


def merge_kernel(mine_ref, other_ref, inv_ref, high_out, low_out):
    odd = lax.rem(lax.axis_index("dp"), 2) == 1
    mine, other = mine_ref[...], other_ref[...]
    low = jnp.concatenate([jnp.where(odd, mine, other), jnp.where(odd, other, mine)], axis=0)
    store_turned(low, inv_ref, high_out, low_out)


def solve_kernel(direction_ref, sub_ref, low_ref, inv_ref, out_ref):
    width = sub_ref.shape[1]
    target = cut(direction_ref, lax.axis_index("crow"), width) - sub_ref[...]
    out_ref[...] = back_apply(target, low_ref, inv_ref)


def pick_kernel(places, *refs):
    row, col = lax.axis_index("crow"), lax.axis_index("ccol")
    out = jnp.zeros_like(refs[0][...])
    for (r, c), ref in zip(places, refs[:-1]):
        out = jnp.where((row == r) & (col == c), ref[...], out)
    refs[-1][...] = out


def solve_pick_kernel(places, direction_ref, sub_ref, low_ref, inv_ref, *refs):
    width = sub_ref.shape[1]
    row, col = lax.axis_index("crow"), lax.axis_index("ccol")
    target = cut(direction_ref, row, width) - sub_ref[...]
    out = jnp.where((row == 0) & (col == 0), back_apply(target, low_ref, inv_ref), 0.0)
    for (r, c), ref in zip(places, refs[:-1]):
        out = jnp.where((row == r) & (col == c), ref[...], out)
    refs[-1][...] = out


def triple(value):
    high, middle = pair(value)
    rest = value - high.astype(jnp.float32) - middle.astype(jnp.float32)
    return high, middle, rest.astype(jnp.bfloat16)


def norm_rows(norm, inputs):
    row = lax.broadcasted_iota(jnp.int32, (inputs, norm.shape[1]), 0)
    wide = jnp.broadcast_to(norm, (inputs, norm.shape[1]))
    high, middle, low = (part.astype(jnp.float32) for part in triple(wide))
    rows = jnp.where(row == 0, high, jnp.where(row == 1, middle, jnp.where(row == 2, low, 0.0)))
    return rows.astype(jnp.bfloat16)


def ones_rows(norm, inputs):
    row = lax.broadcasted_iota(jnp.int32, (inputs, norm.shape[1]), 0)
    return jnp.where(row < 3, 1.0, 0.0).astype(jnp.bfloat16)


def scale_by(value, scales_ref):
    inputs = value.shape[0]
    row = lax.broadcasted_iota(jnp.int32, value.shape, 0)
    scales = jnp.full(value.shape, scales_ref[0], jnp.float32)
    for n in range(1, inputs):
        scales = jnp.where(row == n, scales_ref[n], scales)
    return value / scales


def tile_kernel(scales_ref, centres_ref, data_ref, high_ref, low_ref, right):
    inputs = data_ref.shape[0]

    @pl.when(pl.program_id(0) == 0)
    def _():
        scaled = scale_by(data_ref[...], scales_ref)
        norm = jnp.sum(scaled * scaled, axis=0, keepdims=True) * (-0.5 * LOG2E)
        high, middle, low = triple(scaled)
        right[...] = jnp.concatenate(
            [high, middle, high, middle, low, high, norm_rows(norm, inputs), ones_rows(norm, inputs)],
            axis=0,
        )

    scaled = scale_by(centres_ref[...], scales_ref)
    norm = jnp.sum(scaled * scaled, axis=0, keepdims=True) * (-0.5 * LOG2E)
    high, middle, low = triple(scaled * LOG2E)
    left = jnp.concatenate(
        [high, high, middle, middle, high, low, ones_rows(norm, inputs), norm_rows(norm, inputs)], axis=0
    )
    exponent = lax.dot_general(left, right[...], TN, preferred_element_type=jnp.float32)
    high, low = pair(jnp.exp2(exponent))
    high_ref[...] = high
    low_ref[...] = low


def image_kernel(*refs):
    part_refs = refs[:-4]
    high_ref, low_ref, mine_ref, out_ref = refs[-4:]
    piece = part_refs[0][...]
    for ref in part_refs[1:]:
        piece = piece + ref[...]
    mine_ref[...] = piece
    out_ref[...] = times_pair(piece, high_ref[...], low_ref[...], NN)


def normal_kernel(*refs):
    part_refs = refs[:-5]
    high_ref, low_ref, lower_ref, out_ref, half_ref = refs[-5:]
    tall = half_ref.shape[0]
    at = lax.rem(lax.axis_index("dp"), 2) * tall
    half_ref[...] = lower_ref[pl.ds(pl.multiple_of(at, tall), tall), :]
    piece = part_refs[0][...]
    for ref in part_refs[1:]:
        piece = piece + ref[...]
    both = stacked(piece)
    out = lax.dot_general(high_ref[...], both, NT, preferred_element_type=jnp.float32)
    out = out + lax.dot_general(low_ref[...], both, NT, preferred_element_type=jnp.float32)
    out_ref[...] = fold(out.T, piece.shape[0])


def source_kernel(scale, order, mine_ref, *refs):
    part_refs = refs[:-6]
    high_ref, low_ref, half_ref, out_ref, image_ref, half_out = refs[-6:]
    half_out[...] = half_ref[...]
    total = part_refs[0][...]
    for ref in part_refs[1:]:
        total = total + ref[...]
    normal = total * scale + ridge_weight * mine_ref[...]
    out_ref[...] = normal
    image_ref[...] = fore_apply(normal, high_ref, low_ref, order)


def fore_kernel(order, sides, *refs):
    side_refs = refs[:sides]
    got_ref, source_ref, fh_ref, fl_ref, high_ref, low_ref, image_out = refs[sides:]
    left = source_ref[...] - times_pair(got_ref[...], fh_ref[...], fl_ref[...], NN)
    for ref in side_refs:
        left = left - ref[...]
    image_out[...] = fore_apply(left, high_ref, low_ref, order)


def side_kernel(rows, sides, *refs):
    side_refs = refs[:sides]
    got_refs = refs[sides : sides + len(rows)]
    fh_ref, fl_ref, side_out = refs[sides + len(rows) :]
    row = lax.axis_index("crow")
    piece = got_refs[0][...]
    for at, ref in zip(rows[1:], got_refs[1:]):
        piece = jnp.where(row == at, ref[...], piece)
    side = times_pair(piece, fh_ref[...], fl_ref[...], NN)
    for ref in side_refs:
        side = side + ref[...]
    side_out[...] = side


def sum_kernel(*refs):
    total = refs[0][...]
    for ref in refs[1:-1]:
        total = total + ref[...]
    refs[-1][...] = total


def final_kernel(iterate_ref, residual_ref, direction_ref, *refs):
    part_refs = refs[:-4]
    iterate_out, residual_out, direction_out, image_ref = refs[-4:]
    width = part_refs[0].shape[1]
    row = lax.axis_index("crow")
    for step, ref in enumerate(part_refs):
        at = row ^ step
        image_ref[:, pl.ds(pl.multiple_of(at * width, width), width)] = ref[...]
    residual = residual_ref[...]
    direction = direction_ref[...]
    image = image_ref[...]
    gamma = jnp.sum(residual * residual, axis=1, keepdims=True)
    curvature = jnp.sum(direction * image, axis=1, keepdims=True)
    alpha = gamma / curvature
    iterate_out[...] = iterate_ref[...] + alpha * direction
    new_residual = residual - alpha * image
    residual_out[...] = new_residual
    gamma_next = jnp.sum(new_residual * new_residual, axis=1, keepdims=True)
    direction_out[...] = new_residual + (gamma_next / gamma) * direction


def shaped(*shape):
    return jax.ShapeDtypeStruct(shape, jnp.float32)


def call(kernel, outs, *args, limit=12, cost=(10**6, 10**6), **options):
    return pl.pallas_call(
        kernel,
        out_shape=outs,
        compiler_params=pltpu.CompilerParams(vmem_limit_bytes=limit << 20),
        cost_estimate=pl.CostEstimate(flops=cost[0], bytes_accessed=cost[1], transcendentals=0),
        **options,
    )(*args)


def step_of(data, centres, scales, factor, block_inv, iterate, residual, direction):
    dp, crow, ccol = lax.axis_size("dp"), lax.axis_size("crow"), lax.axis_size("ccol")
    held, order = block_inv.shape[0], block_inv.shape[1]
    width = factor.shape[0]
    rows, total = direction.shape
    assert factor.shape[1] == width and crow == ccol and crow in (4, 8) and dp % 2 == 0
    part = shaped(rows, width)
    last = crow - 1

    def spot(d, r, c):
        return (d * crow + r) * ccol + c

    def permute(value, target):
        perm = [
            (spot(d, r, c), spot(*target(d, r, c)))
            for d in range(dp)
            for r in range(crow)
            for c in range(ccol)
        ]
        return lax.ppermute(value, ("dp", "crow", "ccol"), perm)

    def move(value, *pairs):
        to = dict(pairs)
        to.update((b, a) for a, b in pairs)
        return permute(value, lambda d, r, c: (d ^ 1, *to.get((r, c), (r, c))))

    def shifts(value, axis, flip=1):
        steps = range(1, lax.axis_size(axis))
        if axis == "crow":
            return [permute(value, lambda d, r, c: (d ^ flip, r ^ n, c)) for n in steps]
        return [permute(value, lambda d, r, c: (d ^ flip, r, c ^ n)) for n in steps]

    def with_tri(kernel, outs, *args, limit=12):
        full = [pl.BlockSpec(a.shape, lambda i, n=a.ndim: (0,) * n) for a in args]
        tri = [pl.BlockSpec((order, order), lambda i, r=r, c=c: (r, c)) for r, c in blocks_of(held)]
        shape = outs.shape
        return call(
            kernel, outs, *args, *([factor] * len(tri)), grid=(1,), in_specs=full + tri,
            out_specs=pl.BlockSpec(shape, lambda i: (0, 0)), limit=limit,
        )

    piece = with_tri(first_kernel, part, direction, block_inv, limit=58)
    found = {last: piece}
    low = with_tri(lower_kernel, shaped(order, len(blocks_of(held)) * order), piece, block_inv)
    wide = jax.ShapeDtypeStruct((width, width), jnp.bfloat16)
    high_f, low_f = call(pair_kernel, [wide, wide], factor)
    turned_f = call(turn_factor_kernel, [wide, wide], factor)
    turned = call(turn_kernel, [wide, wide], low, block_inv)

    samples = data.shape[1]
    tile = order
    inputs = data.shape[0]
    kernel_shape = jax.ShapeDtypeStruct((width, samples), jnp.bfloat16)
    high_k, low_k = call(
        tile_kernel, [kernel_shape] * 2, scales, centres, data,
        grid=(width // tile,),
        in_specs=[
            pl.BlockSpec(memory_space=pltpu.SMEM),
            pl.BlockSpec((inputs, tile), lambda i: (0, i)),
            pl.BlockSpec((inputs, samples), lambda i: (0, 0)),
        ],
        out_specs=[pl.BlockSpec((tile, samples), lambda i: (i, 0))] * 2,
        scratch_shapes=[pltpu.VMEM((8 * inputs, samples), jnp.bfloat16)],
        limit=20,
    )

    def spread(cols, extra, got):
        return call(functools.partial(spread_kernel, cols), part, *extra, *got, high_f, low_f)

    sums = []
    for step in range(last, 0, -1):
        cols = list(range(step))[::-1]
        got = [move(piece, ((step, step), (step, c))) for c in cols]
        down = [((step, c), (step - 1, c)) for c in cols]
        if step == last:
            sub = move(spread(cols[:1], [], got[:1]), down[0])
            sums = [move(spread(cols[1:], [], got[1:]), *down[1:])]
        else:
            sub = move(spread(cols, sums, got), *down)
            sums = [sub]
        if step > 1:
            piece = call(solve_kernel, part, direction, sub, low, block_inv)
            found[step - 1] = piece
    places = [(n, n) for n in range(1, crow)]
    own = call(
        functools.partial(solve_pick_kernel, places), part, direction, sub, low, block_inv,
        *[found[n] for n in range(1, crow)],
    )

    parts = [own] + shifts(own, "crow")
    mine, images = call(image_kernel, [part, shaped(rows, samples)], *parts, high_k, low_k, limit=16)
    images = [images] + shifts(images, "ccol", 0)
    half = shaped(order // 2, low.shape[1])
    summed, half = call(normal_kernel, [part, half], *images, high_k, low_k, low, limit=16)
    if dp == 2:
        summed = summed + permute(summed, lambda d, r, c: (d ^ 1, r, c))
    else:
        summed = lax.psum(summed, "dp")
    parts = [summed] + shifts(summed, "crow")
    beside = [((n, n), (n, n - 1)) for n in range(1, crow)]
    half = move(half, *beside)
    scale = 1.0 / (samples * dp * crow)
    source, image, half = call(
        functools.partial(source_kernel, scale, order), [part, part, shaped(*half.shape)],
        mine, *parts, *turned, half,
    )
    near = call(merge_kernel, [wide, wide], half, move(half), block_inv)
    done = [image]
    places = [(0, 0)]
    side = []
    for step in range(1, crow):
        later = list(range(step + 1, crow))
        first = move(image, (places[-1], (step, step - 1)))
        if step == 1:
            source = move(source, *beside)
        if side:
            shift = [((at, step - 2), (at, step - 1)) for at in range(step, crow)]
            side = [move(side[0], *shift)]
        others = [move(image, (places[-1], (at, step - 1))) for at in later]
        image = call(
            functools.partial(fore_kernel, order, len(side)), part,
            *side, first, source, *turned_f, *near,
        )
        if later:
            side = [
                call(
                    functools.partial(side_kernel, later, len(side)), part, *side, *others, *turned_f
                )
            ]
        done.append(image)
        places.append((step, step - 1))
    own = call(functools.partial(pick_kernel, places), part, *done)
    own = call(sum_kernel, part, own, *shifts(own, "ccol"))
    full = shaped(rows, total)
    return tuple(
        call(
            final_kernel, [full, full, full], iterate, residual, direction, own, *shifts(own, "crow"),
            scratch_shapes=[pltpu.VMEM((rows, total), jnp.float32)],
        )
    )


def solution(mesh):
    placed = (
        P(None, ("dp", "crow")),
        P(None, "ccol"),
        P(),
        P("crow", "ccol"),
        P("crow", None, None),
        P(),
        P(),
        P(),
    )
    return jax.shard_map(
        step_of, mesh=mesh, in_specs=placed, out_specs=(P(), P(), P()), check_vma=False
    )
```

```python
import functools
import math

import jax
import jax.numpy as jnp
from jax import lax
from jax.experimental import pallas as pl
from jax.experimental.pallas import tpu as pltpu
from jax.sharding import PartitionSpec as P


ridge_weight = 0.2
LOG2E = 1.0 / math.log(2.0)
NN = (((1,), (0,)), ((), ()))
NT = (((1,), (1,)), ((), ()))
TN = (((0,), (0,)), ((), ()))


def pair(value):
    high = value.astype(jnp.bfloat16)
    low = (value - high.astype(jnp.float32)).astype(jnp.bfloat16)
    return high, low


def stacked(value):
    high, low = pair(value)
    return jnp.concatenate([high, low], axis=0)


def fold(product, rows):
    return product[:rows] + product[rows:]


def times_pair(rows, high, low, dims):
    both = stacked(rows)
    out = lax.dot_general(both, high, dims, preferred_element_type=jnp.float32)
    out = out + lax.dot_general(both, low, dims, preferred_element_type=jnp.float32)
    return fold(out, rows.shape[0])


def times(rows, matrix, dims):
    high, low = pair(matrix)
    return times_pair(rows, high, low, dims)


def blocks_of(held):
    return [(r, c) for r in range(1, held) for c in range(r)]


def lower(low_ref, order, r, c):
    at = r * (r - 1) // 2 + c
    return low_ref[:, at * order : (at + 1) * order]


def square(one, other):
    first, first_low = pair(one)
    second, second_low = pair(other)
    out = lax.dot_general(first, second, NN, preferred_element_type=jnp.float32)
    out = out + lax.dot_general(first, second_low, NN, preferred_element_type=jnp.float32)
    return out + lax.dot_general(first_low, second, NN, preferred_element_type=jnp.float32)


def cut(ref, at, width):
    return ref[:, pl.ds(pl.multiple_of(at * width, width), width)]


def back_apply(target, low_ref, inv_ref):
    held, order = inv_ref.shape[0], inv_ref.shape[1]
    parts = [target[:, n * order : (n + 1) * order] for n in range(held)]
    pieces = []
    for c in range(held):
        piece = times(parts[c], inv_ref[c], NN)
        for r in range(c + 1, held):
            piece = piece + times(parts[r], lower(low_ref, order, r, c), NN)
        pieces.append(piece)
    return jnp.concatenate(pieces, axis=1)


def fore_apply(source, high_ref, low_ref, order):
    pieces = []
    for end in range(order, source.shape[1] + 1, order):
        block = (slice(0, end), slice(end - order, end))
        pieces.append(times_pair(source[:, :end], high_ref[block], low_ref[block], NN))
    return jnp.concatenate(pieces, axis=1)


def store_turned(low, inv_ref, high_out, low_out):
    held, order = inv_ref.shape[0], inv_ref.shape[1]
    for r in range(held):
        for c in range(r + 1):
            at = r * (r - 1) // 2 + c
            block = inv_ref[r] if r == c else low[:, at * order : (at + 1) * order]
            place = (slice(c * order, (c + 1) * order), slice(r * order, (r + 1) * order))
            high_out[place], low_out[place] = pair(block.T)


def turn_kernel(low_ref, inv_ref, high_out, low_out):
    store_turned(low_ref[...], inv_ref, high_out, low_out)


def turn_factor_kernel(factor_ref, high_out, low_out):
    high_out[...], low_out[...] = pair(factor_ref[...].T)


def first_kernel(direction_ref, inv_ref, *refs):
    tri_refs, out_ref = refs[:-1], refs[-1]
    held, order = inv_ref.shape[0], inv_ref.shape[1]
    width = held * order
    tri = dict(zip(blocks_of(held), tri_refs))
    target = cut(direction_ref, lax.axis_index("crow"), width)
    pieces = [None] * held
    for number in reversed(range(held)):
        part = target[:, number * order : (number + 1) * order]
        for later in range(number + 1, held):
            part = part - times(pieces[later], tri[later, number][...], NN)
        pieces[number] = times(part, inv_ref[number], NN)
    out_ref[...] = jnp.concatenate(pieces, axis=1)


def lower_kernel(inv_ref, *refs):
    tri_refs, out_ref, half_ref = refs[:-2], refs[-2], refs[-1]
    held, order = inv_ref.shape[0], inv_ref.shape[1]
    tri = dict(zip(blocks_of(held), tri_refs))
    found = {(n, n): inv_ref[n] for n in range(held)}
    for r in range(1, held):
        for c in range(r):
            total = square(tri[r, c][...], found[c, c])
            for between in range(c + 1, r):
                total = total + square(tri[r, between][...], found[between, c])
            found[r, c] = -square(inv_ref[r], total)
            at = r * (r - 1) // 2 + c
            out_ref[:, at * order : (at + 1) * order] = found[r, c]
    tall = half_ref.shape[0]
    at = lax.rem(lax.axis_index("dp"), 2) * tall
    half_ref[...] = out_ref[pl.ds(pl.multiple_of(at, tall), tall), :]


def pair_kernel(factor_ref, high_ref, low_ref):
    high, low = pair(factor_ref[...])
    high_ref[...] = high
    low_ref[...] = low


def spread_kernel(cols, *refs):
    extra = refs[: len(refs) - 3 - len(cols)]
    got_refs = refs[len(extra) : len(extra) + len(cols)]
    high_ref, low_ref, out_ref = refs[-3:]
    col = lax.axis_index("ccol")
    piece = got_refs[0][...]
    for at, got in zip(cols[1:], got_refs[1:]):
        piece = jnp.where(col == at, got[...], piece)
    out = times_pair(piece, high_ref[...], low_ref[...], NN)
    for ref in extra:
        out = out + ref[...]
    out_ref[...] = out


def merge_kernel(mine_ref, other_ref, inv_ref, high_out, low_out):
    odd = lax.rem(lax.axis_index("dp"), 2) == 1
    mine, other = mine_ref[...], other_ref[...]
    low = jnp.concatenate([jnp.where(odd, mine, other), jnp.where(odd, other, mine)], axis=0)
    store_turned(low, inv_ref, high_out, low_out)


def solve_kernel(direction_ref, sub_ref, low_ref, inv_ref, out_ref):
    width = sub_ref.shape[1]
    target = cut(direction_ref, lax.axis_index("crow"), width) - sub_ref[...]
    out_ref[...] = back_apply(target, low_ref, inv_ref)


def pick_kernel(places, *refs):
    row, col = lax.axis_index("crow"), lax.axis_index("ccol")
    out = jnp.zeros_like(refs[0][...])
    for (r, c), ref in zip(places, refs[:-1]):
        out = jnp.where((row == r) & (col == c), ref[...], out)
    refs[-1][...] = out


def solve_pick_kernel(places, direction_ref, sub_ref, low_ref, inv_ref, *refs):
    width = sub_ref.shape[1]
    row, col = lax.axis_index("crow"), lax.axis_index("ccol")
    target = cut(direction_ref, row, width) - sub_ref[...]
    out = jnp.where((row == 0) & (col == 0), back_apply(target, low_ref, inv_ref), 0.0)
    for (r, c), ref in zip(places, refs[:-1]):
        out = jnp.where((row == r) & (col == c), ref[...], out)
    refs[-1][...] = out


def triple(value):
    high, middle = pair(value)
    rest = value - high.astype(jnp.float32) - middle.astype(jnp.float32)
    return high, middle, rest.astype(jnp.bfloat16)


def norm_rows(norm, inputs):
    row = lax.broadcasted_iota(jnp.int32, (inputs, norm.shape[1]), 0)
    wide = jnp.broadcast_to(norm, (inputs, norm.shape[1]))
    high, middle, low = (part.astype(jnp.float32) for part in triple(wide))
    rows = jnp.where(row == 0, high, jnp.where(row == 1, middle, jnp.where(row == 2, low, 0.0)))
    return rows.astype(jnp.bfloat16)


def ones_rows(norm, inputs):
    row = lax.broadcasted_iota(jnp.int32, (inputs, norm.shape[1]), 0)
    return jnp.where(row < 3, 1.0, 0.0).astype(jnp.bfloat16)


def scale_by(value, scales_ref):
    inputs = value.shape[0]
    row = lax.broadcasted_iota(jnp.int32, value.shape, 0)
    scales = jnp.full(value.shape, scales_ref[0], jnp.float32)
    for n in range(1, inputs):
        scales = jnp.where(row == n, scales_ref[n], scales)
    return value / scales


def tile_kernel(scales_ref, centres_ref, data_ref, high_ref, low_ref, right):
    inputs = data_ref.shape[0]

    @pl.when(pl.program_id(0) == 0)
    def _():
        scaled = scale_by(data_ref[...], scales_ref)
        norm = jnp.sum(scaled * scaled, axis=0, keepdims=True) * (-0.5 * LOG2E)
        high, middle, low = triple(scaled)
        right[...] = jnp.concatenate(
            [high, middle, high, middle, low, high, norm_rows(norm, inputs), ones_rows(norm, inputs)],
            axis=0,
        )

    scaled = scale_by(centres_ref[...], scales_ref)
    norm = jnp.sum(scaled * scaled, axis=0, keepdims=True) * (-0.5 * LOG2E)
    high, middle, low = triple(scaled * LOG2E)
    left = jnp.concatenate(
        [high, high, middle, middle, high, low, ones_rows(norm, inputs), norm_rows(norm, inputs)], axis=0
    )
    exponent = lax.dot_general(left, right[...], TN, preferred_element_type=jnp.float32)
    high, low = pair(jnp.exp2(exponent))
    high_ref[...] = high
    low_ref[...] = low


def image_kernel(*refs):
    part_refs = refs[:-4]
    high_ref, low_ref, mine_ref, out_ref = refs[-4:]
    piece = part_refs[0][...]
    for ref in part_refs[1:]:
        piece = piece + ref[...]
    mine_ref[...] = piece
    out_ref[...] = times_pair(piece, high_ref[...], low_ref[...], NN)


def normal_kernel(*refs):
    part_refs = refs[:-3]
    high_ref, low_ref, out_ref = refs[-3:]
    piece = part_refs[0][...]
    for ref in part_refs[1:]:
        piece = piece + ref[...]
    both = stacked(piece)
    out = lax.dot_general(high_ref[...], both, NT, preferred_element_type=jnp.float32)
    out = out + lax.dot_general(low_ref[...], both, NT, preferred_element_type=jnp.float32)
    out_ref[...] = fold(out.T, piece.shape[0])


def source_kernel(scale, order, mine_ref, *refs):
    part_refs = refs[:-4]
    high_ref, low_ref, out_ref, image_ref = refs[-4:]
    total = part_refs[0][...]
    for ref in part_refs[1:]:
        total = total + ref[...]
    normal = total * scale + ridge_weight * mine_ref[...]
    out_ref[...] = normal
    image_ref[...] = fore_apply(normal, high_ref, low_ref, order)


def fore_kernel(order, sides, *refs):
    side_refs = refs[:sides]
    got_ref, source_ref, fh_ref, fl_ref, high_ref, low_ref, image_out = refs[sides:]
    left = source_ref[...] - times_pair(got_ref[...], fh_ref[...], fl_ref[...], NN)
    for ref in side_refs:
        left = left - ref[...]
    image_out[...] = fore_apply(left, high_ref, low_ref, order)


def side_kernel(rows, sides, *refs):
    side_refs = refs[:sides]
    got_refs = refs[sides : sides + len(rows)]
    fh_ref, fl_ref, side_out = refs[sides + len(rows) :]
    row = lax.axis_index("crow")
    piece = got_refs[0][...]
    for at, ref in zip(rows[1:], got_refs[1:]):
        piece = jnp.where(row == at, ref[...], piece)
    side = times_pair(piece, fh_ref[...], fl_ref[...], NN)
    for ref in side_refs:
        side = side + ref[...]
    side_out[...] = side


def sum_kernel(*refs):
    total = refs[0][...]
    for ref in refs[1:-1]:
        total = total + ref[...]
    refs[-1][...] = total


def final_kernel(iterate_ref, residual_ref, direction_ref, *refs):
    part_refs = refs[:-4]
    iterate_out, residual_out, direction_out, image_ref = refs[-4:]
    width = part_refs[0].shape[1]
    row = lax.axis_index("crow")
    for step, ref in enumerate(part_refs):
        at = row ^ step
        image_ref[:, pl.ds(pl.multiple_of(at * width, width), width)] = ref[...]
    residual = residual_ref[...]
    direction = direction_ref[...]
    image = image_ref[...]
    gamma = jnp.sum(residual * residual, axis=1, keepdims=True)
    curvature = jnp.sum(direction * image, axis=1, keepdims=True)
    alpha = gamma / curvature
    iterate_out[...] = iterate_ref[...] + alpha * direction
    new_residual = residual - alpha * image
    residual_out[...] = new_residual
    gamma_next = jnp.sum(new_residual * new_residual, axis=1, keepdims=True)
    direction_out[...] = new_residual + (gamma_next / gamma) * direction


def shaped(*shape):
    return jax.ShapeDtypeStruct(shape, jnp.float32)


def call(kernel, outs, *args, limit=12, cost=(10**6, 10**6), **options):
    return pl.pallas_call(
        kernel,
        out_shape=outs,
        compiler_params=pltpu.CompilerParams(vmem_limit_bytes=limit << 20),
        cost_estimate=pl.CostEstimate(flops=cost[0], bytes_accessed=cost[1], transcendentals=0),
        **options,
    )(*args)


def step_of(data, centres, scales, factor, block_inv, iterate, residual, direction):
    dp, crow, ccol = lax.axis_size("dp"), lax.axis_size("crow"), lax.axis_size("ccol")
    held, order = block_inv.shape[0], block_inv.shape[1]
    width = factor.shape[0]
    rows, total = direction.shape
    assert factor.shape[1] == width and crow == ccol and crow in (4, 8) and dp % 2 == 0
    part = shaped(rows, width)
    last = crow - 1

    def spot(d, r, c):
        return (d * crow + r) * ccol + c

    def permute(value, target):
        perm = [
            (spot(d, r, c), spot(*target(d, r, c)))
            for d in range(dp)
            for r in range(crow)
            for c in range(ccol)
        ]
        return lax.ppermute(value, ("dp", "crow", "ccol"), perm)

    def move(value, *pairs):
        to = dict(pairs)
        to.update((b, a) for a, b in pairs)
        return permute(value, lambda d, r, c: (d ^ 1, *to.get((r, c), (r, c))))

    def shifts(value, axis, flip=1):
        steps = range(1, lax.axis_size(axis))
        if axis == "crow":
            return [permute(value, lambda d, r, c: (d ^ flip, r ^ n, c)) for n in steps]
        return [permute(value, lambda d, r, c: (d ^ flip, r, c ^ n)) for n in steps]

    def with_tri(kernel, outs, *args, limit=12):
        full = [pl.BlockSpec(a.shape, lambda i, n=a.ndim: (0,) * n) for a in args]
        tri = [pl.BlockSpec((order, order), lambda i, r=r, c=c: (r, c)) for r, c in blocks_of(held)]
        return call(
            kernel, outs, *args, *([factor] * len(tri)), grid=(1,), in_specs=full + tri,
            out_specs=[pl.BlockSpec(out.shape, lambda i: (0, 0)) for out in outs], limit=limit,
        )

    (piece,) = with_tri(first_kernel, [part], direction, block_inv, limit=58)
    found = {last: piece}
    spots = len(blocks_of(held)) * order
    low, half = with_tri(lower_kernel, [shaped(order, spots), shaped(order // 2, spots)], block_inv)
    wide = jax.ShapeDtypeStruct((width, width), jnp.bfloat16)
    high_f, low_f = call(pair_kernel, [wide, wide], factor)
    turned_f = call(turn_factor_kernel, [wide, wide], factor)
    turned = call(turn_kernel, [wide, wide], low, block_inv)

    samples = data.shape[1]
    tile = order
    inputs = data.shape[0]
    kernel_shape = jax.ShapeDtypeStruct((width, samples), jnp.bfloat16)
    high_k, low_k = call(
        tile_kernel, [kernel_shape] * 2, scales, centres, data,
        grid=(width // tile,),
        in_specs=[
            pl.BlockSpec(memory_space=pltpu.SMEM),
            pl.BlockSpec((inputs, tile), lambda i: (0, i)),
            pl.BlockSpec((inputs, samples), lambda i: (0, 0)),
        ],
        out_specs=[pl.BlockSpec((tile, samples), lambda i: (i, 0))] * 2,
        scratch_shapes=[pltpu.VMEM((8 * inputs, samples), jnp.bfloat16)],
        limit=20,
    )

    def spread(cols, extra, got):
        return call(functools.partial(spread_kernel, cols), part, *extra, *got, high_f, low_f)

    sums = []
    for step in range(last, 0, -1):
        cols = list(range(step))[::-1]
        got = [move(piece, ((step, step), (step, c))) for c in cols]
        down = [((step, c), (step - 1, c)) for c in cols]
        if step == last:
            sub = move(spread(cols[:1], [], got[:1]), down[0])
            sums = [move(spread(cols[1:], [], got[1:]), *down[1:])]
        else:
            sub = move(spread(cols, sums, got), *down)
            sums = [sub]
        if step > 1:
            piece = call(solve_kernel, part, direction, sub, low, block_inv)
            found[step - 1] = piece
    places = [(n, n) for n in range(1, crow)]
    own = call(
        functools.partial(solve_pick_kernel, places), part, direction, sub, low, block_inv,
        *[found[n] for n in range(1, crow)],
    )

    parts = [own] + shifts(own, "crow")
    mine, images = call(image_kernel, [part, shaped(rows, samples)], *parts, high_k, low_k, limit=16)
    images = [images] + shifts(images, "ccol", 0)
    summed = call(normal_kernel, part, *images, high_k, low_k, limit=16)
    if dp == 2:
        summed = summed + permute(summed, lambda d, r, c: (d ^ 1, r, c))
    else:
        summed = lax.psum(summed, "dp")
    parts = [summed] + shifts(summed, "crow")
    beside = [((n, n), (n, n - 1)) for n in range(1, crow)]
    half = move(half, *beside)
    scale = 1.0 / (samples * dp * crow)
    source, image = call(
        functools.partial(source_kernel, scale, order), [part, part], mine, *parts, *turned
    )
    near = call(merge_kernel, [wide, wide], half, move(half), block_inv)
    done = [image]
    places = [(0, 0)]
    side = []
    for step in range(1, crow):
        later = list(range(step + 1, crow))
        first = move(image, (places[-1], (step, step - 1)))
        if step == 1:
            source = move(source, *beside)
        if side:
            shift = [((at, step - 2), (at, step - 1)) for at in range(step, crow)]
            side = [move(side[0], *shift)]
        others = [move(image, (places[-1], (at, step - 1))) for at in later]
        image = call(
            functools.partial(fore_kernel, order, len(side)), part,
            *side, first, source, *turned_f, *near,
        )
        if later:
            side = [
                call(
                    functools.partial(side_kernel, later, len(side)), part, *side, *others, *turned_f
                )
            ]
        done.append(image)
        places.append((step, step - 1))
    own = call(functools.partial(pick_kernel, places), part, *done)
    own = call(sum_kernel, part, own, *shifts(own, "ccol"))
    full = shaped(rows, total)
    return tuple(
        call(
            final_kernel, [full, full, full], iterate, residual, direction, own, *shifts(own, "crow"),
            scratch_shapes=[pltpu.VMEM((rows, total), jnp.float32)],
        )
    )


def solution(mesh):
    placed = (
        P(None, ("dp", "crow")),
        P(None, "ccol"),
        P(),
        P("crow", "ccol"),
        P("crow", None, None),
        P(),
        P(),
        P(),
    )
    return jax.shard_map(
        step_of, mesh=mesh, in_specs=placed, out_specs=(P(), P(), P()), check_vma=False
    )
```

```python
import functools
import math

import jax
import jax.numpy as jnp
from jax import lax
from jax.experimental import pallas as pl
from jax.experimental.pallas import tpu as pltpu
from jax.sharding import PartitionSpec as P


ridge_weight = 0.2
LOG2E = 1.0 / math.log(2.0)
NN = (((1,), (0,)), ((), ()))
NT = (((1,), (1,)), ((), ()))
TN = (((0,), (0,)), ((), ()))


def pair(value):
    high = value.astype(jnp.bfloat16)
    low = (value - high.astype(jnp.float32)).astype(jnp.bfloat16)
    return high, low


def stacked(value):
    high, low = pair(value)
    return jnp.concatenate([high, low], axis=0)


def fold(product, rows):
    return product[:rows] + product[rows:]


def times_pair(rows, high, low, dims):
    both = stacked(rows)
    out = lax.dot_general(both, high, dims, preferred_element_type=jnp.float32)
    out = out + lax.dot_general(both, low, dims, preferred_element_type=jnp.float32)
    return fold(out, rows.shape[0])


def times(rows, matrix, dims):
    high, low = pair(matrix)
    return times_pair(rows, high, low, dims)


def blocks_of(held):
    return [(r, c) for r in range(1, held) for c in range(r)]


def lower(low_ref, order, r, c):
    at = r * (r - 1) // 2 + c
    return low_ref[:, at * order : (at + 1) * order]


def square(one, other):
    first, first_low = pair(one)
    second, second_low = pair(other)
    out = lax.dot_general(first, second, NN, preferred_element_type=jnp.float32)
    out = out + lax.dot_general(first, second_low, NN, preferred_element_type=jnp.float32)
    return out + lax.dot_general(first_low, second, NN, preferred_element_type=jnp.float32)


def cut(ref, at, width):
    return ref[:, pl.ds(pl.multiple_of(at * width, width), width)]


def back_apply(target, low_ref, inv_ref):
    held, order = inv_ref.shape[0], inv_ref.shape[1]
    parts = [target[:, n * order : (n + 1) * order] for n in range(held)]
    pieces = []
    for c in range(held):
        piece = times(parts[c], inv_ref[c], NN)
        for r in range(c + 1, held):
            piece = piece + times(parts[r], lower(low_ref, order, r, c), NN)
        pieces.append(piece)
    return jnp.concatenate(pieces, axis=1)


def fore_apply(source, high_ref, low_ref, order):
    pieces = []
    for end in range(order, source.shape[1] + 1, order):
        block = (slice(0, end), slice(end - order, end))
        pieces.append(times_pair(source[:, :end], high_ref[block], low_ref[block], NN))
    return jnp.concatenate(pieces, axis=1)


def store_turned(low, inv_ref, high_out, low_out):
    held, order = inv_ref.shape[0], inv_ref.shape[1]
    for r in range(held):
        for c in range(r + 1):
            at = r * (r - 1) // 2 + c
            block = inv_ref[r] if r == c else low[:, at * order : (at + 1) * order]
            place = (slice(c * order, (c + 1) * order), slice(r * order, (r + 1) * order))
            high_out[place], low_out[place] = pair(block.T)


def turn_kernel(low_ref, inv_ref, high_out, low_out):
    store_turned(low_ref[...], inv_ref, high_out, low_out)


def turn_factor_kernel(factor_ref, high_out, low_out):
    high_out[...], low_out[...] = pair(factor_ref[...].T)


def first_kernel(direction_ref, inv_ref, *refs):
    tri_refs, out_ref = refs[:-1], refs[-1]
    held, order = inv_ref.shape[0], inv_ref.shape[1]
    width = held * order
    tri = dict(zip(blocks_of(held), tri_refs))
    target = cut(direction_ref, lax.axis_index("crow"), width)
    pieces = [None] * held
    for number in reversed(range(held)):
        part = target[:, number * order : (number + 1) * order]
        for later in range(number + 1, held):
            part = part - times(pieces[later], tri[later, number][...], NN)
        pieces[number] = times(part, inv_ref[number], NN)
    out_ref[...] = jnp.concatenate(pieces, axis=1)


def lower_kernel(inv_ref, *refs):
    tri_refs, (out_ref, half_ref, rest_ref) = refs[:-3], refs[-3:]
    held, order = inv_ref.shape[0], inv_ref.shape[1]
    tri = dict(zip(blocks_of(held), tri_refs))
    found = {(n, n): inv_ref[n] for n in range(held)}
    for r in range(1, held):
        for c in range(r):
            total = square(tri[r, c][...], found[c, c])
            for between in range(c + 1, r):
                total = total + square(tri[r, between][...], found[between, c])
            found[r, c] = -square(inv_ref[r], total)
            at = r * (r - 1) // 2 + c
            out_ref[:, at * order : (at + 1) * order] = found[r, c]
    tall = half_ref.shape[0]
    at = lax.rem(lax.axis_index("dp"), 2) * tall
    split = half_ref.shape[1]
    half_ref[...] = out_ref[pl.ds(pl.multiple_of(at, tall), tall), :split]
    rest_ref[...] = out_ref[:, split:]


def pair_kernel(factor_ref, high_ref, low_ref):
    high, low = pair(factor_ref[...])
    high_ref[...] = high
    low_ref[...] = low


def spread_kernel(cols, *refs):
    extra = refs[: len(refs) - 3 - len(cols)]
    got_refs = refs[len(extra) : len(extra) + len(cols)]
    high_ref, low_ref, out_ref = refs[-3:]
    col = lax.axis_index("ccol")
    piece = got_refs[0][...]
    for at, got in zip(cols[1:], got_refs[1:]):
        piece = jnp.where(col == at, got[...], piece)
    out = times_pair(piece, high_ref[...], low_ref[...], NN)
    for ref in extra:
        out = out + ref[...]
    out_ref[...] = out


def merge_kernel(mine_ref, other_ref, rest_ref, inv_ref, high_out, low_out):
    odd = lax.rem(lax.axis_index("dp"), 2) == 1
    mine, other = mine_ref[...], other_ref[...]
    low = jnp.concatenate([jnp.where(odd, mine, other), jnp.where(odd, other, mine)], axis=0)
    low = jnp.concatenate([low, rest_ref[...]], axis=1)
    store_turned(low, inv_ref, high_out, low_out)


def solve_kernel(direction_ref, sub_ref, low_ref, inv_ref, out_ref):
    width = sub_ref.shape[1]
    target = cut(direction_ref, lax.axis_index("crow"), width) - sub_ref[...]
    out_ref[...] = back_apply(target, low_ref, inv_ref)


def pick_kernel(places, *refs):
    row, col = lax.axis_index("crow"), lax.axis_index("ccol")
    out = jnp.zeros_like(refs[0][...])
    for (r, c), ref in zip(places, refs[:-1]):
        out = jnp.where((row == r) & (col == c), ref[...], out)
    refs[-1][...] = out


def solve_pick_kernel(places, direction_ref, sub_ref, low_ref, inv_ref, *refs):
    width = sub_ref.shape[1]
    row, col = lax.axis_index("crow"), lax.axis_index("ccol")
    target = cut(direction_ref, row, width) - sub_ref[...]
    out = jnp.where((row == 0) & (col == 0), back_apply(target, low_ref, inv_ref), 0.0)
    for (r, c), ref in zip(places, refs[:-1]):
        out = jnp.where((row == r) & (col == c), ref[...], out)
    refs[-1][...] = out


def triple(value):
    high, middle = pair(value)
    rest = value - high.astype(jnp.float32) - middle.astype(jnp.float32)
    return high, middle, rest.astype(jnp.bfloat16)


def norm_rows(norm, inputs):
    row = lax.broadcasted_iota(jnp.int32, (inputs, norm.shape[1]), 0)
    wide = jnp.broadcast_to(norm, (inputs, norm.shape[1]))
    high, middle, low = (part.astype(jnp.float32) for part in triple(wide))
    rows = jnp.where(row == 0, high, jnp.where(row == 1, middle, jnp.where(row == 2, low, 0.0)))
    return rows.astype(jnp.bfloat16)


def ones_rows(norm, inputs):
    row = lax.broadcasted_iota(jnp.int32, (inputs, norm.shape[1]), 0)
    return jnp.where(row < 3, 1.0, 0.0).astype(jnp.bfloat16)


def scale_by(value, scales_ref):
    inputs = value.shape[0]
    row = lax.broadcasted_iota(jnp.int32, value.shape, 0)
    scales = jnp.full(value.shape, scales_ref[0], jnp.float32)
    for n in range(1, inputs):
        scales = jnp.where(row == n, scales_ref[n], scales)
    return value / scales


def tile_kernel(scales_ref, centres_ref, data_ref, high_ref, low_ref, right):
    inputs = data_ref.shape[0]

    @pl.when(pl.program_id(0) == 0)
    def _():
        scaled = scale_by(data_ref[...], scales_ref)
        norm = jnp.sum(scaled * scaled, axis=0, keepdims=True) * (-0.5 * LOG2E)
        high, middle, low = triple(scaled)
        right[...] = jnp.concatenate(
            [high, middle, high, middle, low, high, norm_rows(norm, inputs), ones_rows(norm, inputs)],
            axis=0,
        )

    scaled = scale_by(centres_ref[...], scales_ref)
    norm = jnp.sum(scaled * scaled, axis=0, keepdims=True) * (-0.5 * LOG2E)
    high, middle, low = triple(scaled * LOG2E)
    left = jnp.concatenate(
        [high, high, middle, middle, high, low, ones_rows(norm, inputs), norm_rows(norm, inputs)], axis=0
    )
    exponent = lax.dot_general(left, right[...], TN, preferred_element_type=jnp.float32)
    high, low = pair(jnp.exp2(exponent))
    high_ref[...] = high
    low_ref[...] = low


def image_kernel(*refs):
    part_refs = refs[:-4]
    high_ref, low_ref, mine_ref, out_ref = refs[-4:]
    piece = part_refs[0][...]
    for ref in part_refs[1:]:
        piece = piece + ref[...]
    mine_ref[...] = piece
    out_ref[...] = times_pair(piece, high_ref[...], low_ref[...], NN)


def normal_kernel(*refs):
    part_refs = refs[:-3]
    high_ref, low_ref, out_ref = refs[-3:]
    piece = part_refs[0][...]
    for ref in part_refs[1:]:
        piece = piece + ref[...]
    both = stacked(piece)
    out = lax.dot_general(high_ref[...], both, NT, preferred_element_type=jnp.float32)
    out = out + lax.dot_general(low_ref[...], both, NT, preferred_element_type=jnp.float32)
    out_ref[...] = fold(out.T, piece.shape[0])


def source_kernel(scale, order, mine_ref, *refs):
    part_refs = refs[:-4]
    high_ref, low_ref, out_ref, image_ref = refs[-4:]
    total = part_refs[0][...]
    for ref in part_refs[1:]:
        total = total + ref[...]
    normal = total * scale + ridge_weight * mine_ref[...]
    out_ref[...] = normal
    image_ref[...] = fore_apply(normal, high_ref, low_ref, order)


def fore_kernel(order, sides, *refs):
    side_refs = refs[:sides]
    got_ref, source_ref, fh_ref, fl_ref, high_ref, low_ref, image_out = refs[sides:]
    left = source_ref[...] - times_pair(got_ref[...], fh_ref[...], fl_ref[...], NN)
    for ref in side_refs:
        left = left - ref[...]
    image_out[...] = fore_apply(left, high_ref, low_ref, order)


def side_kernel(rows, sides, *refs):
    side_refs = refs[:sides]
    got_refs = refs[sides : sides + len(rows)]
    fh_ref, fl_ref, side_out = refs[sides + len(rows) :]
    row = lax.axis_index("crow")
    piece = got_refs[0][...]
    for at, ref in zip(rows[1:], got_refs[1:]):
        piece = jnp.where(row == at, ref[...], piece)
    side = times_pair(piece, fh_ref[...], fl_ref[...], NN)
    for ref in side_refs:
        side = side + ref[...]
    side_out[...] = side


def sum_kernel(*refs):
    total = refs[0][...]
    for ref in refs[1:-1]:
        total = total + ref[...]
    refs[-1][...] = total


def final_kernel(iterate_ref, residual_ref, direction_ref, *refs):
    part_refs = refs[:-4]
    iterate_out, residual_out, direction_out, image_ref = refs[-4:]
    width = part_refs[0].shape[1]
    row = lax.axis_index("crow")
    for step, ref in enumerate(part_refs):
        at = row ^ step
        image_ref[:, pl.ds(pl.multiple_of(at * width, width), width)] = ref[...]
    residual = residual_ref[...]
    direction = direction_ref[...]
    image = image_ref[...]
    gamma = jnp.sum(residual * residual, axis=1, keepdims=True)
    curvature = jnp.sum(direction * image, axis=1, keepdims=True)
    alpha = gamma / curvature
    iterate_out[...] = iterate_ref[...] + alpha * direction
    new_residual = residual - alpha * image
    residual_out[...] = new_residual
    gamma_next = jnp.sum(new_residual * new_residual, axis=1, keepdims=True)
    direction_out[...] = new_residual + (gamma_next / gamma) * direction


def shaped(*shape):
    return jax.ShapeDtypeStruct(shape, jnp.float32)


def call(kernel, outs, *args, limit=12, cost=(10**6, 10**6), **options):
    return pl.pallas_call(
        kernel,
        out_shape=outs,
        compiler_params=pltpu.CompilerParams(vmem_limit_bytes=limit << 20),
        cost_estimate=pl.CostEstimate(flops=cost[0], bytes_accessed=cost[1], transcendentals=0),
        **options,
    )(*args)


def step_of(data, centres, scales, factor, block_inv, iterate, residual, direction):
    dp, crow, ccol = lax.axis_size("dp"), lax.axis_size("crow"), lax.axis_size("ccol")
    held, order = block_inv.shape[0], block_inv.shape[1]
    width = factor.shape[0]
    rows, total = direction.shape
    assert factor.shape[1] == width and crow == ccol and crow in (4, 8) and dp % 2 == 0
    part = shaped(rows, width)
    last = crow - 1

    def spot(d, r, c):
        return (d * crow + r) * ccol + c

    def permute(value, target):
        perm = [
            (spot(d, r, c), spot(*target(d, r, c)))
            for d in range(dp)
            for r in range(crow)
            for c in range(ccol)
        ]
        return lax.ppermute(value, ("dp", "crow", "ccol"), perm)

    idle = [(r, c) for r in range(crow) for c in range(r + 1, ccol)]

    def move(value, *pairs, direct=False):
        to = dict(pairs)
        for (a, b), spare in zip(pairs, idle):
            if direct:
                to[b] = a
            else:
                to[b], to[spare] = spare, a
        return permute(value, lambda d, r, c: (d ^ 1, *to.get((r, c), (r, c))))

    def shifts(value, axis, flip=1):
        steps = range(1, lax.axis_size(axis))
        if axis == "crow":
            return [permute(value, lambda d, r, c: (d ^ flip, r ^ n, c)) for n in steps]
        return [permute(value, lambda d, r, c: (d ^ flip, r, c ^ n)) for n in steps]

    def with_tri(kernel, outs, *args, limit=12):
        full = [pl.BlockSpec(a.shape, lambda i, n=a.ndim: (0,) * n) for a in args]
        tri = [pl.BlockSpec((order, order), lambda i, r=r, c=c: (r, c)) for r, c in blocks_of(held)]
        return call(
            kernel, outs, *args, *([factor] * len(tri)), grid=(1,), in_specs=full + tri,
            out_specs=[pl.BlockSpec(out.shape, lambda i: (0, 0)) for out in outs], limit=limit,
        )

    (piece,) = with_tri(first_kernel, [part], direction, block_inv, limit=58)
    found = {last: piece}
    spots = len(blocks_of(held)) * order
    low, half, rest = with_tri(
        lower_kernel,
        [shaped(order, spots), shaped(order // 2, spots - order), shaped(order, order)],
        block_inv,
    )
    wide = jax.ShapeDtypeStruct((width, width), jnp.bfloat16)
    high_f, low_f = call(pair_kernel, [wide, wide], factor)
    turned_f = call(turn_factor_kernel, [wide, wide], factor)
    turned = call(turn_kernel, [wide, wide], low, block_inv)

    samples = data.shape[1]
    tile = order
    inputs = data.shape[0]
    kernel_shape = jax.ShapeDtypeStruct((width, samples), jnp.bfloat16)
    high_k, low_k = call(
        tile_kernel, [kernel_shape] * 2, scales, centres, data,
        grid=(width // tile,),
        in_specs=[
            pl.BlockSpec(memory_space=pltpu.SMEM),
            pl.BlockSpec((inputs, tile), lambda i: (0, i)),
            pl.BlockSpec((inputs, samples), lambda i: (0, 0)),
        ],
        out_specs=[pl.BlockSpec((tile, samples), lambda i: (i, 0))] * 2,
        scratch_shapes=[pltpu.VMEM((8 * inputs, samples), jnp.bfloat16)],
        limit=20,
    )

    def spread(cols, extra, got):
        return call(functools.partial(spread_kernel, cols), part, *extra, *got, high_f, low_f)

    sums = []
    for step in range(last, 0, -1):
        cols = list(range(step))[::-1]
        got = [move(piece, ((step, step), (step, c))) for c in cols]
        down = [((step, c), (step - 1, c)) for c in cols]
        if step == last:
            sub = move(spread(cols[:1], [], got[:1]), down[0])
            sums = [move(spread(cols[1:], [], got[1:]), *down[1:])]
        else:
            sub = move(spread(cols, sums, got), *down)
            sums = [sub]
        if step > 1:
            piece = call(solve_kernel, part, direction, sub, low, block_inv)
            found[step - 1] = piece
    places = [(n, n) for n in range(1, crow)]
    own = call(
        functools.partial(solve_pick_kernel, places), part, direction, sub, low, block_inv,
        *[found[n] for n in range(1, crow)],
    )

    parts = [own] + shifts(own, "crow")
    beside = [((n, n), (n, n - 1)) for n in range(1, crow)]
    half = move(half, *beside, direct=True)
    mine, images = call(image_kernel, [part, shaped(rows, samples)], *parts, high_k, low_k, limit=16)
    images = [images] + shifts(images, "ccol", 0)
    summed = call(normal_kernel, part, *images, high_k, low_k, limit=16)
    if dp == 2:
        summed = summed + permute(summed, lambda d, r, c: (d ^ 1, r, c))
    else:
        summed = lax.psum(summed, "dp")
    parts = [summed] + shifts(summed, "crow")
    rest = move(rest, *beside, direct=True)
    scale = 1.0 / (samples * dp * crow)
    source, image = call(
        functools.partial(source_kernel, scale, order), [part, part], mine, *parts, *turned
    )
    near = call(merge_kernel, [wide, wide], half, move(half), rest, block_inv)
    done = [image]
    places = [(0, 0)]
    side = []
    for step in range(1, crow):
        later = list(range(step + 1, crow))
        first = move(image, (places[-1], (step, step - 1)))
        if step == 1:
            source = move(source, *beside)
        if side:
            shift = [((at, step - 2), (at, step - 1)) for at in range(step, crow)]
            side = [move(side[0], *shift)]
        others = [move(image, (places[-1], (at, step - 1))) for at in later]
        image = call(
            functools.partial(fore_kernel, order, len(side)), part,
            *side, first, source, *turned_f, *near,
        )
        if later:
            side = [
                call(
                    functools.partial(side_kernel, later, len(side)), part, *side, *others, *turned_f
                )
            ]
        done.append(image)
        places.append((step, step - 1))
    own = call(functools.partial(pick_kernel, places), part, *done)
    own = call(sum_kernel, part, own, *shifts(own, "ccol"))
    full = shaped(rows, total)
    return tuple(
        call(
            final_kernel, [full, full, full], iterate, residual, direction, own, *shifts(own, "crow"),
            scratch_shapes=[pltpu.VMEM((rows, total), jnp.float32)],
        )
    )


def solution(mesh):
    placed = (
        P(None, ("dp", "crow")),
        P(None, "ccol"),
        P(),
        P("crow", "ccol"),
        P("crow", None, None),
        P(),
        P(),
        P(),
    )
    return jax.shard_map(
        step_of, mesh=mesh, in_specs=placed, out_specs=(P(), P(), P()), check_vma=False
    )
```

```python
import functools
import itertools
import math

import jax
import jax.numpy as jnp
from jax import lax
from jax.experimental import pallas as pl
from jax.experimental.pallas import tpu as pltpu
from jax.sharding import PartitionSpec as P


ridge_weight = 0.2
LOG2E = 1.0 / math.log(2.0)
NN = (((1,), (0,)), ((), ()))
NT = (((1,), (1,)), ((), ()))
TN = (((0,), (0,)), ((), ()))


def pair(value):
    high = value.astype(jnp.bfloat16)
    low = (value - high.astype(jnp.float32)).astype(jnp.bfloat16)
    return high, low


def stacked(value):
    high, low = pair(value)
    return jnp.concatenate([high, low], axis=0)


def fold(product, rows):
    return product[:rows] + product[rows:]


def times_pair(rows, high, low, dims):
    both = stacked(rows)
    out = lax.dot_general(both, high, dims, preferred_element_type=jnp.float32)
    out = out + lax.dot_general(both, low, dims, preferred_element_type=jnp.float32)
    return fold(out, rows.shape[0])


def times(rows, matrix, dims):
    high, low = pair(matrix)
    return times_pair(rows, high, low, dims)


def blocks_of(held):
    return [(r, c) for r in range(1, held) for c in range(r)]


def lower(low_ref, order, r, c):
    at = r * (r - 1) // 2 + c
    return low_ref[:, at * order : (at + 1) * order]


def square(one, other):
    first, first_low = pair(one)
    second, second_low = pair(other)
    out = lax.dot_general(first, second, NN, preferred_element_type=jnp.float32)
    out = out + lax.dot_general(first, second_low, NN, preferred_element_type=jnp.float32)
    return out + lax.dot_general(first_low, second, NN, preferred_element_type=jnp.float32)


def cut(ref, at, width):
    return ref[:, pl.ds(pl.multiple_of(at * width, width), width)]


def back_apply(target, low_ref, inv_ref):
    held, order = inv_ref.shape[0], inv_ref.shape[1]
    parts = [target[:, n * order : (n + 1) * order] for n in range(held)]
    pieces = []
    for c in range(held):
        piece = times(parts[c], inv_ref[c], NN)
        for r in range(c + 1, held):
            piece = piece + times(parts[r], lower(low_ref, order, r, c), NN)
        pieces.append(piece)
    return jnp.concatenate(pieces, axis=1)


def fore_apply(source, high_ref, low_ref, order):
    pieces = []
    for end in range(order, source.shape[1] + 1, order):
        block = (slice(0, end), slice(end - order, end))
        pieces.append(times_pair(source[:, :end], high_ref[block], low_ref[block], NN))
    return jnp.concatenate(pieces, axis=1)


def store_turned(low, inv_ref, high_out, low_out):
    held, order = inv_ref.shape[0], inv_ref.shape[1]
    for r in range(held):
        for c in range(r + 1):
            at = r * (r - 1) // 2 + c
            block = inv_ref[r] if r == c else low[:, at * order : (at + 1) * order]
            place = (slice(c * order, (c + 1) * order), slice(r * order, (r + 1) * order))
            high_out[place], low_out[place] = pair(block.T)


def turn_kernel(low_ref, inv_ref, high_out, low_out):
    store_turned(low_ref[...], inv_ref, high_out, low_out)


def turn_factor_kernel(factor_ref, high_out, low_out):
    high_out[...], low_out[...] = pair(factor_ref[...].T)


def first_kernel(direction_ref, inv_ref, *refs):
    tri_refs, out_ref = refs[:-1], refs[-1]
    held, order = inv_ref.shape[0], inv_ref.shape[1]
    width = held * order
    tri = dict(zip(blocks_of(held), tri_refs))
    target = cut(direction_ref, lax.axis_index("crow"), width)
    pieces = [None] * held
    for number in reversed(range(held)):
        part = target[:, number * order : (number + 1) * order]
        for later in range(number + 1, held):
            part = part - times(pieces[later], tri[later, number][...], NN)
        pieces[number] = times(part, inv_ref[number], NN)
    out_ref[...] = jnp.concatenate(pieces, axis=1)


def lower_kernel(inv_ref, *refs):
    tri_refs, (out_ref, half_ref, rest_ref) = refs[:-3], refs[-3:]
    held, order = inv_ref.shape[0], inv_ref.shape[1]
    tri = dict(zip(blocks_of(held), tri_refs))
    found = {(n, n): inv_ref[n] for n in range(held)}
    for r in range(1, held):
        for c in range(r):
            total = square(tri[r, c][...], found[c, c])
            for between in range(c + 1, r):
                total = total + square(tri[r, between][...], found[between, c])
            found[r, c] = -square(inv_ref[r], total)
            at = r * (r - 1) // 2 + c
            out_ref[:, at * order : (at + 1) * order] = found[r, c]
    tall = half_ref.shape[0]
    at = lax.rem(lax.axis_index("dp"), 2) * tall
    split = half_ref.shape[1]
    half_ref[...] = out_ref[pl.ds(pl.multiple_of(at, tall), tall), :split]
    rest_ref[...] = out_ref[:, split:]


def pair_kernel(factor_ref, high_ref, low_ref):
    high, low = pair(factor_ref[...])
    high_ref[...] = high
    low_ref[...] = low


def spread_kernel(cols, *refs):
    extra = refs[: len(refs) - 3 - len(cols)]
    got_refs = refs[len(extra) : len(extra) + len(cols)]
    high_ref, low_ref, out_ref = refs[-3:]
    col = lax.axis_index("ccol")
    piece = got_refs[0][...]
    for at, got in zip(cols[1:], got_refs[1:]):
        piece = jnp.where(col == at, got[...], piece)
    out = times_pair(piece, high_ref[...], low_ref[...], NN)
    for ref in extra:
        out = out + ref[...]
    out_ref[...] = out


def merge_kernel(mine_ref, other_ref, rest_ref, inv_ref, high_out, low_out):
    odd = lax.rem(lax.axis_index("dp"), 2) == 1
    mine, other = mine_ref[...], other_ref[...]
    low = jnp.concatenate([jnp.where(odd, mine, other), jnp.where(odd, other, mine)], axis=0)
    low = jnp.concatenate([low, rest_ref[...]], axis=1)
    store_turned(low, inv_ref, high_out, low_out)


def solve_kernel(direction_ref, sub_ref, low_ref, inv_ref, out_ref):
    width = sub_ref.shape[1]
    target = cut(direction_ref, lax.axis_index("crow"), width) - sub_ref[...]
    out_ref[...] = back_apply(target, low_ref, inv_ref)


def pick_kernel(places, *refs):
    row, col = lax.axis_index("crow"), lax.axis_index("ccol")
    out = jnp.zeros_like(refs[0][...])
    for (r, c), ref in zip(places, refs[:-1]):
        out = jnp.where((row == r) & (col == c), ref[...], out)
    refs[-1][...] = out


def solve_pick_kernel(places, direction_ref, sub_ref, low_ref, inv_ref, *refs):
    width = sub_ref.shape[1]
    row, col = lax.axis_index("crow"), lax.axis_index("ccol")
    target = cut(direction_ref, row, width) - sub_ref[...]
    out = jnp.where((row == 0) & (col == 0), back_apply(target, low_ref, inv_ref), 0.0)
    for (r, c), ref in zip(places, refs[:-1]):
        out = jnp.where((row == r) & (col == c), ref[...], out)
    refs[-1][...] = out


def triple(value):
    high, middle = pair(value)
    rest = value - high.astype(jnp.float32) - middle.astype(jnp.float32)
    return high, middle, rest.astype(jnp.bfloat16)


def norm_rows(norm, inputs):
    row = lax.broadcasted_iota(jnp.int32, (inputs, norm.shape[1]), 0)
    wide = jnp.broadcast_to(norm, (inputs, norm.shape[1]))
    high, middle, low = (part.astype(jnp.float32) for part in triple(wide))
    rows = jnp.where(row == 0, high, jnp.where(row == 1, middle, jnp.where(row == 2, low, 0.0)))
    return rows.astype(jnp.bfloat16)


def ones_rows(norm, inputs):
    row = lax.broadcasted_iota(jnp.int32, (inputs, norm.shape[1]), 0)
    return jnp.where(row < 3, 1.0, 0.0).astype(jnp.bfloat16)


def scale_by(value, scales_ref):
    inputs = value.shape[0]
    row = lax.broadcasted_iota(jnp.int32, value.shape, 0)
    scales = jnp.full(value.shape, scales_ref[0], jnp.float32)
    for n in range(1, inputs):
        scales = jnp.where(row == n, scales_ref[n], scales)
    return value / scales


def tile_kernel(scales_ref, centres_ref, data_ref, high_ref, low_ref, right):
    inputs = data_ref.shape[0]

    @pl.when(pl.program_id(0) == 0)
    def _():
        scaled = scale_by(data_ref[...], scales_ref)
        norm = jnp.sum(scaled * scaled, axis=0, keepdims=True) * (-0.5 * LOG2E)
        high, middle, low = triple(scaled)
        right[...] = jnp.concatenate(
            [high, middle, high, middle, low, high, norm_rows(norm, inputs), ones_rows(norm, inputs)],
            axis=0,
        )

    scaled = scale_by(centres_ref[...], scales_ref)
    norm = jnp.sum(scaled * scaled, axis=0, keepdims=True) * (-0.5 * LOG2E)
    high, middle, low = triple(scaled * LOG2E)
    left = jnp.concatenate(
        [high, high, middle, middle, high, low, ones_rows(norm, inputs), norm_rows(norm, inputs)], axis=0
    )
    exponent = lax.dot_general(left, right[...], TN, preferred_element_type=jnp.float32)
    high, low = pair(jnp.exp2(exponent))
    high_ref[...] = high
    low_ref[...] = low


def image_kernel(*refs):
    part_refs = refs[:-4]
    high_ref, low_ref, mine_ref, out_ref = refs[-4:]
    piece = part_refs[0][...]
    for ref in part_refs[1:]:
        piece = piece + ref[...]
    mine_ref[...] = piece
    out_ref[...] = times_pair(piece, high_ref[...], low_ref[...], NN)


def normal_kernel(*refs):
    part_refs = refs[:-3]
    high_ref, low_ref, out_ref = refs[-3:]
    piece = part_refs[0][...]
    for ref in part_refs[1:]:
        piece = piece + ref[...]
    both = stacked(piece)
    out = lax.dot_general(high_ref[...], both, NT, preferred_element_type=jnp.float32)
    out = out + lax.dot_general(low_ref[...], both, NT, preferred_element_type=jnp.float32)
    out_ref[...] = fold(out.T, piece.shape[0])


def source_kernel(scale, order, mine_ref, *refs):
    part_refs = refs[:-4]
    high_ref, low_ref, out_ref, image_ref = refs[-4:]
    total = part_refs[0][...]
    for ref in part_refs[1:]:
        total = total + ref[...]
    normal = total * scale + ridge_weight * mine_ref[...]
    out_ref[...] = normal
    image_ref[...] = fore_apply(normal, high_ref, low_ref, order)


def fore_kernel(order, sides, *refs):
    side_refs = refs[:sides]
    got_ref, source_ref, fh_ref, fl_ref, high_ref, low_ref, image_out = refs[sides:]
    left = source_ref[...] - times_pair(got_ref[...], fh_ref[...], fl_ref[...], NN)
    for ref in side_refs:
        left = left - ref[...]
    image_out[...] = fore_apply(left, high_ref, low_ref, order)


def side_kernel(rows, sides, *refs):
    side_refs = refs[:sides]
    got_refs = refs[sides : sides + len(rows)]
    fh_ref, fl_ref, side_out = refs[sides + len(rows) :]
    row = lax.axis_index("crow")
    piece = got_refs[0][...]
    for at, ref in zip(rows[1:], got_refs[1:]):
        piece = jnp.where(row == at, ref[...], piece)
    side = times_pair(piece, fh_ref[...], fl_ref[...], NN)
    for ref in side_refs:
        side = side + ref[...]
    side_out[...] = side


def sum_kernel(*refs):
    total = refs[0][...]
    for ref in refs[1:-1]:
        total = total + ref[...]
    refs[-1][...] = total


def final_kernel(iterate_ref, residual_ref, direction_ref, *refs):
    part_refs = refs[:-4]
    iterate_out, residual_out, direction_out, image_ref = refs[-4:]
    width = part_refs[0].shape[1]
    row = lax.axis_index("crow")
    for step, ref in enumerate(part_refs):
        at = row ^ step
        image_ref[:, pl.ds(pl.multiple_of(at * width, width), width)] = ref[...]
    residual = residual_ref[...]
    direction = direction_ref[...]
    image = image_ref[...]
    gamma = jnp.sum(residual * residual, axis=1, keepdims=True)
    curvature = jnp.sum(direction * image, axis=1, keepdims=True)
    alpha = gamma / curvature
    iterate_out[...] = iterate_ref[...] + alpha * direction
    new_residual = residual - alpha * image
    residual_out[...] = new_residual
    gamma_next = jnp.sum(new_residual * new_residual, axis=1, keepdims=True)
    direction_out[...] = new_residual + (gamma_next / gamma) * direction


def shaped(*shape):
    return jax.ShapeDtypeStruct(shape, jnp.float32)


def call(kernel, outs, *args, limit=12, cost=(10**6, 10**6), **options):
    return pl.pallas_call(
        kernel,
        out_shape=outs,
        compiler_params=pltpu.CompilerParams(vmem_limit_bytes=limit << 20),
        cost_estimate=pl.CostEstimate(flops=cost[0], bytes_accessed=cost[1], transcendentals=0),
        **options,
    )(*args)


def step_of(data, centres, scales, factor, block_inv, iterate, residual, direction):
    dp, crow, ccol = lax.axis_size("dp"), lax.axis_size("crow"), lax.axis_size("ccol")
    held, order = block_inv.shape[0], block_inv.shape[1]
    width = factor.shape[0]
    rows, total = direction.shape
    assert factor.shape[1] == width and crow == ccol and crow in (4, 8) and dp % 2 == 0
    part = shaped(rows, width)
    last = crow - 1

    def spot(d, r, c):
        return (d * crow + r) * ccol + c

    def permute(value, target):
        perm = [
            (spot(d, r, c), spot(*target(d, r, c)))
            for d in range(dp)
            for r in range(crow)
            for c in range(ccol)
        ]
        return lax.ppermute(value, ("dp", "crow", "ccol"), perm)

    idle = itertools.cycle([(r, c) for r in range(crow) for c in range(r + 1, ccol)])

    def move(value, *pairs, direct=False):
        to = dict(pairs)
        for a, b in pairs:
            if direct:
                to[b] = a
            else:
                spare = next(idle)
                to[b], to[spare] = spare, a
        return permute(value, lambda d, r, c: (d ^ 1, *to.get((r, c), (r, c))))

    def shifts(value, axis, flip=1):
        steps = range(1, lax.axis_size(axis))
        if axis == "crow":
            return [permute(value, lambda d, r, c: (d ^ flip, r ^ n, c)) for n in steps]
        return [permute(value, lambda d, r, c: (d ^ flip, r, c ^ n)) for n in steps]

    def with_tri(kernel, outs, *args, limit=12):
        full = [pl.BlockSpec(a.shape, lambda i, n=a.ndim: (0,) * n) for a in args]
        tri = [pl.BlockSpec((order, order), lambda i, r=r, c=c: (r, c)) for r, c in blocks_of(held)]
        return call(
            kernel, outs, *args, *([factor] * len(tri)), grid=(1,), in_specs=full + tri,
            out_specs=[pl.BlockSpec(out.shape, lambda i: (0, 0)) for out in outs], limit=limit,
        )

    (piece,) = with_tri(first_kernel, [part], direction, block_inv, limit=58)
    found = {last: piece}
    spots = len(blocks_of(held)) * order
    low, half, rest = with_tri(
        lower_kernel,
        [shaped(order, spots), shaped(order // 2, spots - order), shaped(order, order)],
        block_inv,
    )
    wide = jax.ShapeDtypeStruct((width, width), jnp.bfloat16)
    high_f, low_f = call(pair_kernel, [wide, wide], factor)
    turned_f = call(turn_factor_kernel, [wide, wide], factor)
    turned = call(turn_kernel, [wide, wide], low, block_inv)

    samples = data.shape[1]
    tile = order
    inputs = data.shape[0]
    kernel_shape = jax.ShapeDtypeStruct((width, samples), jnp.bfloat16)
    high_k, low_k = call(
        tile_kernel, [kernel_shape] * 2, scales, centres, data,
        grid=(width // tile,),
        in_specs=[
            pl.BlockSpec(memory_space=pltpu.SMEM),
            pl.BlockSpec((inputs, tile), lambda i: (0, i)),
            pl.BlockSpec((inputs, samples), lambda i: (0, 0)),
        ],
        out_specs=[pl.BlockSpec((tile, samples), lambda i: (i, 0))] * 2,
        scratch_shapes=[pltpu.VMEM((8 * inputs, samples), jnp.bfloat16)],
        limit=20,
    )

    def spread(cols, extra, got):
        return call(functools.partial(spread_kernel, cols), part, *extra, *got, high_f, low_f)

    sums = []
    for step in range(last, 0, -1):
        cols = list(range(step))[::-1]
        got = [move(piece, ((step, step), (step, c))) for c in cols]
        down = [((step, c), (step - 1, c)) for c in cols]
        if step == last:
            sub = move(spread(cols[:1], [], got[:1]), down[0])
            sums = [move(spread(cols[1:], [], got[1:]), *down[1:])]
        else:
            sub = move(spread(cols, sums, got), *down)
            sums = [sub]
        if step > 1:
            piece = call(solve_kernel, part, direction, sub, low, block_inv)
            found[step - 1] = piece
    places = [(n, n) for n in range(1, crow)]
    own = call(
        functools.partial(solve_pick_kernel, places), part, direction, sub, low, block_inv,
        *[found[n] for n in range(1, crow)],
    )

    parts = [own] + shifts(own, "crow")
    beside = [((n, n), (n, n - 1)) for n in range(1, crow)]
    half = move(half, *beside, direct=True)
    mine, images = call(image_kernel, [part, shaped(rows, samples)], *parts, high_k, low_k, limit=16)
    images = [images] + shifts(images, "ccol", 0)
    summed = call(normal_kernel, part, *images, high_k, low_k, limit=16)
    if dp == 2:
        summed = summed + permute(summed, lambda d, r, c: (d ^ 1, r, c))
    else:
        summed = lax.psum(summed, "dp")
    parts = [summed] + shifts(summed, "crow")
    rest = move(rest, *beside, direct=True)
    scale = 1.0 / (samples * dp * crow)
    source, image = call(
        functools.partial(source_kernel, scale, order), [part, part], mine, *parts, *turned
    )
    near = call(merge_kernel, [wide, wide], half, move(half), rest, block_inv)
    done = [image]
    places = [(0, 0)]
    side = []
    for step in range(1, crow):
        later = list(range(step + 1, crow))
        first = move(image, (places[-1], (step, step - 1)))
        if step == 1:
            source = move(source, *beside)
        if side:
            shift = [((at, step - 2), (at, step - 1)) for at in range(step, crow)]
            side = [move(side[0], *shift)]
        others = [move(image, (places[-1], (at, step - 1))) for at in later]
        image = call(
            functools.partial(fore_kernel, order, len(side)), part,
            *side, first, source, *turned_f, *near,
        )
        if later:
            side = [
                call(
                    functools.partial(side_kernel, later, len(side)), part, *side, *others, *turned_f
                )
            ]
        done.append(image)
        places.append((step, step - 1))
    own = call(functools.partial(pick_kernel, places), part, *done)
    own = call(sum_kernel, part, own, *shifts(own, "ccol"))
    full = shaped(rows, total)
    return tuple(
        call(
            final_kernel, [full, full, full], iterate, residual, direction, own, *shifts(own, "crow"),
            scratch_shapes=[pltpu.VMEM((rows, total), jnp.float32)],
        )
    )


def solution(mesh):
    placed = (
        P(None, ("dp", "crow")),
        P(None, "ccol"),
        P(),
        P("crow", "ccol"),
        P("crow", None, None),
        P(),
        P(),
        P(),
    )
    return jax.shard_map(
        step_of, mesh=mesh, in_specs=placed, out_specs=(P(), P(), P()), check_vma=False
    )
```

```python
import collections
import functools
import math

import jax
import jax.numpy as jnp
from jax import lax
from jax.experimental import pallas as pl
from jax.experimental.pallas import tpu as pltpu
from jax.sharding import PartitionSpec as P


ridge_weight = 0.2
LOG2E = 1.0 / math.log(2.0)
NN = (((1,), (0,)), ((), ()))
NT = (((1,), (1,)), ((), ()))
TN = (((0,), (0,)), ((), ()))


def pair(value):
    high = value.astype(jnp.bfloat16)
    low = (value - high.astype(jnp.float32)).astype(jnp.bfloat16)
    return high, low


def stacked(value):
    high, low = pair(value)
    return jnp.concatenate([high, low], axis=0)


def fold(product, rows):
    return product[:rows] + product[rows:]


def times_pair(rows, high, low, dims):
    both = stacked(rows)
    out = lax.dot_general(both, high, dims, preferred_element_type=jnp.float32)
    out = out + lax.dot_general(both, low, dims, preferred_element_type=jnp.float32)
    return fold(out, rows.shape[0])


def times(rows, matrix, dims):
    high, low = pair(matrix)
    return times_pair(rows, high, low, dims)


def blocks_of(held):
    return [(r, c) for r in range(1, held) for c in range(r)]


def lower(low_ref, order, r, c):
    at = r * (r - 1) // 2 + c
    return low_ref[:, at * order : (at + 1) * order]


def square(one, other):
    first, first_low = pair(one)
    second, second_low = pair(other)
    out = lax.dot_general(first, second, NN, preferred_element_type=jnp.float32)
    out = out + lax.dot_general(first, second_low, NN, preferred_element_type=jnp.float32)
    return out + lax.dot_general(first_low, second, NN, preferred_element_type=jnp.float32)


def cut(ref, at, width):
    return ref[:, pl.ds(pl.multiple_of(at * width, width), width)]


def back_apply(target, low_ref, inv_ref):
    held, order = inv_ref.shape[0], inv_ref.shape[1]
    parts = [target[:, n * order : (n + 1) * order] for n in range(held)]
    pieces = []
    for c in range(held):
        piece = times(parts[c], inv_ref[c], NN)
        for r in range(c + 1, held):
            piece = piece + times(parts[r], lower(low_ref, order, r, c), NN)
        pieces.append(piece)
    return jnp.concatenate(pieces, axis=1)


def fore_apply(source, high_ref, low_ref, order):
    pieces = []
    for end in range(order, source.shape[1] + 1, order):
        block = (slice(0, end), slice(end - order, end))
        pieces.append(times_pair(source[:, :end], high_ref[block], low_ref[block], NN))
    return jnp.concatenate(pieces, axis=1)


def store_turned(low, inv_ref, high_out, low_out):
    held, order = inv_ref.shape[0], inv_ref.shape[1]
    for r in range(held):
        for c in range(r + 1):
            at = r * (r - 1) // 2 + c
            block = inv_ref[r] if r == c else low[:, at * order : (at + 1) * order]
            place = (slice(c * order, (c + 1) * order), slice(r * order, (r + 1) * order))
            high_out[place], low_out[place] = pair(block.T)


def turn_kernel(low_ref, inv_ref, high_out, low_out):
    store_turned(low_ref[...], inv_ref, high_out, low_out)


def turn_factor_kernel(factor_ref, high_out, low_out):
    high_out[...], low_out[...] = pair(factor_ref[...].T)


def first_kernel(direction_ref, inv_ref, *refs):
    tri_refs, out_ref = refs[:-1], refs[-1]
    held, order = inv_ref.shape[0], inv_ref.shape[1]
    width = held * order
    tri = dict(zip(blocks_of(held), tri_refs))
    target = cut(direction_ref, lax.axis_index("crow"), width)
    pieces = [None] * held
    for number in reversed(range(held)):
        part = target[:, number * order : (number + 1) * order]
        for later in range(number + 1, held):
            part = part - times(pieces[later], tri[later, number][...], NN)
        pieces[number] = times(part, inv_ref[number], NN)
    out_ref[...] = jnp.concatenate(pieces, axis=1)


def lower_kernel(inv_ref, *refs):
    tri_refs, (out_ref, half_ref, rest_ref) = refs[:-3], refs[-3:]
    held, order = inv_ref.shape[0], inv_ref.shape[1]
    tri = dict(zip(blocks_of(held), tri_refs))
    found = {(n, n): inv_ref[n] for n in range(held)}
    for r in range(1, held):
        for c in range(r):
            total = square(tri[r, c][...], found[c, c])
            for between in range(c + 1, r):
                total = total + square(tri[r, between][...], found[between, c])
            found[r, c] = -square(inv_ref[r], total)
            at = r * (r - 1) // 2 + c
            out_ref[:, at * order : (at + 1) * order] = found[r, c]
    tall = half_ref.shape[0]
    at = lax.rem(lax.axis_index("dp"), 2) * tall
    split = half_ref.shape[1]
    half_ref[...] = out_ref[pl.ds(pl.multiple_of(at, tall), tall), :split]
    rest_ref[...] = out_ref[:, split:]


def pair_kernel(factor_ref, high_ref, low_ref):
    high, low = pair(factor_ref[...])
    high_ref[...] = high
    low_ref[...] = low


def spread_kernel(cols, *refs):
    extra = refs[: len(refs) - 3 - len(cols)]
    got_refs = refs[len(extra) : len(extra) + len(cols)]
    high_ref, low_ref, out_ref = refs[-3:]
    col = lax.axis_index("ccol")
    piece = got_refs[0][...]
    for at, got in zip(cols[1:], got_refs[1:]):
        piece = jnp.where(col == at, got[...], piece)
    out = times_pair(piece, high_ref[...], low_ref[...], NN)
    for ref in extra:
        out = out + ref[...]
    out_ref[...] = out


def merge_kernel(mine_ref, other_ref, rest_ref, inv_ref, high_out, low_out):
    odd = lax.rem(lax.axis_index("dp"), 2) == 1
    mine, other = mine_ref[...], other_ref[...]
    low = jnp.concatenate([jnp.where(odd, mine, other), jnp.where(odd, other, mine)], axis=0)
    low = jnp.concatenate([low, rest_ref[...]], axis=1)
    store_turned(low, inv_ref, high_out, low_out)


def solve_kernel(direction_ref, sub_ref, low_ref, inv_ref, out_ref):
    width = sub_ref.shape[1]
    target = cut(direction_ref, lax.axis_index("crow"), width) - sub_ref[...]
    out_ref[...] = back_apply(target, low_ref, inv_ref)


def pick_kernel(places, *refs):
    row, col = lax.axis_index("crow"), lax.axis_index("ccol")
    out = jnp.zeros_like(refs[0][...])
    for (r, c), ref in zip(places, refs[:-1]):
        out = jnp.where((row == r) & (col == c), ref[...], out)
    refs[-1][...] = out


def solve_pick_kernel(places, direction_ref, sub_ref, low_ref, inv_ref, *refs):
    width = sub_ref.shape[1]
    row, col = lax.axis_index("crow"), lax.axis_index("ccol")
    target = cut(direction_ref, row, width) - sub_ref[...]
    out = jnp.where((row == 0) & (col == 0), back_apply(target, low_ref, inv_ref), 0.0)
    for (r, c), ref in zip(places, refs[:-1]):
        out = jnp.where((row == r) & (col == c), ref[...], out)
    refs[-1][...] = out


def triple(value):
    high, middle = pair(value)
    rest = value - high.astype(jnp.float32) - middle.astype(jnp.float32)
    return high, middle, rest.astype(jnp.bfloat16)


def norm_rows(norm, inputs):
    row = lax.broadcasted_iota(jnp.int32, (inputs, norm.shape[1]), 0)
    wide = jnp.broadcast_to(norm, (inputs, norm.shape[1]))
    high, middle, low = (part.astype(jnp.float32) for part in triple(wide))
    rows = jnp.where(row == 0, high, jnp.where(row == 1, middle, jnp.where(row == 2, low, 0.0)))
    return rows.astype(jnp.bfloat16)


def ones_rows(norm, inputs):
    row = lax.broadcasted_iota(jnp.int32, (inputs, norm.shape[1]), 0)
    return jnp.where(row < 3, 1.0, 0.0).astype(jnp.bfloat16)


def scale_by(value, scales_ref):
    inputs = value.shape[0]
    row = lax.broadcasted_iota(jnp.int32, value.shape, 0)
    scales = jnp.full(value.shape, scales_ref[0], jnp.float32)
    for n in range(1, inputs):
        scales = jnp.where(row == n, scales_ref[n], scales)
    return value / scales


def tile_kernel(scales_ref, centres_ref, data_ref, high_ref, low_ref, right):
    inputs = data_ref.shape[0]

    @pl.when(pl.program_id(0) == 0)
    def _():
        scaled = scale_by(data_ref[...], scales_ref)
        norm = jnp.sum(scaled * scaled, axis=0, keepdims=True) * (-0.5 * LOG2E)
        high, middle, low = triple(scaled)
        right[...] = jnp.concatenate(
            [high, middle, high, middle, low, high, norm_rows(norm, inputs), ones_rows(norm, inputs)],
            axis=0,
        )

    scaled = scale_by(centres_ref[...], scales_ref)
    norm = jnp.sum(scaled * scaled, axis=0, keepdims=True) * (-0.5 * LOG2E)
    high, middle, low = triple(scaled * LOG2E)
    left = jnp.concatenate(
        [high, high, middle, middle, high, low, ones_rows(norm, inputs), norm_rows(norm, inputs)], axis=0
    )
    exponent = lax.dot_general(left, right[...], TN, preferred_element_type=jnp.float32)
    high, low = pair(jnp.exp2(exponent))
    high_ref[...] = high
    low_ref[...] = low


def image_kernel(*refs):
    part_refs = refs[:-4]
    high_ref, low_ref, mine_ref, out_ref = refs[-4:]
    piece = part_refs[0][...]
    for ref in part_refs[1:]:
        piece = piece + ref[...]
    mine_ref[...] = piece
    out_ref[...] = times_pair(piece, high_ref[...], low_ref[...], NN)


def normal_kernel(*refs):
    part_refs = refs[:-3]
    high_ref, low_ref, out_ref = refs[-3:]
    piece = part_refs[0][...]
    for ref in part_refs[1:]:
        piece = piece + ref[...]
    both = stacked(piece)
    out = lax.dot_general(high_ref[...], both, NT, preferred_element_type=jnp.float32)
    out = out + lax.dot_general(low_ref[...], both, NT, preferred_element_type=jnp.float32)
    out_ref[...] = fold(out.T, piece.shape[0])


def source_kernel(scale, order, mine_ref, *refs):
    part_refs = refs[:-4]
    high_ref, low_ref, out_ref, image_ref = refs[-4:]
    total = part_refs[0][...]
    for ref in part_refs[1:]:
        total = total + ref[...]
    normal = total * scale + ridge_weight * mine_ref[...]
    out_ref[...] = normal
    image_ref[...] = fore_apply(normal, high_ref, low_ref, order)


def fore_kernel(order, sides, *refs):
    side_refs = refs[:sides]
    got_ref, source_ref, fh_ref, fl_ref, high_ref, low_ref, image_out = refs[sides:]
    left = source_ref[...] - times_pair(got_ref[...], fh_ref[...], fl_ref[...], NN)
    for ref in side_refs:
        left = left - ref[...]
    image_out[...] = fore_apply(left, high_ref, low_ref, order)


def side_kernel(rows, sides, *refs):
    side_refs = refs[:sides]
    got_refs = refs[sides : sides + len(rows)]
    fh_ref, fl_ref, side_out = refs[sides + len(rows) :]
    row = lax.axis_index("crow")
    piece = got_refs[0][...]
    for at, ref in zip(rows[1:], got_refs[1:]):
        piece = jnp.where(row == at, ref[...], piece)
    side = times_pair(piece, fh_ref[...], fl_ref[...], NN)
    for ref in side_refs:
        side = side + ref[...]
    side_out[...] = side


def sum_kernel(*refs):
    total = refs[0][...]
    for ref in refs[1:-1]:
        total = total + ref[...]
    refs[-1][...] = total


def final_kernel(iterate_ref, residual_ref, direction_ref, *refs):
    part_refs = refs[:-4]
    iterate_out, residual_out, direction_out, image_ref = refs[-4:]
    width = part_refs[0].shape[1]
    row = lax.axis_index("crow")
    for step, ref in enumerate(part_refs):
        at = row ^ step
        image_ref[:, pl.ds(pl.multiple_of(at * width, width), width)] = ref[...]
    residual = residual_ref[...]
    direction = direction_ref[...]
    image = image_ref[...]
    gamma = jnp.sum(residual * residual, axis=1, keepdims=True)
    curvature = jnp.sum(direction * image, axis=1, keepdims=True)
    alpha = gamma / curvature
    iterate_out[...] = iterate_ref[...] + alpha * direction
    new_residual = residual - alpha * image
    residual_out[...] = new_residual
    gamma_next = jnp.sum(new_residual * new_residual, axis=1, keepdims=True)
    direction_out[...] = new_residual + (gamma_next / gamma) * direction


def shaped(*shape):
    return jax.ShapeDtypeStruct(shape, jnp.float32)


def call(kernel, outs, *args, limit=12, cost=(10**6, 10**6), **options):
    return pl.pallas_call(
        kernel,
        out_shape=outs,
        compiler_params=pltpu.CompilerParams(vmem_limit_bytes=limit << 20),
        cost_estimate=pl.CostEstimate(flops=cost[0], bytes_accessed=cost[1], transcendentals=0),
        **options,
    )(*args)


def step_of(data, centres, scales, factor, block_inv, iterate, residual, direction):
    dp, crow, ccol = lax.axis_size("dp"), lax.axis_size("crow"), lax.axis_size("ccol")
    held, order = block_inv.shape[0], block_inv.shape[1]
    width = factor.shape[0]
    rows, total = direction.shape
    assert factor.shape[1] == width and crow == ccol and crow in (4, 8) and dp % 2 == 0
    part = shaped(rows, width)
    last = crow - 1

    def spot(d, r, c):
        return (d * crow + r) * ccol + c

    def permute(value, target):
        perm = [
            (spot(d, r, c), spot(*target(d, r, c)))
            for d in range(dp)
            for r in range(crow)
            for c in range(ccol)
        ]
        return lax.ppermute(value, ("dp", "crow", "ccol"), perm)

    recent = collections.deque(maxlen=4)
    cells = [(r, c) for r in range(crow) for c in range(ccol)]

    def hops(a, b):
        return (a[0] ^ b[0]).bit_count() + abs(a[1] - b[1])

    def move(value, *pairs, idle=None):
        to, taken = {}, {cell for two in pairs for cell in two}
        for a, b in pairs:
            free = [cell for cell in cells if idle and idle(*cell) and cell not in taken]
            if free:
                spare = min(free, key=lambda cell: (cell in recent, hops(a, cell), hops(b, cell)))
                taken.add(spare)
                recent.append(spare)
                to[a], to[b], to[spare] = b, spare, a
            else:
                to[a], to[b] = b, a
        return permute(value, lambda d, r, c: (d ^ 1, *to.get((r, c), (r, c))))

    def shifts(value, axis, flip=1):
        steps = range(1, lax.axis_size(axis))
        if axis == "crow":
            return [permute(value, lambda d, r, c: (d ^ flip, r ^ n, c)) for n in steps]
        return [permute(value, lambda d, r, c: (d ^ flip, r, c ^ n)) for n in steps]

    def with_tri(kernel, outs, *args, limit=12):
        full = [pl.BlockSpec(a.shape, lambda i, n=a.ndim: (0,) * n) for a in args]
        tri = [pl.BlockSpec((order, order), lambda i, r=r, c=c: (r, c)) for r, c in blocks_of(held)]
        return call(
            kernel, outs, *args, *([factor] * len(tri)), grid=(1,), in_specs=full + tri,
            out_specs=[pl.BlockSpec(out.shape, lambda i: (0, 0)) for out in outs], limit=limit,
        )

    (piece,) = with_tri(first_kernel, [part], direction, block_inv, limit=58)
    found = {last: piece}
    spots = len(blocks_of(held)) * order
    low, half, rest = with_tri(
        lower_kernel,
        [shaped(order, spots), shaped(order // 2, spots - order), shaped(order, order)],
        block_inv,
    )
    wide = jax.ShapeDtypeStruct((width, width), jnp.bfloat16)
    high_f, low_f = call(pair_kernel, [wide, wide], factor)
    turned_f = call(turn_factor_kernel, [wide, wide], factor)
    turned = call(turn_kernel, [wide, wide], low, block_inv)

    samples = data.shape[1]
    tile = order
    inputs = data.shape[0]
    kernel_shape = jax.ShapeDtypeStruct((width, samples), jnp.bfloat16)
    high_k, low_k = call(
        tile_kernel, [kernel_shape] * 2, scales, centres, data,
        grid=(width // tile,),
        in_specs=[
            pl.BlockSpec(memory_space=pltpu.SMEM),
            pl.BlockSpec((inputs, tile), lambda i: (0, i)),
            pl.BlockSpec((inputs, samples), lambda i: (0, 0)),
        ],
        out_specs=[pl.BlockSpec((tile, samples), lambda i: (i, 0))] * 2,
        scratch_shapes=[pltpu.VMEM((8 * inputs, samples), jnp.bfloat16)],
        limit=20,
    )

    def spread(cols, extra, got):
        return call(functools.partial(spread_kernel, cols), part, *extra, *got, high_f, low_f)

    sums = []
    for step in range(last, 0, -1):
        cols = list(range(step))[::-1]
        idle = lambda r, c, step=step: c > r or r > step
        got = [move(piece, ((step, step), (step, c)), idle=idle) for c in cols]
        down = [((step, c), (step - 1, c)) for c in cols]
        if step == last:
            sub = move(spread(cols[:1], [], got[:1]), down[0], idle=idle)
            sums = [move(spread(cols[1:], [], got[1:]), *down[1:], idle=idle)]
        else:
            sub = move(spread(cols, sums, got), *down, idle=idle)
            sums = [sub]
        if step > 1:
            piece = call(solve_kernel, part, direction, sub, low, block_inv)
            found[step - 1] = piece
    places = [(n, n) for n in range(1, crow)]
    own = call(
        functools.partial(solve_pick_kernel, places), part, direction, sub, low, block_inv,
        *[found[n] for n in range(1, crow)],
    )

    parts = [own] + shifts(own, "crow")
    beside = [((n, n), (n, n - 1)) for n in range(1, crow)]
    half = move(half, *beside)
    mine, images = call(image_kernel, [part, shaped(rows, samples)], *parts, high_k, low_k, limit=16)
    images = [images] + shifts(images, "ccol", 0)
    summed = call(normal_kernel, part, *images, high_k, low_k, limit=16)
    if dp == 2:
        summed = summed + permute(summed, lambda d, r, c: (d ^ 1, r, c))
    else:
        summed = lax.psum(summed, "dp")
    parts = [summed] + shifts(summed, "crow")
    rest = move(rest, *beside)
    scale = 1.0 / (samples * dp * crow)
    source, image = call(
        functools.partial(source_kernel, scale, order), [part, part], mine, *parts, *turned
    )
    near = call(merge_kernel, [wide, wide], half, move(half), rest, block_inv)
    done = [image]
    places = [(0, 0)]
    side = []
    for step in range(1, crow):
        later = list(range(step + 1, crow))
        idle = lambda r, c, step=step: step > 1 and (c >= r or r < step - 1)
        first = move(image, (places[-1], (step, step - 1)), idle=idle)
        if step == 1:
            source = move(source, *beside)
        if side:
            shift = [((at, step - 2), (at, step - 1)) for at in range(step, crow)]
            side = [move(side[0], *shift, idle=idle)]
        others = [move(image, (places[-1], (at, step - 1)), idle=idle) for at in later]
        image = call(
            functools.partial(fore_kernel, order, len(side)), part,
            *side, first, source, *turned_f, *near,
        )
        if later:
            side = [
                call(
                    functools.partial(side_kernel, later, len(side)), part, *side, *others, *turned_f
                )
            ]
        done.append(image)
        places.append((step, step - 1))
    own = call(functools.partial(pick_kernel, places), part, *done)
    own = call(sum_kernel, part, own, *shifts(own, "ccol"))
    full = shaped(rows, total)
    return tuple(
        call(
            final_kernel, [full, full, full], iterate, residual, direction, own, *shifts(own, "crow"),
            scratch_shapes=[pltpu.VMEM((rows, total), jnp.float32)],
        )
    )


def solution(mesh):
    placed = (
        P(None, ("dp", "crow")),
        P(None, "ccol"),
        P(),
        P("crow", "ccol"),
        P("crow", None, None),
        P(),
        P(),
        P(),
    )
    return jax.shard_map(
        step_of, mesh=mesh, in_specs=placed, out_specs=(P(), P(), P()), check_vma=False
    )
```

```python
import collections
import functools
import math

import jax
import jax.numpy as jnp
from jax import lax
from jax.experimental import pallas as pl
from jax.experimental.pallas import tpu as pltpu
from jax.sharding import PartitionSpec as P


ridge_weight = 0.2
LOG2E = 1.0 / math.log(2.0)
NN = (((1,), (0,)), ((), ()))
NT = (((1,), (1,)), ((), ()))
TN = (((0,), (0,)), ((), ()))


def pair(value):
    high = value.astype(jnp.bfloat16)
    low = (value - high.astype(jnp.float32)).astype(jnp.bfloat16)
    return high, low


def stacked(value):
    high, low = pair(value)
    return jnp.concatenate([high, low], axis=0)


def fold(product, rows):
    return product[:rows] + product[rows:]


def times_pair(rows, high, low, dims):
    both = stacked(rows)
    out = lax.dot_general(both, high, dims, preferred_element_type=jnp.float32)
    out = out + lax.dot_general(both, low, dims, preferred_element_type=jnp.float32)
    return fold(out, rows.shape[0])


def times(rows, matrix, dims):
    high, low = pair(matrix)
    return times_pair(rows, high, low, dims)


def blocks_of(held):
    return [(r, c) for r in range(1, held) for c in range(r)]


def lower(low_ref, order, r, c):
    at = r * (r - 1) // 2 + c
    return low_ref[:, at * order : (at + 1) * order]


def square(one, other):
    first, first_low = pair(one)
    second, second_low = pair(other)
    out = lax.dot_general(first, second, NN, preferred_element_type=jnp.float32)
    out = out + lax.dot_general(first, second_low, NN, preferred_element_type=jnp.float32)
    return out + lax.dot_general(first_low, second, NN, preferred_element_type=jnp.float32)


def cut(ref, at, width):
    return ref[:, pl.ds(pl.multiple_of(at * width, width), width)]


def back_apply(target, low_ref, inv_ref):
    held, order = inv_ref.shape[0], inv_ref.shape[1]
    parts = [target[:, n * order : (n + 1) * order] for n in range(held)]
    pieces = []
    for c in range(held):
        piece = times(parts[c], inv_ref[c], NN)
        for r in range(c + 1, held):
            piece = piece + times(parts[r], lower(low_ref, order, r, c), NN)
        pieces.append(piece)
    return jnp.concatenate(pieces, axis=1)


def fore_apply(source, high_ref, low_ref, order):
    pieces = []
    for end in range(order, source.shape[1] + 1, order):
        block = (slice(0, end), slice(end - order, end))
        pieces.append(times_pair(source[:, :end], high_ref[block], low_ref[block], NN))
    return jnp.concatenate(pieces, axis=1)


def store_turned(low, inv_ref, high_out, low_out):
    held, order = inv_ref.shape[0], inv_ref.shape[1]
    for r in range(held):
        for c in range(r + 1):
            at = r * (r - 1) // 2 + c
            block = inv_ref[r] if r == c else low[:, at * order : (at + 1) * order]
            place = (slice(c * order, (c + 1) * order), slice(r * order, (r + 1) * order))
            high_out[place], low_out[place] = pair(block.T)


def turn_kernel(low_ref, inv_ref, high_out, low_out):
    store_turned(low_ref[...], inv_ref, high_out, low_out)


def turn_factor_kernel(factor_ref, high_out, low_out):
    high_out[...], low_out[...] = pair(factor_ref[...].T)


def first_kernel(direction_ref, inv_ref, *refs):
    tri_refs, out_ref = refs[:-1], refs[-1]
    held, order = inv_ref.shape[0], inv_ref.shape[1]
    width = held * order
    tri = dict(zip(blocks_of(held), tri_refs))
    target = cut(direction_ref, lax.axis_index("crow"), width)
    pieces = [None] * held
    for number in reversed(range(held)):
        part = target[:, number * order : (number + 1) * order]
        for later in range(number + 1, held):
            part = part - times(pieces[later], tri[later, number][...], NN)
        pieces[number] = times(part, inv_ref[number], NN)
    out_ref[...] = jnp.concatenate(pieces, axis=1)


def lower_kernel(inv_ref, *refs):
    tri_refs, (out_ref, half_ref, rest_ref) = refs[:-3], refs[-3:]
    held, order = inv_ref.shape[0], inv_ref.shape[1]
    tri = dict(zip(blocks_of(held), tri_refs))
    found = {(n, n): inv_ref[n] for n in range(held)}
    for r in range(1, held):
        for c in range(r):
            total = square(tri[r, c][...], found[c, c])
            for between in range(c + 1, r):
                total = total + square(tri[r, between][...], found[between, c])
            found[r, c] = -square(inv_ref[r], total)
            at = r * (r - 1) // 2 + c
            out_ref[:, at * order : (at + 1) * order] = found[r, c]
    tall = half_ref.shape[0]
    at = lax.rem(lax.axis_index("dp"), 2) * tall
    split = half_ref.shape[1]
    half_ref[...] = out_ref[pl.ds(pl.multiple_of(at, tall), tall), :split]
    rest_ref[...] = out_ref[:, split:]


def pair_kernel(factor_ref, high_ref, low_ref):
    high, low = pair(factor_ref[...])
    high_ref[...] = high
    low_ref[...] = low


def spread_kernel(cols, *refs):
    extra = refs[: len(refs) - 3 - len(cols)]
    got_refs = refs[len(extra) : len(extra) + len(cols)]
    high_ref, low_ref, out_ref = refs[-3:]
    col = lax.axis_index("ccol")
    piece = got_refs[0][...]
    for at, got in zip(cols[1:], got_refs[1:]):
        piece = jnp.where(col == at, got[...], piece)
    out = times_pair(piece, high_ref[...], low_ref[...], NN)
    for ref in extra:
        out = out + ref[...]
    out_ref[...] = out


def merge_kernel(mine_ref, other_ref, rest_ref, inv_ref, high_out, low_out):
    odd = lax.rem(lax.axis_index("dp"), 2) == 1
    mine, other = mine_ref[...], other_ref[...]
    low = jnp.concatenate([jnp.where(odd, mine, other), jnp.where(odd, other, mine)], axis=0)
    low = jnp.concatenate([low, rest_ref[...]], axis=1)
    store_turned(low, inv_ref, high_out, low_out)


def solve_kernel(direction_ref, sub_ref, low_ref, inv_ref, out_ref):
    width = sub_ref.shape[1]
    target = cut(direction_ref, lax.axis_index("crow"), width) - sub_ref[...]
    out_ref[...] = back_apply(target, low_ref, inv_ref)


def pick_kernel(places, *refs):
    row, col = lax.axis_index("crow"), lax.axis_index("ccol")
    out = jnp.zeros_like(refs[0][...])
    for (r, c), ref in zip(places, refs[:-1]):
        out = jnp.where((row == r) & (col == c), ref[...], out)
    refs[-1][...] = out


def solve_pick_kernel(places, direction_ref, sub_ref, low_ref, inv_ref, *refs):
    width = sub_ref.shape[1]
    row, col = lax.axis_index("crow"), lax.axis_index("ccol")
    target = cut(direction_ref, row, width) - sub_ref[...]
    out = jnp.where((row == 0) & (col == 0), back_apply(target, low_ref, inv_ref), 0.0)
    for (r, c), ref in zip(places, refs[:-1]):
        out = jnp.where((row == r) & (col == c), ref[...], out)
    refs[-1][...] = out


def triple(value):
    high, middle = pair(value)
    rest = value - high.astype(jnp.float32) - middle.astype(jnp.float32)
    return high, middle, rest.astype(jnp.bfloat16)


def norm_rows(norm, inputs):
    row = lax.broadcasted_iota(jnp.int32, (inputs, norm.shape[1]), 0)
    wide = jnp.broadcast_to(norm, (inputs, norm.shape[1]))
    high, middle, low = (part.astype(jnp.float32) for part in triple(wide))
    rows = jnp.where(row == 0, high, jnp.where(row == 1, middle, jnp.where(row == 2, low, 0.0)))
    return rows.astype(jnp.bfloat16)


def ones_rows(norm, inputs):
    row = lax.broadcasted_iota(jnp.int32, (inputs, norm.shape[1]), 0)
    return jnp.where(row < 3, 1.0, 0.0).astype(jnp.bfloat16)


def scale_by(value, scales_ref):
    inputs = value.shape[0]
    row = lax.broadcasted_iota(jnp.int32, value.shape, 0)
    scales = jnp.full(value.shape, scales_ref[0], jnp.float32)
    for n in range(1, inputs):
        scales = jnp.where(row == n, scales_ref[n], scales)
    return value / scales


def tile_kernel(scales_ref, centres_ref, data_ref, high_ref, low_ref, right):
    inputs = data_ref.shape[0]

    @pl.when(pl.program_id(0) == 0)
    def _():
        scaled = scale_by(data_ref[...], scales_ref)
        norm = jnp.sum(scaled * scaled, axis=0, keepdims=True) * (-0.5 * LOG2E)
        high, middle, low = triple(scaled)
        right[...] = jnp.concatenate(
            [high, middle, high, middle, low, high, norm_rows(norm, inputs), ones_rows(norm, inputs)],
            axis=0,
        )

    scaled = scale_by(centres_ref[...], scales_ref)
    norm = jnp.sum(scaled * scaled, axis=0, keepdims=True) * (-0.5 * LOG2E)
    high, middle, low = triple(scaled * LOG2E)
    left = jnp.concatenate(
        [high, high, middle, middle, high, low, ones_rows(norm, inputs), norm_rows(norm, inputs)], axis=0
    )
    exponent = lax.dot_general(left, right[...], TN, preferred_element_type=jnp.float32)
    high, low = pair(jnp.exp2(exponent))
    high_ref[...] = high
    low_ref[...] = low


def image_kernel(*refs):
    part_refs = refs[:-4]
    high_ref, low_ref, mine_ref, out_ref = refs[-4:]
    piece = part_refs[0][...]
    for ref in part_refs[1:]:
        piece = piece + ref[...]
    mine_ref[...] = piece
    out_ref[...] = times_pair(piece, high_ref[...], low_ref[...], NN)


def normal_kernel(*refs):
    part_refs = refs[:-3]
    high_ref, low_ref, out_ref = refs[-3:]
    piece = part_refs[0][...]
    for ref in part_refs[1:]:
        piece = piece + ref[...]
    both = stacked(piece)
    out = lax.dot_general(high_ref[...], both, NT, preferred_element_type=jnp.float32)
    out = out + lax.dot_general(low_ref[...], both, NT, preferred_element_type=jnp.float32)
    out_ref[...] = fold(out.T, piece.shape[0])


def source_kernel(scale, order, mine_ref, *refs):
    part_refs = refs[:-4]
    high_ref, low_ref, out_ref, image_ref = refs[-4:]
    total = part_refs[0][...]
    for ref in part_refs[1:]:
        total = total + ref[...]
    normal = total * scale + ridge_weight * mine_ref[...]
    out_ref[...] = normal
    image_ref[...] = fore_apply(normal, high_ref, low_ref, order)


def fore_kernel(order, sides, *refs):
    side_refs = refs[:sides]
    got_ref, source_ref, fh_ref, fl_ref, high_ref, low_ref, image_out = refs[sides:]
    left = source_ref[...] - times_pair(got_ref[...], fh_ref[...], fl_ref[...], NN)
    for ref in side_refs:
        left = left - ref[...]
    image_out[...] = fore_apply(left, high_ref, low_ref, order)


def side_kernel(rows, sides, *refs):
    side_refs = refs[:sides]
    got_refs = refs[sides : sides + len(rows)]
    fh_ref, fl_ref, side_out = refs[sides + len(rows) :]
    row = lax.axis_index("crow")
    piece = got_refs[0][...]
    for at, ref in zip(rows[1:], got_refs[1:]):
        piece = jnp.where(row == at, ref[...], piece)
    side = times_pair(piece, fh_ref[...], fl_ref[...], NN)
    for ref in side_refs:
        side = side + ref[...]
    side_out[...] = side


def sum_kernel(*refs):
    total = refs[0][...]
    for ref in refs[1:-1]:
        total = total + ref[...]
    refs[-1][...] = total


def final_kernel(iterate_ref, residual_ref, direction_ref, *refs):
    part_refs = refs[:-4]
    iterate_out, residual_out, direction_out, image_ref = refs[-4:]
    width = part_refs[0].shape[1]
    row = lax.axis_index("crow")
    for step, ref in enumerate(part_refs):
        at = row ^ step
        image_ref[:, pl.ds(pl.multiple_of(at * width, width), width)] = ref[...]
    residual = residual_ref[...]
    direction = direction_ref[...]
    image = image_ref[...]
    gamma = jnp.sum(residual * residual, axis=1, keepdims=True)
    curvature = jnp.sum(direction * image, axis=1, keepdims=True)
    alpha = gamma / curvature
    iterate_out[...] = iterate_ref[...] + alpha * direction
    new_residual = residual - alpha * image
    residual_out[...] = new_residual
    gamma_next = jnp.sum(new_residual * new_residual, axis=1, keepdims=True)
    direction_out[...] = new_residual + (gamma_next / gamma) * direction


def shaped(*shape):
    return jax.ShapeDtypeStruct(shape, jnp.float32)


def call(kernel, outs, *args, limit=12, cost=(10**6, 10**6), **options):
    return pl.pallas_call(
        kernel,
        out_shape=outs,
        compiler_params=pltpu.CompilerParams(vmem_limit_bytes=limit << 20),
        cost_estimate=pl.CostEstimate(flops=cost[0], bytes_accessed=cost[1], transcendentals=0),
        **options,
    )(*args)


def step_of(data, centres, scales, factor, block_inv, iterate, residual, direction):
    dp, crow, ccol = lax.axis_size("dp"), lax.axis_size("crow"), lax.axis_size("ccol")
    held, order = block_inv.shape[0], block_inv.shape[1]
    width = factor.shape[0]
    rows, total = direction.shape
    assert factor.shape[1] == width and crow == ccol and crow in (4, 8) and dp % 2 == 0
    part = shaped(rows, width)
    last = crow - 1

    def spot(d, r, c):
        return (d * crow + r) * ccol + c

    def permute(value, target):
        perm = [
            (spot(d, r, c), spot(*target(d, r, c)))
            for d in range(dp)
            for r in range(crow)
            for c in range(ccol)
        ]
        return lax.ppermute(value, ("dp", "crow", "ccol"), perm)

    recent = collections.deque(maxlen=5)
    cells = [(r, c) for r in range(crow) for c in range(ccol)]

    def hops(a, b):
        return (a[0] ^ b[0]).bit_count() + abs(a[1] - b[1])

    def move(value, *pairs, idle=None):
        to, taken = {}, {cell for two in pairs for cell in two}
        for a, b in pairs:
            free = [cell for cell in cells if idle and idle(*cell) and cell not in taken]
            if free:
                spare = min(free, key=lambda cell: (cell in recent, hops(a, cell), hops(b, cell)))
                taken.add(spare)
                recent.append(spare)
                to[a], to[b], to[spare] = b, spare, a
            else:
                to[a], to[b] = b, a
        return permute(value, lambda d, r, c: (d ^ 1, *to.get((r, c), (r, c))))

    def shifts(value, axis, flip=1):
        steps = range(1, lax.axis_size(axis))
        if axis == "crow":
            return [permute(value, lambda d, r, c: (d ^ flip, r ^ n, c)) for n in steps]
        return [permute(value, lambda d, r, c: (d ^ flip, r, c ^ n)) for n in steps]

    def with_tri(kernel, outs, *args, limit=12):
        full = [pl.BlockSpec(a.shape, lambda i, n=a.ndim: (0,) * n) for a in args]
        tri = [pl.BlockSpec((order, order), lambda i, r=r, c=c: (r, c)) for r, c in blocks_of(held)]
        return call(
            kernel, outs, *args, *([factor] * len(tri)), grid=(1,), in_specs=full + tri,
            out_specs=[pl.BlockSpec(out.shape, lambda i: (0, 0)) for out in outs], limit=limit,
        )

    (piece,) = with_tri(first_kernel, [part], direction, block_inv, limit=58)
    found = {last: piece}
    spots = len(blocks_of(held)) * order
    low, half, rest = with_tri(
        lower_kernel,
        [shaped(order, spots), shaped(order // 2, spots - order), shaped(order, order)],
        block_inv,
    )
    wide = jax.ShapeDtypeStruct((width, width), jnp.bfloat16)
    high_f, low_f = call(pair_kernel, [wide, wide], factor)
    turned_f = call(turn_factor_kernel, [wide, wide], factor)
    turned = call(turn_kernel, [wide, wide], low, block_inv)

    samples = data.shape[1]
    tile = order
    inputs = data.shape[0]
    kernel_shape = jax.ShapeDtypeStruct((width, samples), jnp.bfloat16)
    high_k, low_k = call(
        tile_kernel, [kernel_shape] * 2, scales, centres, data,
        grid=(width // tile,),
        in_specs=[
            pl.BlockSpec(memory_space=pltpu.SMEM),
            pl.BlockSpec((inputs, tile), lambda i: (0, i)),
            pl.BlockSpec((inputs, samples), lambda i: (0, 0)),
        ],
        out_specs=[pl.BlockSpec((tile, samples), lambda i: (i, 0))] * 2,
        scratch_shapes=[pltpu.VMEM((8 * inputs, samples), jnp.bfloat16)],
        limit=20,
    )

    def spread(cols, extra, got):
        return call(functools.partial(spread_kernel, cols), part, *extra, *got, high_f, low_f)

    sums = []
    for step in range(last, 0, -1):
        cols = list(range(step))[::-1]
        idle = (lambda r, c: c > r) if step > 1 else None
        near_idle = lambda r, c: c > r
        got = [move(piece, ((step, step), (step, c)), idle=near_idle) for c in cols]
        down = [((step, c), (step - 1, c)) for c in cols]
        if step == last:
            sub = move(spread(cols[:1], [], got[:1]), down[0], idle=idle)
            sums = [move(spread(cols[1:], [], got[1:]), *down[1:], idle=idle)]
        else:
            sub = move(spread(cols, sums, got), *down, idle=idle)
            sums = [sub]
        if step > 1:
            piece = call(solve_kernel, part, direction, sub, low, block_inv)
            found[step - 1] = piece
    places = [(n, n) for n in range(1, crow)]
    own = call(
        functools.partial(solve_pick_kernel, places), part, direction, sub, low, block_inv,
        *[found[n] for n in range(1, crow)],
    )

    parts = [own] + shifts(own, "crow")
    beside = [((n, n), (n, n - 1)) for n in range(1, crow)]
    half = move(half, *beside)
    mine, images = call(image_kernel, [part, shaped(rows, samples)], *parts, high_k, low_k, limit=16)
    images = [images] + shifts(images, "ccol", 0)
    summed = call(normal_kernel, part, *images, high_k, low_k, limit=16)
    if dp == 2:
        summed = summed + permute(summed, lambda d, r, c: (d ^ 1, r, c))
    else:
        summed = lax.psum(summed, "dp")
    parts = [summed] + shifts(summed, "crow")
    rest = move(rest, *beside)
    scale = 1.0 / (samples * dp * crow)
    source, image = call(
        functools.partial(source_kernel, scale, order), [part, part], mine, *parts, *turned
    )
    near = call(merge_kernel, [wide, wide], half, move(half), rest, block_inv)
    done = [image]
    places = [(0, 0)]
    side = []
    for step in range(1, crow):
        later = list(range(step + 1, crow))
        idle = lambda r, c, step=step: step > 1 and (c >= r or r < step - 1)
        first = move(image, (places[-1], (step, step - 1)), idle=idle)
        if step == 1:
            source = move(source, *beside)
        if side:
            shift = [((at, step - 2), (at, step - 1)) for at in range(step, crow)]
            side = [move(side[0], *shift, idle=idle if step < last else None)]
        others = [move(image, (places[-1], (at, step - 1)), idle=idle) for at in later]
        image = call(
            functools.partial(fore_kernel, order, len(side)), part,
            *side, first, source, *turned_f, *near,
        )
        if later:
            side = [
                call(
                    functools.partial(side_kernel, later, len(side)), part, *side, *others, *turned_f
                )
            ]
        done.append(image)
        places.append((step, step - 1))
    own = call(functools.partial(pick_kernel, places), part, *done)
    own = call(sum_kernel, part, own, *shifts(own, "ccol"))
    full = shaped(rows, total)
    return tuple(
        call(
            final_kernel, [full, full, full], iterate, residual, direction, own, *shifts(own, "crow"),
            scratch_shapes=[pltpu.VMEM((rows, total), jnp.float32)],
        )
    )


def solution(mesh):
    placed = (
        P(None, ("dp", "crow")),
        P(None, "ccol"),
        P(),
        P("crow", "ccol"),
        P("crow", None, None),
        P(),
        P(),
        P(),
    )
    return jax.shard_map(
        step_of, mesh=mesh, in_specs=placed, out_specs=(P(), P(), P()), check_vma=False
    )
```

```python
import functools
import math

import jax
import jax.numpy as jnp
from jax import lax
from jax.experimental import pallas as pl
from jax.experimental.pallas import tpu as pltpu
from jax.sharding import PartitionSpec as P


ridge_weight = 0.2
LOG2E = 1.0 / math.log(2.0)
NN = (((1,), (0,)), ((), ()))
NT = (((1,), (1,)), ((), ()))
TN = (((0,), (0,)), ((), ()))


def pair(value):
    high = value.astype(jnp.bfloat16)
    low = (value - high.astype(jnp.float32)).astype(jnp.bfloat16)
    return high, low


def stacked(value):
    high, low = pair(value)
    return jnp.concatenate([high, low], axis=0)


def fold(product, rows):
    return product[:rows] + product[rows:]


def times_pair(rows, high, low, dims):
    both = stacked(rows)
    out = lax.dot_general(both, high, dims, preferred_element_type=jnp.float32)
    out = out + lax.dot_general(both, low, dims, preferred_element_type=jnp.float32)
    return fold(out, rows.shape[0])


def times(rows, matrix, dims):
    high, low = pair(matrix)
    return times_pair(rows, high, low, dims)


def blocks_of(held):
    return [(r, c) for r in range(1, held) for c in range(r)]


def lower(low_ref, order, r, c):
    at = r * (r - 1) // 2 + c
    return low_ref[:, at * order : (at + 1) * order]


def square(one, other):
    first, first_low = pair(one)
    second, second_low = pair(other)
    out = lax.dot_general(first, second, NN, preferred_element_type=jnp.float32)
    out = out + lax.dot_general(first, second_low, NN, preferred_element_type=jnp.float32)
    return out + lax.dot_general(first_low, second, NN, preferred_element_type=jnp.float32)


def cut(ref, at, width):
    return ref[:, pl.ds(pl.multiple_of(at * width, width), width)]


def back_apply(target, low_ref, inv_ref):
    held, order = inv_ref.shape[0], inv_ref.shape[1]
    parts = [target[:, n * order : (n + 1) * order] for n in range(held)]
    pieces = []
    for c in range(held):
        piece = times(parts[c], inv_ref[c], NN)
        for r in range(c + 1, held):
            piece = piece + times(parts[r], lower(low_ref, order, r, c), NN)
        pieces.append(piece)
    return jnp.concatenate(pieces, axis=1)


def fore_apply(source, high_ref, low_ref, order):
    pieces = []
    for end in range(order, source.shape[1] + 1, order):
        block = (slice(0, end), slice(end - order, end))
        pieces.append(times_pair(source[:, :end], high_ref[block], low_ref[block], NN))
    return jnp.concatenate(pieces, axis=1)


def store_turned(low, inv_ref, high_out, low_out):
    held, order = inv_ref.shape[0], inv_ref.shape[1]
    for r in range(held):
        for c in range(r + 1):
            at = r * (r - 1) // 2 + c
            block = inv_ref[r] if r == c else low[:, at * order : (at + 1) * order]
            place = (slice(c * order, (c + 1) * order), slice(r * order, (r + 1) * order))
            high_out[place], low_out[place] = pair(block.T)


def turn_kernel(low_ref, inv_ref, high_out, low_out):
    store_turned(low_ref[...], inv_ref, high_out, low_out)


def turn_factor_kernel(factor_ref, high_out, low_out):
    high_out[...], low_out[...] = pair(factor_ref[...].T)


def first_kernel(direction_ref, inv_ref, *refs):
    tri_refs, out_ref = refs[:-1], refs[-1]
    held, order = inv_ref.shape[0], inv_ref.shape[1]
    width = held * order
    tri = dict(zip(blocks_of(held), tri_refs))
    target = cut(direction_ref, lax.axis_index("crow"), width)
    pieces = [None] * held
    for number in reversed(range(held)):
        part = target[:, number * order : (number + 1) * order]
        for later in range(number + 1, held):
            part = part - times(pieces[later], tri[later, number][...], NN)
        pieces[number] = times(part, inv_ref[number], NN)
    out_ref[...] = jnp.concatenate(pieces, axis=1)


def lower_kernel(inv_ref, *refs):
    tri_refs, (out_ref, half_ref, rest_ref) = refs[:-3], refs[-3:]
    held, order = inv_ref.shape[0], inv_ref.shape[1]
    tri = dict(zip(blocks_of(held), tri_refs))
    found = {(n, n): inv_ref[n] for n in range(held)}
    for r in range(1, held):
        for c in range(r):
            total = square(tri[r, c][...], found[c, c])
            for between in range(c + 1, r):
                total = total + square(tri[r, between][...], found[between, c])
            found[r, c] = -square(inv_ref[r], total)
            at = r * (r - 1) // 2 + c
            out_ref[:, at * order : (at + 1) * order] = found[r, c]
    tall = half_ref.shape[0]
    at = lax.rem(lax.axis_index("dp"), 2) * tall
    split = half_ref.shape[1]
    half_ref[...] = out_ref[pl.ds(pl.multiple_of(at, tall), tall), :split]
    rest_ref[...] = out_ref[:, split:]


def pair_kernel(factor_ref, high_ref, low_ref):
    high, low = pair(factor_ref[...])
    high_ref[...] = high
    low_ref[...] = low


def spread_kernel(cols, *refs):
    extra = refs[: len(refs) - 3 - len(cols)]
    got_refs = refs[len(extra) : len(extra) + len(cols)]
    high_ref, low_ref, out_ref = refs[-3:]
    col = lax.axis_index("ccol")
    piece = got_refs[0][...]
    for at, got in zip(cols[1:], got_refs[1:]):
        piece = jnp.where(col == at, got[...], piece)
    out = times_pair(piece, high_ref[...], low_ref[...], NN)
    for ref in extra:
        out = out + ref[...]
    out_ref[...] = out


def merge_kernel(mine_ref, other_ref, rest_ref, inv_ref, high_out, low_out):
    odd = lax.rem(lax.axis_index("dp"), 2) == 1
    mine, other = mine_ref[...], other_ref[...]
    low = jnp.concatenate([jnp.where(odd, mine, other), jnp.where(odd, other, mine)], axis=0)
    low = jnp.concatenate([low, rest_ref[...]], axis=1)
    store_turned(low, inv_ref, high_out, low_out)


def solve_kernel(direction_ref, sub_ref, low_ref, inv_ref, out_ref):
    width = sub_ref.shape[1]
    target = cut(direction_ref, lax.axis_index("crow"), width) - sub_ref[...]
    out_ref[...] = back_apply(target, low_ref, inv_ref)


def pick_kernel(places, *refs):
    row, col = lax.axis_index("crow"), lax.axis_index("ccol")
    out = jnp.zeros_like(refs[0][...])
    for (r, c), ref in zip(places, refs[:-1]):
        out = jnp.where((row == r) & (col == c), ref[...], out)
    refs[-1][...] = out


def solve_pick_kernel(places, direction_ref, sub_ref, low_ref, inv_ref, *refs):
    width = sub_ref.shape[1]
    row, col = lax.axis_index("crow"), lax.axis_index("ccol")
    target = cut(direction_ref, row, width) - sub_ref[...]
    out = jnp.where((row == 0) & (col == 0), back_apply(target, low_ref, inv_ref), 0.0)
    for (r, c), ref in zip(places, refs[:-1]):
        out = jnp.where((row == r) & (col == c), ref[...], out)
    refs[-1][...] = out


def triple(value):
    high, middle = pair(value)
    rest = value - high.astype(jnp.float32) - middle.astype(jnp.float32)
    return high, middle, rest.astype(jnp.bfloat16)


def norm_rows(norm, inputs):
    row = lax.broadcasted_iota(jnp.int32, (inputs, norm.shape[1]), 0)
    wide = jnp.broadcast_to(norm, (inputs, norm.shape[1]))
    high, middle, low = (part.astype(jnp.float32) for part in triple(wide))
    rows = jnp.where(row == 0, high, jnp.where(row == 1, middle, jnp.where(row == 2, low, 0.0)))
    return rows.astype(jnp.bfloat16)


def ones_rows(norm, inputs):
    row = lax.broadcasted_iota(jnp.int32, (inputs, norm.shape[1]), 0)
    return jnp.where(row < 3, 1.0, 0.0).astype(jnp.bfloat16)


def scale_by(value, scales_ref):
    inputs = value.shape[0]
    row = lax.broadcasted_iota(jnp.int32, value.shape, 0)
    scales = jnp.full(value.shape, scales_ref[0], jnp.float32)
    for n in range(1, inputs):
        scales = jnp.where(row == n, scales_ref[n], scales)
    return value / scales


def tile_kernel(scales_ref, centres_ref, data_ref, high_ref, low_ref, right):
    inputs = data_ref.shape[0]

    @pl.when(pl.program_id(0) == 0)
    def _():
        scaled = scale_by(data_ref[...], scales_ref)
        norm = jnp.sum(scaled * scaled, axis=0, keepdims=True) * (-0.5 * LOG2E)
        high, middle, low = triple(scaled)
        right[...] = jnp.concatenate(
            [high, middle, high, middle, low, high, norm_rows(norm, inputs), ones_rows(norm, inputs)],
            axis=0,
        )

    scaled = scale_by(centres_ref[...], scales_ref)
    norm = jnp.sum(scaled * scaled, axis=0, keepdims=True) * (-0.5 * LOG2E)
    high, middle, low = triple(scaled * LOG2E)
    left = jnp.concatenate(
        [high, high, middle, middle, high, low, ones_rows(norm, inputs), norm_rows(norm, inputs)], axis=0
    )
    exponent = lax.dot_general(left, right[...], TN, preferred_element_type=jnp.float32)
    high, low = pair(jnp.exp2(exponent))
    high_ref[...] = high
    low_ref[...] = low


def image_kernel(*refs):
    part_refs = refs[:-4]
    high_ref, low_ref, mine_ref, out_ref = refs[-4:]
    piece = part_refs[0][...]
    for ref in part_refs[1:]:
        piece = piece + ref[...]
    mine_ref[...] = piece
    out_ref[...] = times_pair(piece, high_ref[...], low_ref[...], NN)


def normal_kernel(*refs):
    part_refs = refs[:-3]
    high_ref, low_ref, out_ref = refs[-3:]
    piece = part_refs[0][...]
    for ref in part_refs[1:]:
        piece = piece + ref[...]
    both = stacked(piece)
    out = lax.dot_general(high_ref[...], both, NT, preferred_element_type=jnp.float32)
    out = out + lax.dot_general(low_ref[...], both, NT, preferred_element_type=jnp.float32)
    out_ref[...] = fold(out.T, piece.shape[0])


def source_kernel(scale, order, mine_ref, *refs):
    part_refs = refs[:-4]
    high_ref, low_ref, out_ref, image_ref = refs[-4:]
    total = part_refs[0][...]
    for ref in part_refs[1:]:
        total = total + ref[...]
    normal = total * scale + ridge_weight * mine_ref[...]
    out_ref[...] = normal
    image_ref[...] = fore_apply(normal, high_ref, low_ref, order)


def fore_kernel(order, sides, *refs):
    side_refs = refs[:sides]
    got_ref, source_ref, fh_ref, fl_ref, high_ref, low_ref, image_out = refs[sides:]
    left = source_ref[...] - times_pair(got_ref[...], fh_ref[...], fl_ref[...], NN)
    for ref in side_refs:
        left = left - ref[...]
    image_out[...] = fore_apply(left, high_ref, low_ref, order)


def side_kernel(rows, sides, *refs):
    side_refs = refs[:sides]
    got_refs = refs[sides : sides + len(rows)]
    fh_ref, fl_ref, side_out = refs[sides + len(rows) :]
    row = lax.axis_index("crow")
    piece = got_refs[0][...]
    for at, ref in zip(rows[1:], got_refs[1:]):
        piece = jnp.where(row == at, ref[...], piece)
    side = times_pair(piece, fh_ref[...], fl_ref[...], NN)
    for ref in side_refs:
        side = side + ref[...]
    side_out[...] = side


def sum_kernel(*refs):
    total = refs[0][...]
    for ref in refs[1:-1]:
        total = total + ref[...]
    refs[-1][...] = total


def final_kernel(iterate_ref, residual_ref, direction_ref, *refs):
    part_refs = refs[:-4]
    iterate_out, residual_out, direction_out, image_ref = refs[-4:]
    width = part_refs[0].shape[1]
    row = lax.axis_index("crow")
    for step, ref in enumerate(part_refs):
        at = row ^ step
        image_ref[:, pl.ds(pl.multiple_of(at * width, width), width)] = ref[...]
    residual = residual_ref[...]
    direction = direction_ref[...]
    image = image_ref[...]
    gamma = jnp.sum(residual * residual, axis=1, keepdims=True)
    curvature = jnp.sum(direction * image, axis=1, keepdims=True)
    alpha = gamma / curvature
    iterate_out[...] = iterate_ref[...] + alpha * direction
    new_residual = residual - alpha * image
    residual_out[...] = new_residual
    gamma_next = jnp.sum(new_residual * new_residual, axis=1, keepdims=True)
    direction_out[...] = new_residual + (gamma_next / gamma) * direction


def shaped(*shape):
    return jax.ShapeDtypeStruct(shape, jnp.float32)


def call(kernel, outs, *args, limit=12, cost=(10**6, 10**6), **options):
    return pl.pallas_call(
        kernel,
        out_shape=outs,
        compiler_params=pltpu.CompilerParams(vmem_limit_bytes=limit << 20),
        cost_estimate=pl.CostEstimate(flops=cost[0], bytes_accessed=cost[1], transcendentals=0),
        **options,
    )(*args)


def step_of(data, centres, scales, factor, block_inv, iterate, residual, direction):
    dp, crow, ccol = lax.axis_size("dp"), lax.axis_size("crow"), lax.axis_size("ccol")
    held, order = block_inv.shape[0], block_inv.shape[1]
    width = factor.shape[0]
    rows, total = direction.shape
    assert factor.shape[1] == width and crow == ccol and crow in (4, 8) and dp % 2 == 0
    part = shaped(rows, width)
    last = crow - 1

    def spot(d, r, c):
        return (d * crow + r) * ccol + c

    def permute(value, target):
        perm = [
            (spot(d, r, c), spot(*target(d, r, c)))
            for d in range(dp)
            for r in range(crow)
            for c in range(ccol)
        ]
        return lax.ppermute(value, ("dp", "crow", "ccol"), perm)

    def move(value, *pairs):
        to = dict(pairs)
        to.update((b, a) for a, b in pairs)
        return permute(value, lambda d, r, c: (d ^ 1, *to.get((r, c), (r, c))))

    def shifts(value, axis, flip=1):
        steps = range(1, lax.axis_size(axis))
        if axis == "crow":
            return [permute(value, lambda d, r, c: (d ^ flip, r ^ n, c)) for n in steps]
        return [permute(value, lambda d, r, c: (d ^ flip, r, c ^ n)) for n in steps]

    def with_tri(kernel, outs, *args, limit=12):
        full = [pl.BlockSpec(a.shape, lambda i, n=a.ndim: (0,) * n) for a in args]
        tri = [pl.BlockSpec((order, order), lambda i, r=r, c=c: (r, c)) for r, c in blocks_of(held)]
        return call(
            kernel, outs, *args, *([factor] * len(tri)), grid=(1,), in_specs=full + tri,
            out_specs=[pl.BlockSpec(out.shape, lambda i: (0, 0)) for out in outs], limit=limit,
        )

    (piece,) = with_tri(first_kernel, [part], direction, block_inv, limit=58)
    found = {last: piece}
    spots = len(blocks_of(held)) * order
    low, half, rest = with_tri(
        lower_kernel,
        [shaped(order, spots), shaped(order // 2, spots - order), shaped(order, order)],
        block_inv,
    )
    wide = jax.ShapeDtypeStruct((width, width), jnp.bfloat16)
    high_f, low_f = call(pair_kernel, [wide, wide], factor)
    turned_f = call(turn_factor_kernel, [wide, wide], factor)
    turned = call(turn_kernel, [wide, wide], low, block_inv)

    samples = data.shape[1]
    tile = order
    inputs = data.shape[0]
    kernel_shape = jax.ShapeDtypeStruct((width, samples), jnp.bfloat16)
    high_k, low_k = call(
        tile_kernel, [kernel_shape] * 2, scales, centres, data,
        grid=(width // tile,),
        in_specs=[
            pl.BlockSpec(memory_space=pltpu.SMEM),
            pl.BlockSpec((inputs, tile), lambda i: (0, i)),
            pl.BlockSpec((inputs, samples), lambda i: (0, 0)),
        ],
        out_specs=[pl.BlockSpec((tile, samples), lambda i: (i, 0))] * 2,
        scratch_shapes=[pltpu.VMEM((8 * inputs, samples), jnp.bfloat16)],
        limit=20,
    )

    def spread(cols, extra, got):
        return call(functools.partial(spread_kernel, cols), part, *extra, *got, high_f, low_f)

    sums = []
    for step in range(last, 0, -1):
        cols = list(range(step))[::-1]
        got = [move(piece, ((step, step), (step, c))) for c in cols]
        down = [((step, c), (step - 1, c)) for c in cols]
        if step == last:
            sub = move(spread(cols[:1], [], got[:1]), down[0])
            sums = [move(spread(cols[1:], [], got[1:]), *down[1:])]
        else:
            sub = move(spread(cols, sums, got), *down)
            sums = [sub]
        if step > 1:
            piece = call(solve_kernel, part, direction, sub, low, block_inv)
            found[step - 1] = piece
    places = [(n, n) for n in range(1, crow)]
    own = call(
        functools.partial(solve_pick_kernel, places), part, direction, sub, low, block_inv,
        *[found[n] for n in range(1, crow)],
    )

    parts = [own] + shifts(own, "crow")
    beside = [((n, n), (n, n - 1)) for n in range(1, crow)]
    half = move(half, *beside)
    mine, images = call(image_kernel, [part, shaped(rows, samples)], *parts, high_k, low_k, limit=16)
    images = [images] + shifts(images, "ccol", 0)
    summed = call(normal_kernel, part, *images, high_k, low_k, limit=16)
    if dp == 2:
        summed = summed + permute(summed, lambda d, r, c: (d ^ 1, r, c))
    else:
        summed = lax.psum(summed, "dp")
    parts = [summed] + shifts(summed, "crow")
    rest = move(rest, *beside)
    scale = 1.0 / (samples * dp * crow)
    source, image = call(
        functools.partial(source_kernel, scale, order), [part, part], mine, *parts, *turned
    )
    near = call(merge_kernel, [wide, wide], half, move(half), rest, block_inv)
    done = [image]
    places = [(0, 0)]
    side = []
    for step in range(1, crow):
        later = list(range(step + 1, crow))
        first = move(image, (places[-1], (step, step - 1)))
        if step == 1:
            source = move(source, *beside)
        if side:
            shift = [((at, step - 2), (at, step - 1)) for at in range(step, crow)]
            side = [move(side[0], *shift)]
        others = [move(image, (places[-1], (at, step - 1))) for at in later]
        image = call(
            functools.partial(fore_kernel, order, len(side)), part,
            *side, first, source, *turned_f, *near,
        )
        if later:
            side = [
                call(
                    functools.partial(side_kernel, later, len(side)), part, *side, *others, *turned_f
                )
            ]
        done.append(image)
        places.append((step, step - 1))
    own = call(functools.partial(pick_kernel, places), part, *done)
    own = call(sum_kernel, part, own, *shifts(own, "ccol"))
    full = shaped(rows, total)
    return tuple(
        call(
            final_kernel, [full, full, full], iterate, residual, direction, own, *shifts(own, "crow"),
            scratch_shapes=[pltpu.VMEM((rows, total), jnp.float32)],
        )
    )


def solution(mesh):
    placed = (
        P(None, ("dp", "crow")),
        P(None, "ccol"),
        P(),
        P("crow", "ccol"),
        P("crow", None, None),
        P(),
        P(),
        P(),
    )
    return jax.shard_map(
        step_of, mesh=mesh, in_specs=placed, out_specs=(P(), P(), P()), check_vma=False
    )
```

```python
import collections
import functools
import math

import jax
import jax.numpy as jnp
from jax import lax
from jax.experimental import pallas as pl
from jax.experimental.pallas import tpu as pltpu
from jax.sharding import PartitionSpec as P


ridge_weight = 0.2
LOG2E = 1.0 / math.log(2.0)
NN = (((1,), (0,)), ((), ()))
NT = (((1,), (1,)), ((), ()))
TN = (((0,), (0,)), ((), ()))


def pair(value):
    high = value.astype(jnp.bfloat16)
    low = (value - high.astype(jnp.float32)).astype(jnp.bfloat16)
    return high, low


def stacked(value):
    high, low = pair(value)
    return jnp.concatenate([high, low], axis=0)


def fold(product, rows):
    return product[:rows] + product[rows:]


def times_pair(rows, high, low, dims):
    both = stacked(rows)
    out = lax.dot_general(both, high, dims, preferred_element_type=jnp.float32)
    out = out + lax.dot_general(both, low, dims, preferred_element_type=jnp.float32)
    return fold(out, rows.shape[0])


def times(rows, matrix, dims):
    high, low = pair(matrix)
    return times_pair(rows, high, low, dims)


def blocks_of(held):
    return [(r, c) for r in range(1, held) for c in range(r)]


def lower(low_ref, order, r, c):
    at = r * (r - 1) // 2 + c
    return low_ref[:, at * order : (at + 1) * order]


def square(one, other):
    first, first_low = pair(one)
    second, second_low = pair(other)
    out = lax.dot_general(first, second, NN, preferred_element_type=jnp.float32)
    out = out + lax.dot_general(first, second_low, NN, preferred_element_type=jnp.float32)
    return out + lax.dot_general(first_low, second, NN, preferred_element_type=jnp.float32)


def cut(ref, at, width):
    return ref[:, pl.ds(pl.multiple_of(at * width, width), width)]


def back_apply(target, low_ref, inv_ref):
    held, order = inv_ref.shape[0], inv_ref.shape[1]
    parts = [target[:, n * order : (n + 1) * order] for n in range(held)]
    pieces = []
    for c in range(held):
        piece = times(parts[c], inv_ref[c], NN)
        for r in range(c + 1, held):
            piece = piece + times(parts[r], lower(low_ref, order, r, c), NN)
        pieces.append(piece)
    return jnp.concatenate(pieces, axis=1)


def fore_apply(source, high_ref, low_ref, order):
    pieces = []
    for end in range(order, source.shape[1] + 1, order):
        block = (slice(0, end), slice(end - order, end))
        pieces.append(times_pair(source[:, :end], high_ref[block], low_ref[block], NN))
    return jnp.concatenate(pieces, axis=1)


def store_turned(low, inv_ref, high_out, low_out):
    held, order = inv_ref.shape[0], inv_ref.shape[1]
    for r in range(held):
        for c in range(r + 1):
            at = r * (r - 1) // 2 + c
            block = inv_ref[r] if r == c else low[:, at * order : (at + 1) * order]
            place = (slice(c * order, (c + 1) * order), slice(r * order, (r + 1) * order))
            high_out[place], low_out[place] = pair(block.T)


def turn_kernel(low_ref, inv_ref, high_out, low_out):
    store_turned(low_ref[...], inv_ref, high_out, low_out)


def turn_factor_kernel(factor_ref, high_out, low_out):
    high_out[...], low_out[...] = pair(factor_ref[...].T)


def first_kernel(direction_ref, inv_ref, *refs):
    tri_refs, out_ref = refs[:-1], refs[-1]
    held, order = inv_ref.shape[0], inv_ref.shape[1]
    width = held * order
    tri = dict(zip(blocks_of(held), tri_refs))
    target = cut(direction_ref, lax.axis_index("crow"), width)
    pieces = [None] * held
    for number in reversed(range(held)):
        part = target[:, number * order : (number + 1) * order]
        for later in range(number + 1, held):
            part = part - times(pieces[later], tri[later, number][...], NN)
        pieces[number] = times(part, inv_ref[number], NN)
    out_ref[...] = jnp.concatenate(pieces, axis=1)


def lower_kernel(inv_ref, *refs):
    tri_refs, out_ref, half_ref = refs[:-2], refs[-2], refs[-1]
    held, order = inv_ref.shape[0], inv_ref.shape[1]
    tri = dict(zip(blocks_of(held), tri_refs))
    found = {(n, n): inv_ref[n] for n in range(held)}
    for r in range(1, held):
        for c in range(r):
            total = square(tri[r, c][...], found[c, c])
            for between in range(c + 1, r):
                total = total + square(tri[r, between][...], found[between, c])
            found[r, c] = -square(inv_ref[r], total)
            at = r * (r - 1) // 2 + c
            out_ref[:, at * order : (at + 1) * order] = found[r, c]
    tall = half_ref.shape[0]
    at = lax.rem(lax.axis_index("dp"), 2) * tall
    half_ref[...] = out_ref[pl.ds(pl.multiple_of(at, tall), tall), :]


def pair_kernel(factor_ref, high_ref, low_ref):
    high, low = pair(factor_ref[...])
    high_ref[...] = high
    low_ref[...] = low


def spread_kernel(cols, *refs):
    extra = refs[: len(refs) - 3 - len(cols)]
    got_refs = refs[len(extra) : len(extra) + len(cols)]
    high_ref, low_ref, out_ref = refs[-3:]
    col = lax.axis_index("ccol")
    piece = got_refs[0][...]
    for at, got in zip(cols[1:], got_refs[1:]):
        piece = jnp.where(col == at, got[...], piece)
    out = times_pair(piece, high_ref[...], low_ref[...], NN)
    for ref in extra:
        out = out + ref[...]
    out_ref[...] = out


def join_kernel(at, one_ref, other_ref, out_ref):
    out_ref[...] = jnp.where(lax.axis_index("crow") == at, other_ref[...], one_ref[...])


def merge_kernel(mine_ref, other_ref, inv_ref, high_out, low_out):
    odd = lax.rem(lax.axis_index("dp"), 2) == 1
    mine, other = mine_ref[...], other_ref[...]
    low = jnp.concatenate([jnp.where(odd, mine, other), jnp.where(odd, other, mine)], axis=0)
    store_turned(low, inv_ref, high_out, low_out)


def solve_kernel(direction_ref, sub_ref, low_ref, inv_ref, out_ref):
    width = sub_ref.shape[1]
    target = cut(direction_ref, lax.axis_index("crow"), width) - sub_ref[...]
    out_ref[...] = back_apply(target, low_ref, inv_ref)


def pick_kernel(places, *refs):
    row, col = lax.axis_index("crow"), lax.axis_index("ccol")
    out = jnp.zeros_like(refs[0][...])
    for (r, c), ref in zip(places, refs[:-1]):
        out = jnp.where((row == r) & (col == c), ref[...], out)
    refs[-1][...] = out


def solve_pick_kernel(places, direction_ref, sub_ref, low_ref, inv_ref, *refs):
    width = sub_ref.shape[1]
    row, col = lax.axis_index("crow"), lax.axis_index("ccol")
    target = cut(direction_ref, row, width) - sub_ref[...]
    out = jnp.where((row == 0) & (col == 0), back_apply(target, low_ref, inv_ref), 0.0)
    for (r, c), ref in zip(places, refs[:-1]):
        out = jnp.where((row == r) & (col == c), ref[...], out)
    refs[-1][...] = out


def triple(value):
    high, middle = pair(value)
    rest = value - high.astype(jnp.float32) - middle.astype(jnp.float32)
    return high, middle, rest.astype(jnp.bfloat16)


def norm_rows(norm, inputs):
    row = lax.broadcasted_iota(jnp.int32, (inputs, norm.shape[1]), 0)
    wide = jnp.broadcast_to(norm, (inputs, norm.shape[1]))
    high, middle, low = (part.astype(jnp.float32) for part in triple(wide))
    rows = jnp.where(row == 0, high, jnp.where(row == 1, middle, jnp.where(row == 2, low, 0.0)))
    return rows.astype(jnp.bfloat16)


def ones_rows(norm, inputs):
    row = lax.broadcasted_iota(jnp.int32, (inputs, norm.shape[1]), 0)
    return jnp.where(row < 3, 1.0, 0.0).astype(jnp.bfloat16)


def scale_by(value, scales_ref):
    inputs = value.shape[0]
    row = lax.broadcasted_iota(jnp.int32, value.shape, 0)
    scales = jnp.full(value.shape, scales_ref[0], jnp.float32)
    for n in range(1, inputs):
        scales = jnp.where(row == n, scales_ref[n], scales)
    return value / scales


def tile_kernel(scales_ref, centres_ref, data_ref, high_ref, low_ref, right):
    inputs = data_ref.shape[0]

    @pl.when(pl.program_id(0) == 0)
    def _():
        scaled = scale_by(data_ref[...], scales_ref)
        norm = jnp.sum(scaled * scaled, axis=0, keepdims=True) * (-0.5 * LOG2E)
        high, middle, low = triple(scaled)
        right[...] = jnp.concatenate(
            [high, middle, high, middle, low, high, norm_rows(norm, inputs), ones_rows(norm, inputs)],
            axis=0,
        )

    scaled = scale_by(centres_ref[...], scales_ref)
    norm = jnp.sum(scaled * scaled, axis=0, keepdims=True) * (-0.5 * LOG2E)
    high, middle, low = triple(scaled * LOG2E)
    left = jnp.concatenate(
        [high, high, middle, middle, high, low, ones_rows(norm, inputs), norm_rows(norm, inputs)], axis=0
    )
    exponent = lax.dot_general(left, right[...], TN, preferred_element_type=jnp.float32)
    high, low = pair(jnp.exp2(exponent))
    high_ref[...] = high
    low_ref[...] = low


def image_kernel(*refs):
    part_refs = refs[:-4]
    high_ref, low_ref, mine_ref, out_ref = refs[-4:]
    piece = part_refs[0][...]
    for ref in part_refs[1:]:
        piece = piece + ref[...]
    mine_ref[...] = piece
    out_ref[...] = times_pair(piece, high_ref[...], low_ref[...], NN)


def normal_kernel(*refs):
    part_refs = refs[:-3]
    high_ref, low_ref, out_ref = refs[-3:]
    piece = part_refs[0][...]
    for ref in part_refs[1:]:
        piece = piece + ref[...]
    both = stacked(piece)
    out = lax.dot_general(high_ref[...], both, NT, preferred_element_type=jnp.float32)
    out = out + lax.dot_general(low_ref[...], both, NT, preferred_element_type=jnp.float32)
    out_ref[...] = fold(out.T, piece.shape[0])


def source_kernel(scale, order, mine_ref, *refs):
    part_refs = refs[:-4]
    high_ref, low_ref, out_ref, image_ref = refs[-4:]
    total = part_refs[0][...]
    for ref in part_refs[1:]:
        total = total + ref[...]
    normal = total * scale + ridge_weight * mine_ref[...]
    out_ref[...] = normal
    image_ref[...] = fore_apply(normal, high_ref, low_ref, order)


def fore_kernel(order, sides, *refs):
    side_refs = refs[:sides]
    got_ref, source_ref, fh_ref, fl_ref, high_ref, low_ref, image_out = refs[sides:]
    left = source_ref[...] - times_pair(got_ref[...], fh_ref[...], fl_ref[...], NN)
    for ref in side_refs:
        left = left - ref[...]
    image_out[...] = fore_apply(left, high_ref, low_ref, order)


def side_kernel(rows, sides, *refs):
    side_refs = refs[:sides]
    got_refs = refs[sides : sides + len(rows)]
    fh_ref, fl_ref, side_out = refs[sides + len(rows) :]
    row = lax.axis_index("crow")
    piece = got_refs[0][...]
    for at, ref in zip(rows[1:], got_refs[1:]):
        piece = jnp.where(row == at, ref[...], piece)
    side = times_pair(piece, fh_ref[...], fl_ref[...], NN)
    for ref in side_refs:
        side = side + ref[...]
    side_out[...] = side


def sum_kernel(*refs):
    total = refs[0][...]
    for ref in refs[1:-1]:
        total = total + ref[...]
    refs[-1][...] = total


def final_kernel(iterate_ref, residual_ref, direction_ref, *refs):
    part_refs = refs[:-4]
    iterate_out, residual_out, direction_out, image_ref = refs[-4:]
    width = part_refs[0].shape[1]
    row = lax.axis_index("crow")
    for step, ref in enumerate(part_refs):
        at = row ^ step
        image_ref[:, pl.ds(pl.multiple_of(at * width, width), width)] = ref[...]
    residual = residual_ref[...]
    direction = direction_ref[...]
    image = image_ref[...]
    gamma = jnp.sum(residual * residual, axis=1, keepdims=True)
    curvature = jnp.sum(direction * image, axis=1, keepdims=True)
    alpha = gamma / curvature
    iterate_out[...] = iterate_ref[...] + alpha * direction
    new_residual = residual - alpha * image
    residual_out[...] = new_residual
    gamma_next = jnp.sum(new_residual * new_residual, axis=1, keepdims=True)
    direction_out[...] = new_residual + (gamma_next / gamma) * direction


def shaped(*shape):
    return jax.ShapeDtypeStruct(shape, jnp.float32)


def call(kernel, outs, *args, limit=12, cost=(10**6, 10**6), **options):
    return pl.pallas_call(
        kernel,
        out_shape=outs,
        compiler_params=pltpu.CompilerParams(vmem_limit_bytes=limit << 20),
        cost_estimate=pl.CostEstimate(flops=cost[0], bytes_accessed=cost[1], transcendentals=0),
        **options,
    )(*args)


def step_of(data, centres, scales, factor, block_inv, iterate, residual, direction):
    dp, crow, ccol = lax.axis_size("dp"), lax.axis_size("crow"), lax.axis_size("ccol")
    held, order = block_inv.shape[0], block_inv.shape[1]
    width = factor.shape[0]
    rows, total = direction.shape
    assert factor.shape[1] == width and crow == ccol and crow in (4, 8) and dp % 2 == 0
    part = shaped(rows, width)
    last = crow - 1

    def spot(d, r, c):
        return (d * crow + r) * ccol + c

    def permute(value, target):
        perm = [
            (spot(d, r, c), spot(*target(d, r, c)))
            for d in range(dp)
            for r in range(crow)
            for c in range(ccol)
        ]
        return lax.ppermute(value, ("dp", "crow", "ccol"), perm)

    recent = collections.deque(maxlen=5)
    cells = [(r, c) for r in range(crow) for c in range(ccol)]

    def hops(a, b):
        return (a[0] ^ b[0]).bit_count() + abs(a[1] - b[1])

    def move(value, *pairs, idle=None):
        to, taken = {}, {cell for two in pairs for cell in two}
        for a, b in pairs:
            free = [cell for cell in cells if idle and idle(*cell) and cell not in taken]
            if free:
                spare = min(free, key=lambda cell: (cell in recent, hops(a, cell), hops(b, cell)))
                taken.add(spare)
                recent.append(spare)
                to[a], to[b], to[spare] = b, spare, a
            else:
                to[a], to[b] = b, a
        return permute(value, lambda d, r, c: (d ^ 1, *to.get((r, c), (r, c))))

    def shifts(value, axis, flip=1):
        steps = range(1, lax.axis_size(axis))
        if axis == "crow":
            return [permute(value, lambda d, r, c: (d ^ flip, r ^ n, c)) for n in steps]
        return [permute(value, lambda d, r, c: (d ^ flip, r, c ^ n)) for n in steps]

    def with_tri(kernel, outs, *args, limit=12):
        full = [pl.BlockSpec(a.shape, lambda i, n=a.ndim: (0,) * n) for a in args]
        tri = [pl.BlockSpec((order, order), lambda i, r=r, c=c: (r, c)) for r, c in blocks_of(held)]
        return call(
            kernel, outs, *args, *([factor] * len(tri)), grid=(1,), in_specs=full + tri,
            out_specs=[pl.BlockSpec(out.shape, lambda i: (0, 0)) for out in outs], limit=limit,
        )

    (piece,) = with_tri(first_kernel, [part], direction, block_inv, limit=58)
    found = {last: piece}
    spots = len(blocks_of(held)) * order
    low, half = with_tri(lower_kernel, [shaped(order, spots), shaped(order // 2, spots)], block_inv)
    wide = jax.ShapeDtypeStruct((width, width), jnp.bfloat16)
    high_f, low_f = call(pair_kernel, [wide, wide], factor)
    turned_f = call(turn_factor_kernel, [wide, wide], factor)
    turned = call(turn_kernel, [wide, wide], low, block_inv)

    samples = data.shape[1]
    tile = order
    inputs = data.shape[0]
    kernel_shape = jax.ShapeDtypeStruct((width, samples), jnp.bfloat16)
    high_k, low_k = call(
        tile_kernel, [kernel_shape] * 2, scales, centres, data,
        grid=(width // tile,),
        in_specs=[
            pl.BlockSpec(memory_space=pltpu.SMEM),
            pl.BlockSpec((inputs, tile), lambda i: (0, i)),
            pl.BlockSpec((inputs, samples), lambda i: (0, 0)),
        ],
        out_specs=[pl.BlockSpec((tile, samples), lambda i: (i, 0))] * 2,
        scratch_shapes=[pltpu.VMEM((8 * inputs, samples), jnp.bfloat16)],
        limit=20,
    )

    def spread(cols, extra, got):
        return call(functools.partial(spread_kernel, cols), part, *extra, *got, high_f, low_f)

    sums = []
    for step in range(last, 0, -1):
        cols = list(range(step))[::-1]
        idle = (lambda r, c: c > r) if step > 1 else None
        near_idle = lambda r, c: c > r
        got = [move(piece, ((step, step), (step, c)), idle=near_idle) for c in cols]
        down = [((step, c), (step - 1, c)) for c in cols]
        if step == last:
            sub = move(spread(cols[:1], [], got[:1]), down[0], idle=idle)
            sums = [move(spread(cols[1:], [], got[1:]), *down[1:], idle=idle)]
        else:
            sub = move(spread(cols, sums, got), *down, idle=idle)
            sums = [sub]
        if step > 1:
            piece = call(solve_kernel, part, direction, sub, low, block_inv)
            found[step - 1] = piece
    places = [(n, n) for n in range(1, crow)]
    own = call(
        functools.partial(solve_pick_kernel, places), part, direction, sub, low, block_inv,
        *[found[n] for n in range(1, crow)],
    )

    parts = [own] + shifts(own, "crow")
    beside = [((n, n), (n, n - 1)) for n in range(1, crow)]
    early = move(half, *beside[: last - 2], beside[last - 1])
    late = move(half, beside[last - 2])
    half = call(functools.partial(join_kernel, last - 1), shaped(*half.shape), early, late)
    mine, images = call(image_kernel, [part, shaped(rows, samples)], *parts, high_k, low_k, limit=16)
    images = [images] + shifts(images, "ccol", 0)
    summed = call(normal_kernel, part, *images, high_k, low_k, limit=16)
    if dp == 2:
        summed = summed + permute(summed, lambda d, r, c: (d ^ 1, r, c))
    else:
        summed = lax.psum(summed, "dp")
    parts = [summed] + shifts(summed, "crow")
    scale = 1.0 / (samples * dp * crow)
    source, image = call(
        functools.partial(source_kernel, scale, order), [part, part], mine, *parts, *turned
    )
    near = call(merge_kernel, [wide, wide], half, move(half), block_inv)
    done = [image]
    places = [(0, 0)]
    side = []
    for step in range(1, crow):
        later = list(range(step + 1, crow))
        idle = lambda r, c, step=step: step > 1 and (c >= r or r < step - 1)
        first = move(image, (places[-1], (step, step - 1)), idle=idle)
        if step == 1:
            source = move(source, *beside)
        if side:
            shift = [((at, step - 2), (at, step - 1)) for at in range(step, crow)]
            side = [move(side[0], *shift, idle=idle if step < last else None)]
        others = [move(image, (places[-1], (at, step - 1)), idle=idle) for at in later]
        image = call(
            functools.partial(fore_kernel, order, len(side)), part,
            *side, first, source, *turned_f, *near,
        )
        if later:
            side = [
                call(
                    functools.partial(side_kernel, later, len(side)), part, *side, *others, *turned_f
                )
            ]
        done.append(image)
        places.append((step, step - 1))
    own = call(functools.partial(pick_kernel, places), part, *done)
    own = call(sum_kernel, part, own, *shifts(own, "ccol"))
    full = shaped(rows, total)
    return tuple(
        call(
            final_kernel, [full, full, full], iterate, residual, direction, own, *shifts(own, "crow"),
            scratch_shapes=[pltpu.VMEM((rows, total), jnp.float32)],
        )
    )


def solution(mesh):
    placed = (
        P(None, ("dp", "crow")),
        P(None, "ccol"),
        P(),
        P("crow", "ccol"),
        P("crow", None, None),
        P(),
        P(),
        P(),
    )
    return jax.shard_map(step_of, mesh=mesh, in_specs=placed, out_specs=(P(), P(), P()), check_vma=False)
```

```python
import collections
import functools
import math

import jax
import jax.numpy as jnp
from jax import lax
from jax.experimental import pallas as pl
from jax.experimental.pallas import tpu as pltpu
from jax.sharding import PartitionSpec as P


ridge_weight = 0.2
LOG2E = 1.0 / math.log(2.0)
NN = (((1,), (0,)), ((), ()))
NT = (((1,), (1,)), ((), ()))
TN = (((0,), (0,)), ((), ()))


def pair(value):
    high = value.astype(jnp.bfloat16)
    low = (value - high.astype(jnp.float32)).astype(jnp.bfloat16)
    return high, low


def stacked(value):
    high, low = pair(value)
    return jnp.concatenate([high, low], axis=0)


def fold(product, rows):
    return product[:rows] + product[rows:]


def times_pair(rows, high, low, dims):
    both = stacked(rows)
    out = lax.dot_general(both, high, dims, preferred_element_type=jnp.float32)
    out = out + lax.dot_general(both, low, dims, preferred_element_type=jnp.float32)
    return fold(out, rows.shape[0])


def times(rows, matrix, dims):
    high, low = pair(matrix)
    return times_pair(rows, high, low, dims)


def blocks_of(held):
    return [(r, c) for r in range(1, held) for c in range(r)]


def lower(low_ref, order, r, c):
    at = r * (r - 1) // 2 + c
    return low_ref[:, at * order : (at + 1) * order]


def square(one, other):
    first, first_low = pair(one)
    second, second_low = pair(other)
    out = lax.dot_general(first, second, NN, preferred_element_type=jnp.float32)
    out = out + lax.dot_general(first, second_low, NN, preferred_element_type=jnp.float32)
    return out + lax.dot_general(first_low, second, NN, preferred_element_type=jnp.float32)


def cut(ref, at, width):
    return ref[:, pl.ds(pl.multiple_of(at * width, width), width)]


def back_apply(target, low_ref, inv_ref):
    held, order = inv_ref.shape[0], inv_ref.shape[1]
    parts = [target[:, n * order : (n + 1) * order] for n in range(held)]
    pieces = []
    for c in range(held):
        piece = times(parts[c], inv_ref[c], NN)
        for r in range(c + 1, held):
            piece = piece + times(parts[r], lower(low_ref, order, r, c), NN)
        pieces.append(piece)
    return jnp.concatenate(pieces, axis=1)


def fore_apply(source, high_ref, low_ref, order):
    pieces = []
    for end in range(order, source.shape[1] + 1, order):
        block = (slice(0, end), slice(end - order, end))
        pieces.append(times_pair(source[:, :end], high_ref[block], low_ref[block], NN))
    return jnp.concatenate(pieces, axis=1)


def store_turned(low, inv_ref, high_out, low_out):
    held, order = inv_ref.shape[0], inv_ref.shape[1]
    for r in range(held):
        for c in range(r + 1):
            at = r * (r - 1) // 2 + c
            block = inv_ref[r] if r == c else low[:, at * order : (at + 1) * order]
            place = (slice(c * order, (c + 1) * order), slice(r * order, (r + 1) * order))
            high_out[place], low_out[place] = pair(block.T)


def turn_kernel(low_ref, inv_ref, high_out, low_out):
    store_turned(low_ref[...], inv_ref, high_out, low_out)


def turn_factor_kernel(factor_ref, high_out, low_out):
    high_out[...], low_out[...] = pair(factor_ref[...].T)


def first_kernel(direction_ref, inv_ref, *refs):
    tri_refs, out_ref = refs[:-1], refs[-1]
    held, order = inv_ref.shape[0], inv_ref.shape[1]
    width = held * order
    tri = dict(zip(blocks_of(held), tri_refs))
    target = cut(direction_ref, lax.axis_index("crow"), width)
    pieces = [None] * held
    for number in reversed(range(held)):
        part = target[:, number * order : (number + 1) * order]
        for later in range(number + 1, held):
            part = part - times(pieces[later], tri[later, number][...], NN)
        pieces[number] = times(part, inv_ref[number], NN)
    out_ref[...] = jnp.concatenate(pieces, axis=1)


def lower_kernel(inv_ref, *refs):
    tri_refs, out_ref, half_ref = refs[:-2], refs[-2], refs[-1]
    held, order = inv_ref.shape[0], inv_ref.shape[1]
    tri = dict(zip(blocks_of(held), tri_refs))
    found = {(n, n): inv_ref[n] for n in range(held)}
    for r in range(1, held):
        for c in range(r):
            total = square(tri[r, c][...], found[c, c])
            for between in range(c + 1, r):
                total = total + square(tri[r, between][...], found[between, c])
            found[r, c] = -square(inv_ref[r], total)
            at = r * (r - 1) // 2 + c
            out_ref[:, at * order : (at + 1) * order] = found[r, c]
    tall = half_ref.shape[0]
    at = lax.rem(lax.axis_index("dp"), 2) * tall
    half_ref[...] = out_ref[pl.ds(pl.multiple_of(at, tall), tall), :]


def pair_kernel(factor_ref, high_ref, low_ref):
    high, low = pair(factor_ref[...])
    high_ref[...] = high
    low_ref[...] = low


def spread_kernel(cols, *refs):
    extra = refs[: len(refs) - 3 - len(cols)]
    got_refs = refs[len(extra) : len(extra) + len(cols)]
    high_ref, low_ref, out_ref = refs[-3:]
    col = lax.axis_index("ccol")
    piece = got_refs[0][...]
    for at, got in zip(cols[1:], got_refs[1:]):
        piece = jnp.where(col == at, got[...], piece)
    out = times_pair(piece, high_ref[...], low_ref[...], NN)
    for ref in extra:
        out = out + ref[...]
    out_ref[...] = out


def join_kernel(at, one_ref, other_ref, out_ref):
    out_ref[...] = jnp.where(lax.axis_index("crow") == at, other_ref[...], one_ref[...])


def merge_kernel(mine_ref, other_ref, inv_ref, high_out, low_out):
    odd = lax.rem(lax.axis_index("dp"), 2) == 1
    mine, other = mine_ref[...], other_ref[...]
    low = jnp.concatenate([jnp.where(odd, mine, other), jnp.where(odd, other, mine)], axis=0)
    store_turned(low, inv_ref, high_out, low_out)


def solve_kernel(direction_ref, sub_ref, low_ref, inv_ref, out_ref):
    width = sub_ref.shape[1]
    target = cut(direction_ref, lax.axis_index("crow"), width) - sub_ref[...]
    out_ref[...] = back_apply(target, low_ref, inv_ref)


def pick_kernel(places, *refs):
    row, col = lax.axis_index("crow"), lax.axis_index("ccol")
    out = jnp.zeros_like(refs[0][...])
    for (r, c), ref in zip(places, refs[:-1]):
        out = jnp.where((row == r) & (col == c), ref[...], out)
    refs[-1][...] = out


def solve_pick_kernel(places, direction_ref, sub_ref, low_ref, inv_ref, *refs):
    width = sub_ref.shape[1]
    row, col = lax.axis_index("crow"), lax.axis_index("ccol")
    target = cut(direction_ref, row, width) - sub_ref[...]
    out = jnp.where((row == 0) & (col == 0), back_apply(target, low_ref, inv_ref), 0.0)
    for (r, c), ref in zip(places, refs[:-1]):
        out = jnp.where((row == r) & (col == c), ref[...], out)
    refs[-1][...] = out


def triple(value):
    high, middle = pair(value)
    rest = value - high.astype(jnp.float32) - middle.astype(jnp.float32)
    return high, middle, rest.astype(jnp.bfloat16)


def norm_rows(norm, inputs):
    row = lax.broadcasted_iota(jnp.int32, (inputs, norm.shape[1]), 0)
    wide = jnp.broadcast_to(norm, (inputs, norm.shape[1]))
    high, middle, low = (part.astype(jnp.float32) for part in triple(wide))
    rows = jnp.where(row == 0, high, jnp.where(row == 1, middle, jnp.where(row == 2, low, 0.0)))
    return rows.astype(jnp.bfloat16)


def ones_rows(norm, inputs):
    row = lax.broadcasted_iota(jnp.int32, (inputs, norm.shape[1]), 0)
    return jnp.where(row < 3, 1.0, 0.0).astype(jnp.bfloat16)


def scale_by(value, scales_ref):
    inputs = value.shape[0]
    row = lax.broadcasted_iota(jnp.int32, value.shape, 0)
    scales = jnp.full(value.shape, scales_ref[0], jnp.float32)
    for n in range(1, inputs):
        scales = jnp.where(row == n, scales_ref[n], scales)
    return value / scales


def tile_kernel(scales_ref, centres_ref, data_ref, high_ref, low_ref, right):
    inputs = data_ref.shape[0]

    @pl.when(pl.program_id(0) == 0)
    def _():
        scaled = scale_by(data_ref[...], scales_ref)
        norm = jnp.sum(scaled * scaled, axis=0, keepdims=True) * (-0.5 * LOG2E)
        high, middle, low = triple(scaled)
        right[...] = jnp.concatenate(
            [high, middle, high, middle, low, high, norm_rows(norm, inputs), ones_rows(norm, inputs)],
            axis=0,
        )

    scaled = scale_by(centres_ref[...], scales_ref)
    norm = jnp.sum(scaled * scaled, axis=0, keepdims=True) * (-0.5 * LOG2E)
    high, middle, low = triple(scaled * LOG2E)
    left = jnp.concatenate(
        [high, high, middle, middle, high, low, ones_rows(norm, inputs), norm_rows(norm, inputs)], axis=0
    )
    exponent = lax.dot_general(left, right[...], TN, preferred_element_type=jnp.float32)
    high, low = pair(jnp.exp2(exponent))
    high_ref[...] = high
    low_ref[...] = low


def image_kernel(*refs):
    part_refs = refs[:-4]
    high_ref, low_ref, mine_ref, out_ref = refs[-4:]
    piece = part_refs[0][...]
    for ref in part_refs[1:]:
        piece = piece + ref[...]
    mine_ref[...] = piece
    out_ref[...] = times_pair(piece, high_ref[...], low_ref[...], NN)


def normal_kernel(*refs):
    part_refs = refs[:-3]
    high_ref, low_ref, out_ref = refs[-3:]
    piece = part_refs[0][...]
    for ref in part_refs[1:]:
        piece = piece + ref[...]
    both = stacked(piece)
    out = lax.dot_general(high_ref[...], both, NT, preferred_element_type=jnp.float32)
    out = out + lax.dot_general(low_ref[...], both, NT, preferred_element_type=jnp.float32)
    out_ref[...] = fold(out.T, piece.shape[0])


def source_kernel(scale, order, mine_ref, *refs):
    part_refs = refs[:-4]
    high_ref, low_ref, out_ref, image_ref = refs[-4:]
    total = part_refs[0][...]
    for ref in part_refs[1:]:
        total = total + ref[...]
    normal = total * scale + ridge_weight * mine_ref[...]
    out_ref[...] = normal
    image_ref[...] = fore_apply(normal, high_ref, low_ref, order)


def fore_kernel(order, sides, *refs):
    side_refs = refs[:sides]
    got_ref, source_ref, fh_ref, fl_ref, high_ref, low_ref, image_out = refs[sides:]
    left = source_ref[...] - times_pair(got_ref[...], fh_ref[...], fl_ref[...], NN)
    for ref in side_refs:
        left = left - ref[...]
    image_out[...] = fore_apply(left, high_ref, low_ref, order)


def side_kernel(rows, sides, *refs):
    side_refs = refs[:sides]
    got_refs = refs[sides : sides + len(rows)]
    fh_ref, fl_ref, side_out = refs[sides + len(rows) :]
    row = lax.axis_index("crow")
    piece = got_refs[0][...]
    for at, ref in zip(rows[1:], got_refs[1:]):
        piece = jnp.where(row == at, ref[...], piece)
    side = times_pair(piece, fh_ref[...], fl_ref[...], NN)
    for ref in side_refs:
        side = side + ref[...]
    side_out[...] = side


def sum_kernel(*refs):
    total = refs[0][...]
    for ref in refs[1:-1]:
        total = total + ref[...]
    refs[-1][...] = total


def final_kernel(iterate_ref, residual_ref, direction_ref, *refs):
    part_refs = refs[:-4]
    iterate_out, residual_out, direction_out, image_ref = refs[-4:]
    width = part_refs[0].shape[1]
    row = lax.axis_index("crow")
    for step, ref in enumerate(part_refs):
        at = row ^ step
        image_ref[:, pl.ds(pl.multiple_of(at * width, width), width)] = ref[...]
    residual = residual_ref[...]
    direction = direction_ref[...]
    image = image_ref[...]
    gamma = jnp.sum(residual * residual, axis=1, keepdims=True)
    curvature = jnp.sum(direction * image, axis=1, keepdims=True)
    alpha = gamma / curvature
    iterate_out[...] = iterate_ref[...] + alpha * direction
    new_residual = residual - alpha * image
    residual_out[...] = new_residual
    gamma_next = jnp.sum(new_residual * new_residual, axis=1, keepdims=True)
    direction_out[...] = new_residual + (gamma_next / gamma) * direction


def shaped(*shape):
    return jax.ShapeDtypeStruct(shape, jnp.float32)


def call(kernel, outs, *args, limit=12, cost=(10**6, 10**6), **options):
    return pl.pallas_call(
        kernel,
        out_shape=outs,
        compiler_params=pltpu.CompilerParams(vmem_limit_bytes=limit << 20),
        cost_estimate=pl.CostEstimate(flops=cost[0], bytes_accessed=cost[1], transcendentals=0),
        **options,
    )(*args)


def step_of(data, centres, scales, factor, block_inv, iterate, residual, direction):
    dp, crow, ccol = lax.axis_size("dp"), lax.axis_size("crow"), lax.axis_size("ccol")
    held, order = block_inv.shape[0], block_inv.shape[1]
    width = factor.shape[0]
    rows, total = direction.shape
    assert factor.shape[1] == width and crow == ccol and crow in (4, 8) and dp % 2 == 0
    part = shaped(rows, width)
    last = crow - 1

    def spot(d, r, c):
        return (d * crow + r) * ccol + c

    def permute(value, target):
        perm = [
            (spot(d, r, c), spot(*target(d, r, c)))
            for d in range(dp)
            for r in range(crow)
            for c in range(ccol)
        ]
        return lax.ppermute(value, ("dp", "crow", "ccol"), perm)

    recent = collections.deque(maxlen=5)
    cells = [(r, c) for r in range(crow) for c in range(ccol)]

    def hops(a, b):
        return (a[0] ^ b[0]).bit_count() + abs(a[1] - b[1])

    def move(value, *pairs, idle=None):
        to, taken = {}, {cell for two in pairs for cell in two}
        for a, b in pairs:
            free = [cell for cell in cells if idle and idle(*cell) and cell not in taken]
            if free:
                spare = min(free, key=lambda cell: (cell in recent, hops(a, cell), hops(b, cell)))
                taken.add(spare)
                recent.append(spare)
                to[a], to[b], to[spare] = b, spare, a
            else:
                to[a], to[b] = b, a
        return permute(value, lambda d, r, c: (d ^ 1, *to.get((r, c), (r, c))))

    def shifts(value, axis, flip=1):
        steps = range(1, lax.axis_size(axis))
        if axis == "crow":
            return [permute(value, lambda d, r, c: (d ^ flip, r ^ n, c)) for n in steps]
        return [permute(value, lambda d, r, c: (d ^ flip, r, c ^ n)) for n in steps]

    def with_tri(kernel, outs, *args, limit=12):
        full = [pl.BlockSpec(a.shape, lambda i, n=a.ndim: (0,) * n) for a in args]
        tri = [pl.BlockSpec((order, order), lambda i, r=r, c=c: (r, c)) for r, c in blocks_of(held)]
        return call(
            kernel, outs, *args, *([factor] * len(tri)), grid=(1,), in_specs=full + tri,
            out_specs=[pl.BlockSpec(out.shape, lambda i: (0, 0)) for out in outs], limit=limit,
        )

    (piece,) = with_tri(first_kernel, [part], direction, block_inv, limit=58)
    found = {last: piece}
    spots = len(blocks_of(held)) * order
    low, half = with_tri(lower_kernel, [shaped(order, spots), shaped(order // 2, spots)], block_inv)
    wide = jax.ShapeDtypeStruct((width, width), jnp.bfloat16)
    high_f, low_f = call(pair_kernel, [wide, wide], factor)
    turned_f = call(turn_factor_kernel, [wide, wide], factor)
    turned = call(turn_kernel, [wide, wide], low, block_inv)

    samples = data.shape[1]
    tile = order
    inputs = data.shape[0]
    kernel_shape = jax.ShapeDtypeStruct((width, samples), jnp.bfloat16)
    high_k, low_k = call(
        tile_kernel, [kernel_shape] * 2, scales, centres, data,
        grid=(width // tile,),
        in_specs=[
            pl.BlockSpec(memory_space=pltpu.SMEM),
            pl.BlockSpec((inputs, tile), lambda i: (0, i)),
            pl.BlockSpec((inputs, samples), lambda i: (0, 0)),
        ],
        out_specs=[pl.BlockSpec((tile, samples), lambda i: (i, 0))] * 2,
        scratch_shapes=[pltpu.VMEM((8 * inputs, samples), jnp.bfloat16)],
        limit=20,
    )

    def spread(cols, extra, got):
        return call(functools.partial(spread_kernel, cols), part, *extra, *got, high_f, low_f)

    sums = []
    for step in range(last, 0, -1):
        cols = list(range(step))[::-1]
        got = [move(piece, ((step, step), (step, c))) for c in cols]
        down = [((step, c), (step - 1, c)) for c in cols]
        if step == last:
            sub = move(spread(cols[:1], [], got[:1]), down[0])
            sums = [move(spread(cols[1:], [], got[1:]), *down[1:])]
        else:
            sub = move(spread(cols, sums, got), *down)
            sums = [sub]
        if step > 1:
            piece = call(solve_kernel, part, direction, sub, low, block_inv)
            found[step - 1] = piece
    places = [(n, n) for n in range(1, crow)]
    own = call(
        functools.partial(solve_pick_kernel, places), part, direction, sub, low, block_inv,
        *[found[n] for n in range(1, crow)],
    )

    parts = [own] + shifts(own, "crow")
    beside = [((n, n), (n, n - 1)) for n in range(1, crow)]
    early = move(half, *beside[: last - 2], beside[last - 1])
    late = move(half, beside[last - 2])
    half = call(functools.partial(join_kernel, last - 1), shaped(*half.shape), early, late)
    mine, images = call(image_kernel, [part, shaped(rows, samples)], *parts, high_k, low_k, limit=16)
    images = [images] + shifts(images, "ccol", 0)
    summed = call(normal_kernel, part, *images, high_k, low_k, limit=16)
    if dp == 2:
        summed = summed + permute(summed, lambda d, r, c: (d ^ 1, r, c))
    else:
        summed = lax.psum(summed, "dp")
    parts = [summed] + shifts(summed, "crow")
    scale = 1.0 / (samples * dp * crow)
    source, image = call(
        functools.partial(source_kernel, scale, order), [part, part], mine, *parts, *turned
    )
    near = call(merge_kernel, [wide, wide], half, move(half), block_inv)
    done = [image]
    places = [(0, 0)]
    side = []
    for step in range(1, crow):
        later = list(range(step + 1, crow))
        idle = lambda r, c, step=step: step > 1 and (c >= r or r < step - 1)
        first = move(image, (places[-1], (step, step - 1)), idle=idle)
        if step == 1:
            source = move(source, *beside)
        if side:
            shift = [((at, step - 2), (at, step - 1)) for at in range(step, crow)]
            side = [move(side[0], *shift, idle=idle if step < last else None)]
        others = [move(image, (places[-1], (at, step - 1)), idle=idle) for at in later]
        image = call(
            functools.partial(fore_kernel, order, len(side)), part,
            *side, first, source, *turned_f, *near,
        )
        if later:
            side = [
                call(
                    functools.partial(side_kernel, later, len(side)), part, *side, *others, *turned_f
                )
            ]
        done.append(image)
        places.append((step, step - 1))
    own = call(functools.partial(pick_kernel, places), part, *done)
    own = call(sum_kernel, part, own, *shifts(own, "ccol"))
    full = shaped(rows, total)
    return tuple(
        call(
            final_kernel, [full, full, full], iterate, residual, direction, own, *shifts(own, "crow"),
            scratch_shapes=[pltpu.VMEM((rows, total), jnp.float32)],
        )
    )


def solution(mesh):
    placed = (
        P(None, ("dp", "crow")),
        P(None, "ccol"),
        P(),
        P("crow", "ccol"),
        P("crow", None, None),
        P(),
        P(),
        P(),
    )
    return jax.shard_map(
        step_of, mesh=mesh, in_specs=placed, out_specs=(P(), P(), P()), check_vma=False
    )
```
